32 devices in a mesh: seq: 8 (over z, y), kv: 4 (over x, core).
Axes of the slice: x: 2, y: 2, z: 4, core: 2. Of those that a mesh axis runs over, the one named last changes fastest.
Arguments:
- tokens: bfloat16 [8192, 2048], P(('seq', 'kv')), may hold values from -6 to 6
- cotangent: bfloat16 [8192, 2048], P(('seq', 'kv')), may hold values from -6 to 6
- corpus_id: int32 [8], P('seq'), may hold values from 0 to 7
- corpus_weight: float32 [8], replicated, may hold values from 0.5 to 2
- step_count: int32 [1], replicated, may hold values from 1 to 20
- qkv_weight: float32 [2048, 1920], P(('seq', 'kv')), may hold values from -0.125 to 0.125
- out_weight: float32 [1280, 2048], P(('seq', 'kv')), may hold values from -1.25 to 1.25
- gains: float32 [4224], P(('seq', 'kv')), may hold values from 0.5 to 1.5
- gate_weight: float32 [2048, 5632], P('seq', 'kv'), may hold values from -0.125 to 0.125
- up_weight: float32 [2048, 5632], P('seq', 'kv'), may hold values from -0.125 to 0.125
- down_weight: float32 [2048, 5632], P('seq', 'kv'), may hold values from -0.078125 to 0.078125
- first_qkv: float32 [2048, 1920], P(('seq', 'kv')), may hold values from -64 to 64
- first_out: float32 [1280, 2048], P(('seq', 'kv')), may hold values from -8 to 8
- first_gains: float32 [4224], P(('seq', 'kv')), may hold values from -96 to 96
- first_gate: float32 [2048, 5632], P('seq', 'kv'), may hold values from -16 to 16
- first_up: float32 [2048, 5632], P('seq', 'kv'), may hold values from -16 to 16
- first_down: float32 [2048, 5632], P('seq', 'kv'), may hold values from -40 to 40
- second_qkv: float32 [2048, 1920], P(('seq', 'kv')), may hold values from 434.176 to 1720.32
- second_out: float32 [1280, 2048], P(('seq', 'kv')), may hold values from 9.8304 to 38.5024
- second_gains: float32 [4224], P(('seq', 'kv')), may hold values from 983.04 to 3850.24
- second_gate: float32 [2048, 5632], P('seq', 'kv'), may hold values from 39.3216 to 155.648
- second_up: float32 [2048, 5632], P('seq', 'kv'), may hold values from 39.3216 to 155.648
- second_down: float32 [2048, 5632], P('seq', 'kv'), may hold values from 212.992 to 819.2
Outputs:
- block_out: bfloat16 [8192, 2048], P(('seq', 'kv'))
- grad_input: float32 [8192, 2048], P(('seq', 'kv'))
- new_qkv: float32 [2048, 1920], P(('seq', 'kv'))
- moments_qkv: float32 [2, 2048, 1920], P(None, ('seq', 'kv'))
- new_out: float32 [1280, 2048], P(('seq', 'kv'))
- moments_out: float32 [2, 1280, 2048], P(None, ('seq', 'kv'))
- new_gains: float32 [4224], P(('seq', 'kv'))
- moments_gains: float32 [2, 4224], P(None, ('seq', 'kv'))
- new_gate: float32 [2048, 5632], P('seq', 'kv')
- moments_gate: float32 [2, 2048, 5632], P(None, 'seq', 'kv')
- new_up: float32 [2048, 5632], P('seq', 'kv')
- moments_up: float32 [2, 2048, 5632], P(None, 'seq', 'kv')
- new_down: float32 [2048, 5632], P('seq', 'kv')
- moments_down: float32 [2, 2048, 5632], P(None, 'seq', 'kv')
The draws below stay inside these ranges and needn't reach their ends.
All inputs are finite; a program needn't handle non-finite values.
Results may differ from the reference program's by a relative error of at most 0.014.
The reference program's roundings to bfloat16 on the way count: a program that leaves them out, or rounds other values in their place, can miss the bound.
Values may be sent and summed in bfloat16 or wider, within the bound.
No kernel may reach another device: no remote copies, remote signals or barrier semaphores. Data moves between devices by JAX's collectives and lax.ppermute only.
A program may use at most 256 MiB of HBM per device.

```python
import math
import jax
import jax.numpy as jnp
from jax import lax

D = 2048
QUERY_HEADS = 20
VALUE_GROUPS = 5
HEAD_SIZE = 64
FF = 5632
CORPORA = 8
QKV = 1920
GAINS = 4224
SEQLEN = 1024
SEQS = 8
TOKENS = 8192
QB = 512


def set_ends(entries, rng, smallest, high):
    shape = entries.shape
    index_at = [jax.random.randint(jax.random.fold_in(rng, axis), (), 0, shape[axis]) for axis in range(len(shape))]
    entries = entries.at[tuple(index_at)].set(smallest)
    longest = shape.index(max(shape))
    index_at[longest] = (index_at[longest] + 1) % shape[longest]
    return entries.at[tuple(index_at)].set(high)


def block_scale(key, dims, split, least, top_value):
    factor_of, own = 1.0, jax.random.fold_in(key, 6)
    for dim, shards_of in split:
        draws = jnp.exp(jax.random.uniform(jax.random.fold_in(own, dim), (shards_of,), jnp.float32, least / len(split), top_value / len(split)))
        factor_of = factor_of * jnp.repeat(draws, dims[dim] // shards_of).reshape([-1 if axis == dim else 1 for axis in range(len(dims))])
    return factor_of


def centred(rng, extent, scale, limit, cuts=(), dtype=jnp.bfloat16):
    array = scale * jax.random.normal(rng, extent, jnp.float32)
    if cuts:
        array = array * block_scale(rng, extent, cuts, -0.22, 0.18)
    return jnp.clip(array, -limit, limit).astype(dtype)


def setup_inputs(seed: int = 0) -> dict:
    keys = jax.random.split(jax.random.key(seed), 24)
    return {
        "tokens": centred(keys[0], (TOKENS, D), 1.0, 6.0, ((0, 32),)),
        "cotangent": centred(keys[1], (TOKENS, D), 1.0, 6.0, ((0, 32),)),
        "corpus_id": set_ends(jax.random.randint(keys[2], (SEQS,), 0, CORPORA), jax.random.fold_in(keys[2], 1), 0, CORPORA - 1).astype(jnp.int32),
        "corpus_weight": jnp.clip(jnp.exp(jax.random.uniform(keys[3], (CORPORA,), jnp.float32, math.log(0.5), math.log(2.0))), 0.5, 2.0),
        "step_count": jax.random.randint(keys[4], (1,), 1, 21).astype(jnp.int32),
        "qkv_weight": centred(keys[5], (D, QKV), D ** -0.5, 0.125, ((0, 32),), jnp.float32),
        "out_weight": centred(keys[6], (QUERY_HEADS * HEAD_SIZE, D), QUERY_HEADS ** -0.5, 1.25, ((0, 32),), jnp.float32),
        "gains": jnp.clip(1.0 + 0.1 * jax.random.normal(keys[7], (GAINS,), jnp.float32), 0.5, 1.5),
        "gate_weight": centred(keys[8], (D, FF), D ** -0.5, 0.125, ((0, 8), (1, 4)), jnp.float32),
        "up_weight": centred(keys[9], (D, FF), D ** -0.5, 0.125, ((0, 8), (1, 4)), jnp.float32),
        "down_weight": centred(keys[10], (D, FF), FF ** -0.5, 0.078125, ((0, 8), (1, 4)), jnp.float32),
        "first_qkv": centred(keys[11], (D, QKV), (0.11 * TOKENS ** 0.5), 64.0, ((0, 32),), jnp.float32),
        "first_out": centred(keys[12], (QUERY_HEADS * HEAD_SIZE, D), (0.0165 * TOKENS ** 0.5), 8.0, ((0, 32),), jnp.float32),
        "first_gains": centred(keys[13], (GAINS,), (0.165 * TOKENS ** 0.5), 96.0, ((0, 32),), jnp.float32),
        "first_gate": centred(keys[14], (D, FF), (0.033 * TOKENS ** 0.5), 16.0, ((0, 8), (1, 4)), jnp.float32),
        "first_up": centred(keys[15], (D, FF), (0.033 * TOKENS ** 0.5), 16.0, ((0, 8), (1, 4)), jnp.float32),
        "first_down": centred(keys[16], (D, FF), (0.077 * TOKENS ** 0.5), 40.0, ((0, 8), (1, 4)), jnp.float32),
        "second_qkv": jnp.clip(jnp.exp(math.log(1720.32) - 1.3768156 * jax.random.uniform(keys[17], (D, QKV), jnp.float32) ** block_scale(keys[17], (D, QKV), ((0, 32),), -0.2, 0.2)), 434.176, 1720.32),
        "second_out": jnp.clip(jnp.exp(math.log(38.5024) - 1.3652409 * jax.random.uniform(keys[18], (QUERY_HEADS * HEAD_SIZE, D), jnp.float32) ** block_scale(keys[18], (QUERY_HEADS * HEAD_SIZE, D), ((0, 32),), -0.2, 0.2)), 9.8304, 38.5024),
        "second_gains": jnp.clip(jnp.exp(math.log(3850.24) - 1.36524097 * jax.random.uniform(keys[19], (GAINS,), jnp.float32) ** block_scale(keys[19], (GAINS,), ((0, 32),), -0.2, 0.2)), 983.04, 3850.24),
        "second_gate": jnp.clip(jnp.exp(math.log(155.648) - 1.375823 * jax.random.uniform(keys[20], (D, FF), jnp.float32) ** block_scale(keys[20], (D, FF), ((0, 8), (1, 4)), -0.2, 0.2)), 39.3216, 155.648),
        "second_up": jnp.clip(jnp.exp(math.log(155.648) - 1.375823 * jax.random.uniform(keys[21], (D, FF), jnp.float32) ** block_scale(keys[21], (D, FF), ((0, 8), (1, 4)), -0.2, 0.2)), 39.3216, 155.648),
        "second_down": jnp.clip(jnp.exp(math.log(819.2) - 1.34707364 * jax.random.uniform(keys[22], (D, FF), jnp.float32) ** block_scale(keys[22], (D, FF), ((0, 8), (1, 4)), -0.2, 0.2)), 212.992, 819.2),
    }


@jax.custom_vjp
def low(v):
    return lax.optimization_barrier(v.astype(jnp.bfloat16)).astype(jnp.float32)

@jax.custom_vjp
def low_back(v):
    return v

def low_keep(v):
    return (low(v), None)

def low_pass(kept, grad):
    return (grad,)

def back_keep(v):
    return (v, None)

def back_low(kept, grad):
    return (low(grad),)
low.defvjp(low_keep, low_pass)
low_back.defvjp(back_keep, back_low)
eps_norm = 1e-06
masked_value = -1e+30
beta_first = 0.9
beta_second = 0.95
adam_eps = 1e-08

def matmul(left, right):
    return jnp.dot(left, right, precision=lax.Precision.HIGHEST)

def angle_tables(item_count, model_width):
    places = jnp.arange(item_count).astype(jnp.float32)
    freqs = 10000.0 ** (-(jnp.arange(model_width // 2).astype(jnp.float32) * 2.0 / model_width))
    angles = places[:, None] * freqs[None, :]
    angles = jnp.concatenate([angles, angles], axis=-1)
    return (jnp.cos(angles)[:, None, :], jnp.sin(angles)[:, None, :])

def rotate(value_rows, cosine, sine):
    half = value_rows.shape[-1] // 2
    turned = jnp.concatenate([-value_rows[..., half:], value_rows[..., :half]], axis=-1)
    return value_rows * cosine + turned * sine

def head_norm(value_rows, gain):
    return value_rows * lax.rsqrt(lax.optimization_barrier(jnp.mean(value_rows * value_rows, -1, keepdims=True)) + eps_norm) * gain

def sequence_forward(rows, mixer, output, gain_values, gate_low, up_low, down_low):
    token_length = rows.shape[0]
    model_width = QUERY_HEADS // VALUE_GROUPS
    scale = lax.rsqrt(lax.optimization_barrier(jnp.mean(rows * rows, -1, keepdims=True)) + eps_norm)
    normed = low(rows * scale * gain_values[:D])
    mixed_output = low_back(matmul(normed, mixer))
    queries = mixed_output[:, :QUERY_HEADS * HEAD_SIZE].reshape(token_length, QUERY_HEADS, HEAD_SIZE)
    key_rows = mixed_output[:, QUERY_HEADS * HEAD_SIZE:(QUERY_HEADS + VALUE_GROUPS) * HEAD_SIZE].reshape(token_length, VALUE_GROUPS, HEAD_SIZE)
    value_rows = mixed_output[:, (QUERY_HEADS + VALUE_GROUPS) * HEAD_SIZE:].reshape(token_length, VALUE_GROUPS, HEAD_SIZE)
    gain_q = gain_values[2 * D:2 * D + HEAD_SIZE]
    gain_k = gain_values[2 * D + HEAD_SIZE:]
    cosine, sine = angle_tables(token_length, HEAD_SIZE)
    rotated_query = low_back(low(rotate(head_norm(queries, gain_q), cosine, sine)))
    rotated_key = low_back(low(rotate(head_norm(key_rows, gain_k), cosine, sine)))
    value_rows = low_back(low(value_rows))
    grouped_rows = rotated_query.reshape(token_length, VALUE_GROUPS, model_width, HEAD_SIZE)
    places = jnp.arange(token_length)

    def attend(index):
        start = (index * QB).astype(jnp.int32)
        part = lax.dynamic_slice_in_dim(grouped_rows, start, QB, 0)
        scores = jnp.einsum('qgjd,kgd->gjqk', part, rotated_key, precision=lax.Precision.HIGHEST) * 0.125
        scores = low_back(scores)
        allowed = places[None, :] <= (start + jnp.arange(QB))[:, None]
        scores = jnp.where(allowed, scores, masked_value)
        top = lax.optimization_barrier(jnp.max(scores, -1, keepdims=True))
        weights = jnp.exp(scores - top)
        probs = weights / lax.optimization_barrier(jnp.sum(weights, -1, keepdims=True))
        return jnp.einsum('gjqk,kgd->qgjd', low(probs), value_rows, precision=lax.Precision.HIGHEST)
    attended = lax.map(jax.checkpoint(attend), jnp.arange(token_length // QB))
    attended = low_back(low(attended.reshape(token_length, QUERY_HEADS * HEAD_SIZE)))
    hidden = rows + low_back(matmul(attended, output))
    scale_two = lax.rsqrt(lax.optimization_barrier(jnp.mean(hidden * hidden, -1, keepdims=True)) + eps_norm)
    normed_two = low(hidden * scale_two * gain_values[D:2 * D])
    gate = low_back(matmul(normed_two, gate_low))
    up_part = low_back(matmul(normed_two, up_low))
    acted = low(jax.nn.silu(gate) * up_part)
    ffn = low_back(matmul(acted, down_low.T))
    return hidden + ffn

def adamw(weight, grad, first, second, rate, shrink, item_count):
    first_new = beta_first * first + (1.0 - beta_first) * grad
    second_new = beta_second * second + (1.0 - beta_second) * grad * grad
    fix_first = 1.0 - jnp.power(beta_first, item_count)
    fix_second = 1.0 - jnp.power(beta_second, item_count)
    stepped = first_new / fix_first / (jnp.sqrt(second_new / fix_second) + adam_eps)
    return (weight - rate * (stepped + shrink * weight), jnp.stack([first_new, jnp.sqrt(second_new)]))

def reference(tokens, cotangent, corpus_id, corpus_weight, step_count, qkv_weight, out_weight, gains, gate_weight, up_weight, down_weight, first_qkv, first_out, first_gains, first_gate, first_up, first_down, second_qkv, second_out, second_gains, second_gate, second_up, second_down):

    def forward(inputs, mixer_w, output_w, gain_w, gate_w, up_w, down_w):
        mixer = low(mixer_w)
        output = low(output_w)
        gain_values = low(gain_w)
        gate_low = low(gate_w)
        up_low = low(up_w)
        down_low = low(down_w)
        stacked = inputs.reshape(SEQS, SEQLEN, D)

        def one_sequence(rows):
            return sequence_forward(rows, mixer, output, gain_values, gate_low, up_low, down_low)
        result = lax.map(jax.checkpoint(one_sequence), stacked)
        return result.reshape(TOKENS, D)
    result, pull = jax.vjp(forward, tokens.astype(jnp.float32), qkv_weight, out_weight, gains, gate_weight, up_weight, down_weight)
    factors = corpus_weight[corpus_id]
    weighted = (cotangent.astype(jnp.float32).reshape(SEQS, SEQLEN, D) * factors[:, None, None]).reshape(TOKENS, D)
    grads = pull(weighted)
    item_count = step_count[0].astype(jnp.float32)
    new_qkv, moments_qkv = adamw(qkv_weight, grads[1], first_qkv, second_qkv, 0.02, 0.1, item_count)
    new_out, moments_out = adamw(out_weight, grads[2], first_out, second_out, 0.2, 0.1, item_count)
    new_gains, moments_gains = adamw(gains, grads[3], first_gains, second_gains, 0.6, 0.0, item_count)
    new_gate, moments_gate = adamw(gate_weight, grads[4], first_gate, second_gate, 0.02, 0.1, item_count)
    new_up, moments_up = adamw(up_weight, grads[5], first_up, second_up, 0.02, 0.1, item_count)
    new_down, moments_down = adamw(down_weight, grads[6], first_down, second_down, 0.013, 0.1, item_count)
    return (result.astype(jnp.bfloat16), grads[0], new_qkv, moments_qkv, new_out, moments_out, new_gains, moments_gains, new_gate, moments_gate, new_up, moments_up, new_down, moments_down)
```

```python
import functools

import jax
import jax.numpy as jnp
import numpy as np
from jax import lax
from jax.experimental import pallas as pl
from jax.experimental.pallas import tpu as pltpu
from jax.sharding import Mesh, PartitionSpec as P

QUERY_HEADS = 20
VALUE_GROUPS = 5
HEAD_SIZE = 64

eps_norm = 1e-06
masked_value = -1e30
beta_first = 0.9
beta_second = 0.95
adam_eps = 1e-08

ALL = ("sh", "sl", "kh", "kl")
SEQ = ("sh", "sl")
KV = ("kh", "kl")
OWNERS = ("sh", "kl")
VMEM_LIMIT = 40 * 1024 * 1024


def rms_scale(value_rows):
    return lax.rsqrt(jnp.mean(value_rows * value_rows, -1, keepdims=True) + eps_norm)


def norm_back(grad_out, value_rows, scale, gain):
    shaped = value_rows * scale
    pushed = grad_out * gain
    grad_in = scale * (pushed - shaped * jnp.mean(pushed * shaped, -1, keepdims=True))
    return (grad_in, grad_out * shaped)


def angle_tables(item_count):
    places = np.arange(item_count).astype(np.float32)
    steps = np.arange(HEAD_SIZE // 2).astype(np.float32) * np.float32(2.0) / np.float32(HEAD_SIZE)
    freqs = np.float32(10000.0) ** (-steps)
    angles = freqs[:, None].astype(np.float32) * places[None, :]
    return (np.cos(angles).astype(np.float32), np.sin(angles).astype(np.float32))


def contract(left, right, left_dim, right_dim):
    return lax.dot_general(
        left,
        right,
        (((left_dim,), (right_dim,)), ((), ())),
        preferred_element_type=jnp.float32,
    )


def head_scale(rows):
    return lax.rsqrt(jnp.mean(rows * rows, 0, keepdims=True) + eps_norm)


def rotated(rows, scale, gain, cosine, sine):
    half = HEAD_SIZE // 2
    shaped = rows * scale * gain
    first, second = shaped[:half], shaped[half:]
    return jnp.concatenate(
        [first * cosine - second * sine, second * cosine + first * sine], axis=0
    )


def unrotated_norm_back(grad, rows, scale, gain, cosine, sine):
    half = HEAD_SIZE // 2
    first, second = grad[:half], grad[half:]
    turned = jnp.concatenate(
        [first * cosine + second * sine, second * cosine - first * sine], axis=0
    )
    shaped = rows * scale
    pushed = turned * gain
    grad_in = scale * (pushed - shaped * jnp.mean(pushed * shaped, 0, keepdims=True))
    return (grad_in, turned * shaped)


def causal(block):
    keys = lax.broadcasted_iota(jnp.int32, (block, block), 0)
    places = lax.broadcasted_iota(jnp.int32, (block, block), 1)
    return keys <= places


def forward_kernel(
    group_ref, qp_ref, kp_ref, vp_ref, cos_ref, sin_ref, gq_ref, gk_ref,
    q_ref, k_ref, v_ref, out_ref, lse_ref, *, block,
):
    cosine, sine = cos_ref[...], sin_ref[...]
    qp, kp = qp_ref[...], kp_ref[...]
    query = (rotated(qp, head_scale(qp), gq_ref[...], cosine, sine) * 0.125).astype(jnp.bfloat16)
    key = rotated(kp, head_scale(kp), gk_ref[...], cosine, sine).astype(jnp.bfloat16)
    value = vp_ref[...].astype(jnp.bfloat16)
    q_ref[0] = query
    k_ref[0] = key
    v_ref[0] = value
    allowed = causal(block)
    for index in range(query.shape[1] // block):
        start, stop = index * block, (index + 1) * block
        part = query[:, start:stop]
        near = contract(key[:, start:stop], part, 0, 0)
        near = jnp.where(allowed, near, masked_value)
        top = jnp.max(near, 0, keepdims=True)
        if index:
            far = contract(key[:, :start], part, 0, 0)
            top = jnp.maximum(top, jnp.max(far, 0, keepdims=True))
        near = jnp.exp(near - top)
        total = jnp.sum(near, 0, keepdims=True)
        if index:
            far = jnp.exp(far - top)
            total = total + jnp.sum(far, 0, keepdims=True)
        share = 1.0 / total
        result = contract(value[:, start:stop], (near * share).astype(jnp.bfloat16), 1, 0)
        if index:
            result = result + contract(value[:, :start], (far * share).astype(jnp.bfloat16), 1, 0)
        out_ref[0, :, start:stop] = result.astype(jnp.bfloat16)
        lse_ref[0, :, start:stop] = top + jnp.log(total)


def backward_kernel(
    group_ref, qp_ref, kp_ref, q_ref, k_ref, v_ref, do_ref, lse_ref, cos_ref, sin_ref,
    gq_ref, gk_ref,
    gqp_ref, gkp_ref, gv_ref, gain_q_ref, gain_k_ref,
    dq_ref, dk_ref, dv_ref, sum_q_ref, sum_k_ref, *, block,
):
    head = pl.program_id(0)
    heads = pl.num_programs(0)
    group = group_ref[head]
    opens = jnp.logical_or(head == 0, group_ref[jnp.maximum(head - 1, 0)] != group)
    closes = jnp.logical_or(
        head == heads - 1, group_ref[jnp.minimum(head + 1, heads - 1)] != group
    )

    @pl.when(head == 0)
    def _():
        sum_q_ref[...] = jnp.zeros_like(sum_q_ref)
        sum_k_ref[...] = jnp.zeros_like(sum_k_ref)

    @pl.when(opens)
    def _():
        dk_ref[...] = jnp.zeros_like(dk_ref)
        dv_ref[...] = jnp.zeros_like(dv_ref)

    query, key, value, grad = q_ref[0], k_ref[0], v_ref[0], do_ref[...]
    allowed = causal(block)
    for index in range(query.shape[1] // block):
        start, stop = index * block, (index + 1) * block
        part, grad_part = query[:, start:stop], grad[:, start:stop]
        sums_log = lse_ref[0, :, start:stop]
        near = jnp.exp(contract(key[:, start:stop], part, 0, 0) - sums_log)
        near = jnp.where(allowed, near, 0.0)
        grad_near = contract(value[:, start:stop], grad_part, 0, 0)
        inner = jnp.sum(near * grad_near, 0, keepdims=True)
        if index:
            far = jnp.exp(contract(key[:, :start], part, 0, 0) - sums_log)
            grad_far = contract(value[:, :start], grad_part, 0, 0)
            inner = inner + jnp.sum(far * grad_far, 0, keepdims=True)
        step = (near * (grad_near - inner)).astype(jnp.bfloat16)
        total = contract(key[:, start:stop], step, 1, 0)
        dk_ref[:, start:stop] += contract(part, step, 1, 1)
        dv_ref[:, start:stop] += contract(grad_part, near.astype(jnp.bfloat16), 1, 1)
        if index:
            step = (far * (grad_far - inner)).astype(jnp.bfloat16)
            total = total + contract(key[:, :start], step, 1, 0)
            dk_ref[:, :start] += contract(part, step, 1, 1)
            dv_ref[:, :start] += contract(grad_part, far.astype(jnp.bfloat16), 1, 1)
        dq_ref[:, start:stop] = total * 0.125

    cosine, sine = cos_ref[...], sin_ref[...]
    qp = qp_ref[...]
    grad_qp, gain_terms = unrotated_norm_back(
        dq_ref[...].astype(jnp.bfloat16).astype(jnp.float32),
        qp, head_scale(qp), gq_ref[...], cosine, sine,
    )
    gqp_ref[...] = grad_qp.astype(jnp.bfloat16)
    sum_q_ref[...] += gain_terms

    @pl.when(closes)
    def _():
        kp = kp_ref[...]
        grad_kp, terms = unrotated_norm_back(
            dk_ref[...].astype(jnp.bfloat16).astype(jnp.float32),
            kp, head_scale(kp), gk_ref[...], cosine, sine,
        )
        gkp_ref[0] = grad_kp.astype(jnp.bfloat16)
        gv_ref[0] = dv_ref[...].astype(jnp.bfloat16)
        sum_k_ref[...] += terms

    @pl.when(head == heads - 1)
    def _():
        gain_q_ref[...] = jnp.sum(sum_q_ref[...], 1, keepdims=True)
        gain_k_ref[...] = jnp.sum(sum_k_ref[...], 1, keepdims=True)


def attention_specs(length, heads):
    half = HEAD_SIZE // 2
    tall = (HEAD_SIZE, length)
    whole = lambda shape: pl.BlockSpec(shape, lambda h, g: (0, 0))
    per_head = pl.BlockSpec((1,) + tall, lambda h, g: (h, 0, 0))
    per_group = pl.BlockSpec((1,) + tall, lambda h, g: (g[h], 0, 0))
    per_row = pl.BlockSpec((1, 1, length), lambda h, g: (h, 0, 0))
    query = pl.BlockSpec(tall, lambda h, g: (h, 0))
    key = pl.BlockSpec(tall, lambda h, g: (heads + g[h], 0))
    value = pl.BlockSpec(tall, lambda h, g: (heads + 2 + g[h], 0))
    table = whole((half, length))
    gain = whole((HEAD_SIZE, 1))
    return (query, key, value, per_head, per_group, per_row, table, gain)


def attend(groups, mixed, cosine, sine, gain_q, gain_k, heads):
    length = mixed.shape[1]
    query, key, value, per_head, per_group, per_row, table, gain = attention_specs(length, heads)
    per = lambda count: jax.ShapeDtypeStruct((count, HEAD_SIZE, length), jnp.bfloat16)
    scores = heads * length * length // 2
    return pl.pallas_call(
        functools.partial(forward_kernel, block=min(256, length)),
        name="attention_forward",
        out_shape=(
            per(heads), per(2), per(2), per(heads),
            jax.ShapeDtypeStruct((heads, 1, length), jnp.float32),
        ),
        grid_spec=pltpu.PrefetchScalarGridSpec(
            num_scalar_prefetch=1,
            grid=(heads,),
            in_specs=[query, key, value, table, table, gain, gain],
            out_specs=[per_head, per_group, per_group, per_head, per_row],
        ),
        compiler_params=pltpu.CompilerParams(
            dimension_semantics=("arbitrary",), vmem_limit_bytes=VMEM_LIMIT
        ),
        cost_estimate=pl.CostEstimate(
            flops=scores * 4 * HEAD_SIZE, transcendentals=scores, bytes_accessed=8_000_000
        ),
    )(groups, mixed, mixed, mixed, cosine, sine, gain_q, gain_k)


def attend_back(groups, mixed, query_rows, key_rows, value_rows, grads, lse, cosine, sine, gain_q, gain_k, heads):
    length = mixed.shape[1]
    query, key, value, per_head, per_group, per_row, table, gain = attention_specs(length, heads)
    tall = (HEAD_SIZE, length)
    scores = heads * length * length // 2
    return pl.pallas_call(
        functools.partial(backward_kernel, block=min(256, length)),
        name="attention_backward",
        out_shape=(
            jax.ShapeDtypeStruct((heads * HEAD_SIZE, length), jnp.bfloat16),
            jax.ShapeDtypeStruct((2,) + tall, jnp.bfloat16),
            jax.ShapeDtypeStruct((2,) + tall, jnp.bfloat16),
            jax.ShapeDtypeStruct((HEAD_SIZE, 1), jnp.float32),
            jax.ShapeDtypeStruct((HEAD_SIZE, 1), jnp.float32),
        ),
        grid_spec=pltpu.PrefetchScalarGridSpec(
            num_scalar_prefetch=1,
            grid=(heads,),
            in_specs=[
                query, key, per_head, per_group, per_group, query, per_row, table, table, gain, gain,
            ],
            out_specs=[query, per_group, per_group, gain, gain],
            scratch_shapes=[pltpu.VMEM(tall, jnp.float32)] * 5,
        ),
        compiler_params=pltpu.CompilerParams(
            dimension_semantics=("arbitrary",), vmem_limit_bytes=VMEM_LIMIT
        ),
        cost_estimate=pl.CostEstimate(
            flops=scores * 10 * HEAD_SIZE, transcendentals=scores, bytes_accessed=10_000_000
        ),
    )(groups, mixed, mixed, query_rows, key_rows, value_rows, grads, lse, cosine, sine, gain_q, gain_k)


def adamw(weight, grad, first, second, rate, shrink, item_count):
    first_new = beta_first * first + (1.0 - beta_first) * grad
    second_new = beta_second * second + (1.0 - beta_second) * grad * grad
    fix_first = 1.0 - jnp.power(beta_first, item_count)
    fix_second = 1.0 - jnp.power(beta_second, item_count)
    stepped = first_new / fix_first / (jnp.sqrt(second_new / fix_second) + adam_eps)
    return (
        weight - rate * (stepped + shrink * weight),
        jnp.stack([first_new, jnp.sqrt(second_new)]),
    )


def local(
    sizes,
    tokens,
    cotangent,
    corpus_id,
    corpus_weight,
    step_count,
    qkv_weight,
    out_weight,
    gains,
    gate_weight,
    up_weight,
    down_weight,
    first_qkv,
    first_out,
    first_gains,
    first_gate,
    first_up,
    first_down,
    second_qkv,
    second_out,
    second_gains,
    second_gate,
    second_up,
    second_down,
):
    low = jnp.bfloat16
    high = jnp.float32
    devices = int(np.prod(sizes))
    seqs = sizes[0] * sizes[1]
    parts = sizes[2] * sizes[3]
    places = np.arange(devices).reshape(sizes)
    where = np.stack(np.unravel_index(np.arange(devices), sizes), -1)

    def permute(array, target):
        pairs = [(int(i), int(places[tuple(target(*where[i]))])) for i in range(devices)]
        return lax.ppermute(array, ALL, pairs)

    def swap(array):
        return permute(array, lambda sh, sl, kh, kl: (sh, kl, kh, sl))

    def in_ffn_group(array, r):
        return permute(array, lambda sh, sl, kh, kl: (sh, sl ^ (r & 1), kh ^ (r >> 1), kl))

    def in_sequence(array, r):
        return permute(array, lambda sh, sl, kh, kl: (sh, sl, kh ^ (r >> 1), kl ^ (r & 1)))

    item_count, model = tokens.shape
    heads = QUERY_HEADS // parts
    width = heads * HEAD_SIZE
    pair = 2 * HEAD_SIZE
    keys_at = QUERY_HEADS * HEAD_SIZE
    values_at = keys_at + VALUE_GROUPS * HEAD_SIZE
    kv = lax.axis_index(KV)
    length = item_count * parts
    cosine, sine = angle_tables(length)
    groups = ((jnp.arange(heads, dtype=jnp.int32) + kv) // 4).astype(jnp.int32)

    qkv_low = qkv_weight.astype(low)
    qkv_parts = jnp.stack(
        [
            jnp.concatenate(
                [
                    qkv_low[:, d * width : (d + 1) * width],
                    qkv_low[:, keys_at + d * HEAD_SIZE : keys_at + d * HEAD_SIZE + pair],
                    qkv_low[:, values_at + d * HEAD_SIZE : values_at + d * HEAD_SIZE + pair],
                ],
                axis=1,
            )
            for d in range(parts)
        ]
    )
    qkv_rows = lax.all_to_all(qkv_parts, KV, split_axis=0, concat_axis=0, tiled=True)
    qkv_full = lax.all_gather(
        qkv_rows.reshape(-1, width + 2 * pair), SEQ, axis=0, tiled=True
    )
    gains_low = lax.all_to_all(
        jnp.broadcast_to(gains.astype(low)[None], (devices, gains.shape[0])),
        ALL, split_axis=0, concat_axis=0, tiled=True,
    ).reshape(-1)
    gain_values = gains_low.astype(high)
    out_rows = lax.all_gather(out_weight.astype(low), SEQ, axis=0, tiled=True)
    gate_full = lax.all_gather(swap(gate_weight.astype(low)), OWNERS, axis=0, tiled=True)
    up_full = lax.all_gather(swap(up_weight.astype(low)), OWNERS, axis=0, tiled=True)
    down_full = lax.all_gather(swap(down_weight.astype(low)), OWNERS, axis=0, tiled=True)

    all_rows = jnp.zeros((parts, item_count, model), low)
    all_rows = lax.dynamic_update_slice_in_dim(all_rows, tokens[None], kv, 0)
    for r in range(1, parts):
        all_rows = lax.dynamic_update_slice_in_dim(
            all_rows, in_sequence(tokens, r)[None], kv ^ r, 0
        )
    all_rows = all_rows.reshape(length, model).astype(high)
    normed = (all_rows * rms_scale(all_rows) * gain_values[:model]).astype(low)

    factor = jnp.sum(
        jnp.where(jnp.arange(corpus_weight.shape[0]) == corpus_id[0], corpus_weight, 0.0)
    )
    weighted = cotangent.astype(high) * factor
    weighted_low = weighted.astype(low)
    weighted_rows = jnp.concatenate(
        [weighted_low] + [in_ffn_group(weighted_low, r) for r in range(1, 4)], axis=0
    )

    gain_q = gain_values[2 * model : 2 * model + HEAD_SIZE].reshape(HEAD_SIZE, 1)
    gain_k = gain_values[2 * model + HEAD_SIZE :].reshape(HEAD_SIZE, 1)
    mixed = contract(qkv_full, normed, 0, 1)
    query_rows, key_rows, value_rows, result, lse = attend(
        groups, mixed, cosine, sine, gain_q, gain_k, heads
    )
    outgoing = jnp.stack(
        [result.reshape(width, length)[:, d * item_count : (d + 1) * item_count] for d in range(parts)]
    )
    attended = lax.all_to_all(outgoing, KV, split_axis=0, concat_axis=0, tiled=True).reshape(
        parts * width, item_count
    )

    out_near = out_rows.reshape(seqs, 1, -1, model)
    out_far = in_sequence(out_near, 2)
    out_full = jnp.zeros((seqs, parts) + out_near.shape[2:], low)
    for r, piece in enumerate((out_near, in_sequence(out_near, 1), out_far, in_sequence(out_far, 1))):
        out_full = lax.dynamic_update_slice_in_dim(out_full, piece, kv ^ r, 1)
    out_full = out_full.reshape(-1, model)
    inputs = tokens.astype(high)
    hidden = inputs + contract(attended, out_full, 0, 0)

    scale_two = rms_scale(hidden)
    gain_two = gain_values[model : 2 * model]
    normed_two = (hidden * scale_two * gain_two).astype(low)
    ffn_rows = jnp.concatenate(
        [normed_two] + [in_ffn_group(normed_two, r) for r in range(1, 4)], axis=0
    )
    gate = contract(ffn_rows, gate_full, 1, 0)
    up_part = contract(ffn_rows, up_full, 1, 0)
    sigma = jax.nn.sigmoid(gate)
    swish = gate * sigma
    acted = (swish * up_part).astype(low)

    def to_owners(partial):
        blocks = partial.reshape(4, item_count, model)
        total = blocks[0]
        for r in range(1, 4):
            total = total + in_ffn_group(blocks[r].astype(low), r).astype(high)
        return total

    def share(grad):
        return swap(
            lax.psum_scatter(grad.astype(low), OWNERS, scatter_dimension=0, tiled=True)
        ).astype(high)

    grad_down = share(contract(weighted_rows, acted, 0, 0))
    grad_acted = contract(weighted_rows, down_full, 1, 0)
    grad_gate = (grad_acted * up_part * sigma * (1.0 + gate * (1.0 - sigma))).astype(low)
    grad_up = (grad_acted * swish).astype(low)
    grad_normed_two = to_owners(
        contract(grad_gate, gate_full, 1, 1) + contract(grad_up, up_full, 1, 1)
    )
    grad_gate_w = share(contract(ffn_rows, grad_gate, 0, 0))
    grad_up_w = share(contract(ffn_rows, grad_up, 0, 0))
    ffn = to_owners(contract(acted, down_full, 1, 1))
    block_out = (hidden + ffn).astype(low)

    pushed_two, gain_two_terms = norm_back(grad_normed_two, hidden, scale_two, gain_two)
    grad_hidden = weighted + pushed_two
    hidden_low = grad_hidden.astype(low)

    attended_gradient = contract(out_full, hidden_low, 1, 1).astype(low)
    incoming = lax.all_to_all(
        attended_gradient.reshape(parts, width, item_count), KV, split_axis=0, concat_axis=0, tiled=True
    )
    grads = jnp.concatenate([incoming[d] for d in range(parts)], axis=1)
    grad_queries, grad_keys, grad_values, gain_q_sum, gain_k_sum = attend_back(
        groups, mixed, query_rows, key_rows, value_rows, grads, lse,
        cosine, sine, gain_q, gain_k, heads,
    )
    grad_mixed = jnp.concatenate(
        [grad_queries, grad_keys.reshape(pair, length), grad_values.reshape(pair, length)], axis=0
    )
    grad_mixer = contract(normed, grad_mixed, 0, 1).astype(low)
    mixer_share = lax.psum_scatter(grad_mixer, SEQ, scatter_dimension=0, tiled=True)
    mixer_parts = lax.all_to_all(
        mixer_share.reshape(parts, -1, width + 2 * pair), KV, split_axis=0, concat_axis=0, tiled=True
    ).astype(high)
    slots = [[None] * VALUE_GROUPS, [None] * VALUE_GROUPS]
    for d in range(parts):
        for kind in range(2):
            for j in range(2):
                at = width + kind * pair + j * HEAD_SIZE
                piece = mixer_parts[d, :, at : at + HEAD_SIZE]
                held = slots[kind][d + j]
                slots[kind][d + j] = piece if held is None else held + piece
    qkv_grad = jnp.concatenate(
        [mixer_parts[d, :, :width] for d in range(parts)] + slots[0] + slots[1], axis=1
    )

    grad_normed = contract(grad_mixed, qkv_full, 0, 1).astype(low)
    grad_normed = jnp.sum(
        lax.all_to_all(
            grad_normed.reshape(parts, item_count, model), KV, split_axis=0, concat_axis=0, tiled=True
        ).astype(high),
        axis=0,
    )
    pushed_one, gain_one_terms = norm_back(
        grad_normed, inputs, rms_scale(inputs), gain_values[:model]
    )
    grad_input = grad_hidden + pushed_one

    grad_output = contract(attended, hidden_low, 1, 0)
    blocks = grad_output.reshape(seqs, 2, 2, -1, model)
    is_low = lax.axis_index("kl") == 0
    kept = jnp.where(is_low, blocks[:, :, 0], blocks[:, :, 1])
    sent = jnp.where(is_low, blocks[:, :, 1], blocks[:, :, 0]).astype(low)
    blocks = kept + in_sequence(sent, 1).astype(high)
    is_first = lax.axis_index("kh") == 0
    kept = jnp.where(is_first, blocks[:, 0], blocks[:, 1])
    sent = jnp.where(is_first, blocks[:, 1], blocks[:, 0]).astype(low)
    blocks = kept + in_sequence(sent, 2).astype(high)
    out_grad = lax.psum_scatter(
        blocks.astype(low).reshape(-1, model), SEQ, scatter_dimension=0, tiled=True
    ).astype(high)

    grad_gains = jnp.concatenate(
        [
            jnp.sum(gain_one_terms, 0),
            jnp.sum(gain_two_terms, 0),
            gain_q_sum.reshape(-1),
            gain_k_sum.reshape(-1),
        ]
    )
    gains_grad = jnp.sum(
        lax.all_to_all(
            grad_gains.reshape(devices, -1), ALL, split_axis=0, concat_axis=0, tiled=True
        ),
        axis=0,
    )

    steps_done = step_count[0].astype(high)
    new_qkv, moments_qkv = adamw(qkv_weight, qkv_grad, first_qkv, second_qkv, 0.02, 0.1, steps_done)
    new_out, moments_out = adamw(out_weight, out_grad, first_out, second_out, 0.2, 0.1, steps_done)
    new_gains, moments_gains = adamw(
        gains, gains_grad, first_gains, second_gains, 0.6, 0.0, steps_done
    )
    new_gate, moments_gate = adamw(
        gate_weight, grad_gate_w, first_gate, second_gate, 0.02, 0.1, steps_done
    )
    new_up, moments_up = adamw(up_weight, grad_up_w, first_up, second_up, 0.02, 0.1, steps_done)
    new_down, moments_down = adamw(
        down_weight, grad_down, first_down, second_down, 0.013, 0.1, steps_done
    )
    return (
        block_out,
        grad_input,
        new_qkv,
        moments_qkv,
        new_out,
        moments_out,
        new_gains,
        moments_gains,
        new_gate,
        moments_gate,
        new_up,
        moments_up,
        new_down,
        moments_down,
    )


def solution(mesh):
    seqs, parts = mesh.shape["seq"], mesh.shape["kv"]
    sizes = (seqs // 2, 2, parts // 2, 2)
    fine = Mesh(mesh.devices.reshape(sizes), ALL)
    rows = P(ALL, None)
    block = P(SEQ, KV)
    return jax.shard_map(
        functools.partial(local, sizes),
        mesh=fine,
        in_specs=(
            rows, rows, P(SEQ), P(), P(),
            rows, rows, P(ALL), block, block, block,
            rows, rows, P(ALL), block, block, block,
            rows, rows, P(ALL), block, block, block,
        ),
        out_specs=(
            rows, rows,
            rows, P(None, ALL, None),
            rows, P(None, ALL, None),
            P(ALL), P(None, ALL),
            block, P(None, SEQ, KV),
            block, P(None, SEQ, KV),
            block, P(None, SEQ, KV),
        ),
        check_vma=False,
    )
```

```python
import functools

import jax
import jax.numpy as jnp
import numpy as np
from jax import lax
from jax.experimental import pallas as pl
from jax.experimental.pallas import tpu as pltpu
from jax.sharding import Mesh, PartitionSpec as P

QUERY_HEADS = 20
VALUE_GROUPS = 5
HEAD_SIZE = 64

eps_norm = 1e-06
masked_value = -1e30
beta_first = 0.9
beta_second = 0.95
adam_eps = 1e-08

ALL = ("sh", "sl", "kh", "kl")
SEQ = ("sh", "sl")
KV = ("kh", "kl")
OWNERS = ("sh", "kl")
VMEM_LIMIT = 40 * 1024 * 1024


def rms_scale(value_rows):
    return lax.rsqrt(jnp.mean(value_rows * value_rows, -1, keepdims=True) + eps_norm)


def norm_back(grad_out, value_rows, scale, gain):
    shaped = value_rows * scale
    pushed = grad_out * gain
    grad_in = scale * (pushed - shaped * jnp.mean(pushed * shaped, -1, keepdims=True))
    return (grad_in, grad_out * shaped)


def angle_tables(item_count):
    places = np.arange(item_count).astype(np.float32)
    steps = np.arange(HEAD_SIZE // 2).astype(np.float32) * np.float32(2.0) / np.float32(HEAD_SIZE)
    freqs = np.float32(10000.0) ** (-steps)
    angles = freqs[:, None].astype(np.float32) * places[None, :]
    return (np.cos(angles).astype(np.float32), np.sin(angles).astype(np.float32))


def contract(left, right, left_dim, right_dim):
    return lax.dot_general(
        left,
        right,
        (((left_dim,), (right_dim,)), ((), ())),
        preferred_element_type=jnp.float32,
    )


def head_scale(rows):
    return lax.rsqrt(jnp.mean(rows * rows, 0, keepdims=True) + eps_norm)


def rotated(rows, scale, gain, cosine, sine):
    half = HEAD_SIZE // 2
    shaped = rows * scale * gain
    first, second = shaped[:half], shaped[half:]
    return jnp.concatenate(
        [first * cosine - second * sine, second * cosine + first * sine], axis=0
    )


def unrotated_norm_back(grad, rows, scale, gain, cosine, sine):
    half = HEAD_SIZE // 2
    first, second = grad[:half], grad[half:]
    turned = jnp.concatenate(
        [first * cosine + second * sine, second * cosine - first * sine], axis=0
    )
    shaped = rows * scale
    pushed = turned * gain
    grad_in = scale * (pushed - shaped * jnp.mean(pushed * shaped, 0, keepdims=True))
    return (grad_in, turned * shaped)


def causal(block):
    keys = lax.broadcasted_iota(jnp.int32, (block, block), 0)
    places = lax.broadcasted_iota(jnp.int32, (block, block), 1)
    return keys <= places


def forward_kernel(
    group_ref, qp_ref, kp_ref, vp_ref, cos_ref, sin_ref, gq_ref, gk_ref,
    q_ref, k_ref, v_ref, out_ref, lse_ref, *, block,
):
    cosine, sine = cos_ref[...], sin_ref[...]
    qp, kp = qp_ref[...], kp_ref[...]
    query = (rotated(qp, head_scale(qp), gq_ref[...], cosine, sine) * 0.125).astype(jnp.bfloat16)
    key = rotated(kp, head_scale(kp), gk_ref[...], cosine, sine).astype(jnp.bfloat16)
    value = vp_ref[...].astype(jnp.bfloat16)
    q_ref[0] = query
    k_ref[0] = key
    v_ref[0] = value
    allowed = causal(block)
    for index in range(query.shape[1] // block):
        start, stop = index * block, (index + 1) * block
        part = query[:, start:stop]
        near = contract(key[:, start:stop], part, 0, 0)
        near = jnp.where(allowed, near, masked_value)
        top = jnp.max(near, 0, keepdims=True)
        if index:
            far = contract(key[:, :start], part, 0, 0)
            top = jnp.maximum(top, jnp.max(far, 0, keepdims=True))
        near = jnp.exp(near - top)
        total = jnp.sum(near, 0, keepdims=True)
        if index:
            far = jnp.exp(far - top)
            total = total + jnp.sum(far, 0, keepdims=True)
        share = 1.0 / total
        result = contract(value[:, start:stop], (near * share).astype(jnp.bfloat16), 1, 0)
        if index:
            result = result + contract(value[:, :start], (far * share).astype(jnp.bfloat16), 1, 0)
        out_ref[0, :, start:stop] = result.astype(jnp.bfloat16)
        lse_ref[0, :, start:stop] = top + jnp.log(total)


def backward_kernel(
    group_ref, qp_ref, kp_ref, q_ref, k_ref, v_ref, do_ref, lse_ref, cos_ref, sin_ref,
    gq_ref, gk_ref,
    gqp_ref, gkp_ref, gv_ref, gain_q_ref, gain_k_ref,
    dq_ref, dk_ref, dv_ref, sum_q_ref, sum_k_ref, *, block,
):
    head = pl.program_id(0)
    heads = pl.num_programs(0)
    group = group_ref[head]
    opens = jnp.logical_or(head == 0, group_ref[jnp.maximum(head - 1, 0)] != group)
    closes = jnp.logical_or(
        head == heads - 1, group_ref[jnp.minimum(head + 1, heads - 1)] != group
    )

    @pl.when(head == 0)
    def _():
        sum_q_ref[...] = jnp.zeros_like(sum_q_ref)
        sum_k_ref[...] = jnp.zeros_like(sum_k_ref)

    @pl.when(opens)
    def _():
        dk_ref[...] = jnp.zeros_like(dk_ref)
        dv_ref[...] = jnp.zeros_like(dv_ref)

    query, key, value, grad = q_ref[0], k_ref[0], v_ref[0], do_ref[...]
    allowed = causal(block)
    for index in range(query.shape[1] // block):
        start, stop = index * block, (index + 1) * block
        part, grad_part = query[:, start:stop], grad[:, start:stop]
        sums_log = lse_ref[0, :, start:stop]
        near = jnp.exp(contract(key[:, start:stop], part, 0, 0) - sums_log)
        near = jnp.where(allowed, near, 0.0)
        grad_near = contract(value[:, start:stop], grad_part, 0, 0)
        inner = jnp.sum(near * grad_near, 0, keepdims=True)
        if index:
            far = jnp.exp(contract(key[:, :start], part, 0, 0) - sums_log)
            grad_far = contract(value[:, :start], grad_part, 0, 0)
            inner = inner + jnp.sum(far * grad_far, 0, keepdims=True)
        step = (near * (grad_near - inner)).astype(jnp.bfloat16)
        total = contract(key[:, start:stop], step, 1, 0)
        dk_ref[:, start:stop] += contract(part, step, 1, 1)
        dv_ref[:, start:stop] += contract(grad_part, near.astype(jnp.bfloat16), 1, 1)
        if index:
            step = (far * (grad_far - inner)).astype(jnp.bfloat16)
            total = total + contract(key[:, :start], step, 1, 0)
            dk_ref[:, :start] += contract(part, step, 1, 1)
            dv_ref[:, :start] += contract(grad_part, far.astype(jnp.bfloat16), 1, 1)
        dq_ref[:, start:stop] = total * 0.125

    cosine, sine = cos_ref[...], sin_ref[...]
    qp = qp_ref[...]
    grad_qp, gain_terms = unrotated_norm_back(
        dq_ref[...].astype(jnp.bfloat16).astype(jnp.float32),
        qp, head_scale(qp), gq_ref[...], cosine, sine,
    )
    gqp_ref[...] = grad_qp.astype(jnp.bfloat16)
    sum_q_ref[...] += gain_terms

    @pl.when(closes)
    def _():
        kp = kp_ref[...]
        grad_kp, terms = unrotated_norm_back(
            dk_ref[...].astype(jnp.bfloat16).astype(jnp.float32),
            kp, head_scale(kp), gk_ref[...], cosine, sine,
        )
        gkp_ref[0] = grad_kp.astype(jnp.bfloat16)
        gv_ref[0] = dv_ref[...].astype(jnp.bfloat16)
        sum_k_ref[...] += terms

    @pl.when(head == heads - 1)
    def _():
        gain_q_ref[...] = jnp.sum(sum_q_ref[...], 1, keepdims=True)
        gain_k_ref[...] = jnp.sum(sum_k_ref[...], 1, keepdims=True)


def attention_specs(length, heads):
    half = HEAD_SIZE // 2
    tall = (HEAD_SIZE, length)
    whole = lambda shape: pl.BlockSpec(shape, lambda h, g: (0, 0))
    per_head = pl.BlockSpec((1,) + tall, lambda h, g: (h, 0, 0))
    per_group = pl.BlockSpec((1,) + tall, lambda h, g: (g[h], 0, 0))
    per_row = pl.BlockSpec((1, 1, length), lambda h, g: (h, 0, 0))
    query = pl.BlockSpec(tall, lambda h, g: (h, 0))
    key = pl.BlockSpec(tall, lambda h, g: (heads + g[h], 0))
    value = pl.BlockSpec(tall, lambda h, g: (heads + 2 + g[h], 0))
    table = whole((half, length))
    gain = whole((HEAD_SIZE, 1))
    return (query, key, value, per_head, per_group, per_row, table, gain)


def attend(groups, mixed, cosine, sine, gain_q, gain_k, heads):
    length = mixed.shape[1]
    query, key, value, per_head, per_group, per_row, table, gain = attention_specs(length, heads)
    per = lambda count: jax.ShapeDtypeStruct((count, HEAD_SIZE, length), jnp.bfloat16)
    scores = heads * length * length // 2
    return pl.pallas_call(
        functools.partial(forward_kernel, block=min(256, length)),
        name="attention_forward",
        out_shape=(
            per(heads), per(2), per(2), per(heads),
            jax.ShapeDtypeStruct((heads, 1, length), jnp.float32),
        ),
        grid_spec=pltpu.PrefetchScalarGridSpec(
            num_scalar_prefetch=1,
            grid=(heads,),
            in_specs=[query, key, value, table, table, gain, gain],
            out_specs=[per_head, per_group, per_group, per_head, per_row],
        ),
        compiler_params=pltpu.CompilerParams(
            dimension_semantics=("arbitrary",), vmem_limit_bytes=VMEM_LIMIT
        ),
        cost_estimate=pl.CostEstimate(
            flops=scores * 4 * HEAD_SIZE, transcendentals=scores, bytes_accessed=8_000_000
        ),
    )(groups, mixed, mixed, mixed, cosine, sine, gain_q, gain_k)


def attend_back(groups, mixed, query_rows, key_rows, value_rows, grads, lse, cosine, sine, gain_q, gain_k, heads):
    length = mixed.shape[1]
    query, key, value, per_head, per_group, per_row, table, gain = attention_specs(length, heads)
    tall = (HEAD_SIZE, length)
    scores = heads * length * length // 2
    return pl.pallas_call(
        functools.partial(backward_kernel, block=min(256, length)),
        name="attention_backward",
        out_shape=(
            jax.ShapeDtypeStruct((heads * HEAD_SIZE, length), jnp.bfloat16),
            jax.ShapeDtypeStruct((2,) + tall, jnp.bfloat16),
            jax.ShapeDtypeStruct((2,) + tall, jnp.bfloat16),
            jax.ShapeDtypeStruct((HEAD_SIZE, 1), jnp.float32),
            jax.ShapeDtypeStruct((HEAD_SIZE, 1), jnp.float32),
        ),
        grid_spec=pltpu.PrefetchScalarGridSpec(
            num_scalar_prefetch=1,
            grid=(heads,),
            in_specs=[
                query, key, per_head, per_group, per_group, query, per_row, table, table, gain, gain,
            ],
            out_specs=[query, per_group, per_group, gain, gain],
            scratch_shapes=[pltpu.VMEM(tall, jnp.float32)] * 5,
        ),
        compiler_params=pltpu.CompilerParams(
            dimension_semantics=("arbitrary",), vmem_limit_bytes=VMEM_LIMIT
        ),
        cost_estimate=pl.CostEstimate(
            flops=scores * 10 * HEAD_SIZE, transcendentals=scores, bytes_accessed=10_000_000
        ),
    )(groups, mixed, mixed, query_rows, key_rows, value_rows, grads, lse, cosine, sine, gain_q, gain_k)


def block_order_kernel(mine_ref, in_ref, out_ref, *, offsets, back, columns):
    mine = mine_ref[0]
    for index, offset in enumerate(offsets):
        held = mine ^ offset
        if columns:
            width = in_ref.shape[1] // len(offsets)
            held = pl.ds(pl.multiple_of(held * width, width), width)
            here = slice(index * width, (index + 1) * width)
            if back:
                out_ref[:, held] = in_ref[:, here]
            else:
                out_ref[:, here] = in_ref[:, held]
        elif back:
            out_ref[held] = in_ref[index]
        else:
            out_ref[index] = in_ref[held]


def block_order(array, mine, offsets, back=False, columns=False):
    if columns and array.shape[1] // len(offsets) % 128:
        width = array.shape[1] // len(offsets)
        sources = [mine ^ offset for offset in offsets]
        if back:
            place = {offset: index for index, offset in enumerate(offsets)}
            table = jnp.array([place[v] for v in range(len(offsets))], jnp.int32)
            sources = [
                jnp.sum(jnp.where(jnp.arange(len(offsets)) == (mine ^ j), table, 0))
                for j in range(len(offsets))
            ]
        return jnp.concatenate(
            [lax.dynamic_slice_in_dim(array, at * width, width, 1) for at in sources], axis=1
        )
    return pl.pallas_call(
        functools.partial(
            block_order_kernel, offsets=tuple(offsets), back=back, columns=columns
        ),
        name="block_order",
        out_shape=jax.ShapeDtypeStruct(array.shape, array.dtype),
        in_specs=[
            pl.BlockSpec(memory_space=pltpu.SMEM),
            pl.BlockSpec(memory_space=pltpu.VMEM),
        ],
        out_specs=pl.BlockSpec(memory_space=pltpu.VMEM),
        compiler_params=pltpu.CompilerParams(vmem_limit_bytes=VMEM_LIMIT),
        cost_estimate=pl.CostEstimate(
            flops=0, transcendentals=0, bytes_accessed=4 * array.size
        ),
    )(mine.reshape(1).astype(jnp.int32), array)


def adamw(weight, grad, first, second, rate, shrink, item_count):
    first_new = beta_first * first + (1.0 - beta_first) * grad
    second_new = beta_second * second + (1.0 - beta_second) * grad * grad
    fix_first = 1.0 - jnp.power(beta_first, item_count)
    fix_second = 1.0 - jnp.power(beta_second, item_count)
    stepped = first_new / fix_first / (jnp.sqrt(second_new / fix_second) + adam_eps)
    return (
        weight - rate * (stepped + shrink * weight),
        jnp.stack([first_new, jnp.sqrt(second_new)]),
    )


def local(
    sizes,
    tokens,
    cotangent,
    corpus_id,
    corpus_weight,
    step_count,
    qkv_weight,
    out_weight,
    gains,
    gate_weight,
    up_weight,
    down_weight,
    first_qkv,
    first_out,
    first_gains,
    first_gate,
    first_up,
    first_down,
    second_qkv,
    second_out,
    second_gains,
    second_gate,
    second_up,
    second_down,
):
    low = jnp.bfloat16
    high = jnp.float32
    devices = int(np.prod(sizes))
    seqs = sizes[0] * sizes[1]
    parts = sizes[2] * sizes[3]
    places = np.arange(devices).reshape(sizes)
    where = np.stack(np.unravel_index(np.arange(devices), sizes), -1)

    def permute(array, target):
        pairs = [(int(i), int(places[tuple(target(*where[i]))])) for i in range(devices)]
        return lax.ppermute(array, ALL, pairs)

    def swap(array):
        return permute(array, lambda sh, sl, kh, kl: (sh, kl, kh, sl))

    def in_ffn_group(array, r):
        return permute(array, lambda sh, sl, kh, kl: (sh, sl ^ (r & 1), kh ^ (r >> 1), kl))

    def in_sequence(array, r):
        return permute(array, lambda sh, sl, kh, kl: (sh, sl, kh ^ (r >> 1), kl ^ (r & 1)))

    def along_z(array, r):
        return permute(array, lambda sh, sl, kh, kl: (sh ^ r, sl, kh, kl))

    def along_y(array):
        return permute(array, lambda sh, sl, kh, kl: (sh, sl ^ 1, kh, kl))

    z_size = sizes[0]

    def gather_line(piece):
        return jnp.stack([piece] + [along_z(piece, r) for r in range(1, z_size)])

    def halve(blocks, index, axis, move):
        kept = lax.dynamic_index_in_dim(blocks, index, axis, keepdims=False)
        sent = lax.dynamic_index_in_dim(blocks, index ^ 1, axis, keepdims=False)
        return kept.astype(high) + move(sent.astype(low)).astype(high)

    def scatter_line(line):
        total = line[0]
        for r in range(1, z_size):
            total = total + along_z(line[r].astype(low), r).astype(high)
        return total

    item_count, model = tokens.shape
    heads = QUERY_HEADS // parts
    width = heads * HEAD_SIZE
    pair = 2 * HEAD_SIZE
    keys_at = QUERY_HEADS * HEAD_SIZE
    values_at = keys_at + VALUE_GROUPS * HEAD_SIZE
    kv = lax.axis_index(KV)
    length = item_count * parts
    cosine, sine = angle_tables(length)
    groups = ((jnp.arange(heads, dtype=jnp.int32) + kv) // 4).astype(jnp.int32)

    def stage(ready, waiting):
        return lax.optimization_barrier((ready, waiting))

    column_offsets = [rz * 2 + rs for rs in range(2) for rz in range(z_size)]
    row_offsets = [
        (rz * 2 + rs) * parts + r for r in range(parts) for rs in range(2) for rz in range(z_size)
    ]

    def columns_moved(array, back=False):
        return block_order(array, lax.axis_index(SEQ), column_offsets, back=back, columns=True)

    def rows_moved(array, back=False):
        blocks = array.reshape(devices, -1, item_count)
        return block_order(blocks, lax.axis_index(ALL), row_offsets, back=back).reshape(-1, item_count)

    gate_block = swap(gate_weight.astype(low))
    qkv_low = qkv_weight.astype(low)
    span = width + 2 * pair
    qkv_parts = jnp.stack(
        [
            jnp.concatenate(
                [
                    qkv_low[:, d * width : (d + 1) * width],
                    qkv_low[:, keys_at + d * HEAD_SIZE : keys_at + d * HEAD_SIZE + pair],
                    qkv_low[:, values_at + d * HEAD_SIZE : values_at + d * HEAD_SIZE + pair],
                ],
                axis=1,
            )
            for d in range(parts)
        ]
    )
    qkv_rows = lax.all_to_all(qkv_parts, KV, split_axis=0, concat_axis=0, tiled=True)
    moved_tokens = columns_moved(tokens)
    tokens_far = in_sequence(moved_tokens, 2)
    factor = jnp.sum(
        jnp.where(jnp.arange(corpus_weight.shape[0]) == corpus_id[0], corpus_weight, 0.0)
    )
    weighted = cotangent.astype(high) * factor
    (gate_block, qkv_rows, tokens_far), (up_low, down_low, out_low, tokens_near, weighted_low, gains_own) = stage(
        (gate_block, qkv_rows, tokens_far),
        (
            up_weight.astype(low), down_weight.astype(low), out_weight.astype(low), moved_tokens,
            weighted.astype(low), gains,
        ),
    )

    qkv_line = gather_line(qkv_rows.reshape(-1, span))
    out_line = gather_line(out_low)
    up_block = swap(up_low)
    down_block = swap(down_low)
    tokens_pair = (in_sequence(tokens_near, 1), in_sequence(tokens_far, 1))
    gains_low = lax.all_to_all(
        jnp.broadcast_to(gains_own.astype(low)[None], (devices, gains.shape[0])),
        ALL, split_axis=0, concat_axis=0, tiled=True,
    )
    weighted_far = in_ffn_group(weighted_low, 2)
    (qkv_line, out_line, tokens_pair, gains_low), (gate_block,) = stage(
        (qkv_line, out_line, tokens_pair, gains_low), (gate_block,)
    )
    gate_full = lax.all_gather(gate_block, OWNERS, axis=0, tiled=True)
    gain_values = gains_low.reshape(-1).astype(high)
    gain_one = gain_values[:model]
    gain_two = gain_values[model : 2 * model]
    gain_q = gain_values[2 * model : 2 * model + HEAD_SIZE].reshape(HEAD_SIZE, 1)
    gain_k = gain_values[2 * model + HEAD_SIZE :].reshape(HEAD_SIZE, 1)
    gain_moved = columns_moved(jnp.broadcast_to(gain_one[None], (8, model)))[:1]
    all_rows = jnp.zeros((parts, item_count, model), low)
    for r, piece in enumerate((tokens_near, tokens_pair[0], tokens_far, tokens_pair[1])):
        all_rows = lax.dynamic_update_slice_in_dim(all_rows, piece[None], kv ^ r, 0)
    all_rows = all_rows.reshape(length, model).astype(high)
    normed = (all_rows * rms_scale(all_rows) * gain_moved).astype(low)

    qkv_far = along_y(qkv_line)
    (qkv_far, weighted_far, normed), (out_line, up_block, weighted_low) = stage(
        (qkv_far, weighted_far, normed), (out_line, up_block, weighted_low)
    )
    up_full = lax.all_gather(up_block, OWNERS, axis=0, tiled=True)
    qkv_full = jnp.concatenate([qkv_line, qkv_far]).reshape(model, span)

    out_near = jnp.stack([out_line, along_y(out_line)])
    out_far = in_sequence(out_near, 2)
    mixed = contract(qkv_full, normed, 0, 1)
    query_rows, key_rows, value_rows, result, lse = attend(
        groups, mixed, cosine, sine, gain_q, gain_k, heads
    )
    outgoing = jnp.stack(
        [result.reshape(width, length)[:, d * item_count : (d + 1) * item_count] for d in range(parts)]
    )
    out_far, (outgoing, out_near, weighted_low, weighted_far, down_block) = stage(
        out_far, (outgoing, out_near, weighted_low, weighted_far, down_block)
    )
    down_full = lax.all_gather(down_block, OWNERS, axis=0, tiled=True)

    attended = rows_moved(
        lax.all_to_all(outgoing, KV, split_axis=0, concat_axis=0, tiled=True)
    )
    out_pair = (in_sequence(out_near, 1), in_sequence(out_far, 1))
    out_full = jnp.stack([out_near, out_pair[0], out_far, out_pair[1]]).reshape(-1, model)
    attended, weighted_low, weighted_far = lax.optimization_barrier(
        (attended, weighted_low, weighted_far)
    )
    weighted_rows = jnp.concatenate(
        [weighted_low, in_ffn_group(weighted_low, 1), weighted_far, in_ffn_group(weighted_far, 1)],
        axis=0,
    )
    inputs = tokens.astype(high)
    hidden = inputs + contract(attended, out_full, 0, 0)

    scale_two = rms_scale(hidden)
    normed_two = (hidden * scale_two * gain_two).astype(low)
    ffn_rows = jnp.concatenate(
        [normed_two] + [in_ffn_group(normed_two, r) for r in (1, 2, 3)], axis=0
    )
    gate = contract(ffn_rows, gate_full, 1, 0)
    up_part = contract(ffn_rows, up_full, 1, 0)
    sigma = jax.nn.sigmoid(gate)
    swish = gate * sigma
    acted = (swish * up_part).astype(low)

    def from_group(sent):
        return [
            in_ffn_group(sent[(r - 1) * item_count : r * item_count], r) for r in (1, 2, 3)
        ]

    def share(grad):
        return lax.psum_scatter(grad, OWNERS, scatter_dimension=0, tiled=True)

    grad_down_low = contract(weighted_rows, acted, 0, 0).astype(low)
    down_full, grad_down_low = stage(down_full, grad_down_low)
    grad_down_share = share(grad_down_low)
    grad_acted = contract(weighted_rows, down_full, 1, 0)
    grad_gate = (grad_acted * up_part * sigma * (1.0 + gate * (1.0 - sigma))).astype(low)
    grad_up = (grad_acted * swish).astype(low)
    rows_partial = contract(grad_gate, gate_full, 1, 1) + contract(grad_up, up_full, 1, 1)
    own_rows = rows_partial[:item_count]
    (sent_rows, own_rows), (grad_gate, grad_up) = stage(
        (rows_partial[item_count:].astype(low), own_rows), (grad_gate, grad_up)
    )
    received = from_group(sent_rows)
    grad_gate_low = contract(ffn_rows, grad_gate, 0, 0).astype(low)
    grad_up_low = contract(ffn_rows, grad_up, 0, 0).astype(low)
    ffn_partial = contract(acted, down_full, 1, 1).astype(low)
    received, (grad_gate_low, grad_up_low, ffn_partial) = stage(
        received, (grad_gate_low, grad_up_low, ffn_partial)
    )
    grad_gate_share = share(grad_gate_low)
    grad_up_share = share(grad_up_low)
    grad_normed_two = own_rows + sum(piece.astype(high) for piece in received)

    pushed_two, gain_two_terms = norm_back(grad_normed_two, hidden, scale_two, gain_two)
    grad_hidden = weighted + pushed_two
    hidden_low = grad_hidden.astype(low)

    attended_gradient = rows_moved(contract(out_full, hidden_low, 1, 1).astype(low), back=True)
    incoming = lax.all_to_all(
        attended_gradient.reshape(parts, width, item_count), KV, split_axis=0, concat_axis=0, tiled=True
    )
    ffn_blocks = ffn_partial.reshape(2, 2, item_count, model)
    ffn_line = [
        ffn_blocks[r, 0].astype(high) + in_ffn_group(ffn_blocks[r, 1], 1).astype(high) for r in range(2)
    ]
    attended = attended.reshape(2, 2, -1, item_count)
    sent_out = [contract(attended[r, 1], hidden_low, 1, 0).astype(low) for r in range(2)]
    kept_out = [contract(attended[r, 0], hidden_low, 1, 0) for r in range(2)]
    (incoming, kept_out), (sent_out,) = stage((incoming, kept_out), (sent_out,))
    grads = jnp.concatenate([incoming[d] for d in range(parts)], axis=1)

    out_line = [kept_out[r] + in_sequence(sent_out[r], 1).astype(high) for r in range(2)]
    out_line = out_line[0] + in_sequence(out_line[1].astype(low), 2).astype(high)
    grad_queries, grad_keys, grad_values, gain_q_sum, gain_k_sum = attend_back(
        groups, mixed, query_rows, key_rows, value_rows, grads, lse,
        cosine, sine, gain_q, gain_k, heads,
    )
    grad_mixed = jnp.concatenate(
        [grad_queries, grad_keys.reshape(pair, length), grad_values.reshape(pair, length)], axis=0
    )

    half_model = model // 2
    mixer_sent = contract(normed[:, half_model:], grad_mixed, 0, 1).astype(low)
    mixer_line = contract(normed[:, :half_model], grad_mixed, 0, 1)
    (mixer_sent, mixer_line), (grad_mixed, out_line, ffn_line) = stage(
        (mixer_sent, mixer_line), (grad_mixed, out_line, ffn_line)
    )
    mixer_line = mixer_line + along_y(mixer_sent).astype(high)
    out_line = out_line.reshape(2, z_size, -1, model)
    out_line = out_line[0] + along_y(out_line[1].astype(low)).astype(high)
    grad_normed = contract(grad_mixed, qkv_full, 0, 1).astype(low)
    grad_normed = halve(
        grad_normed.reshape(2, 2, item_count, model), lax.axis_index("kl"), 1, lambda v: in_sequence(v, 1)
    )
    (mixer_line, grad_normed), (ffn_line, grad_down_share, grad_gate_share) = stage(
        (mixer_line, grad_normed), (ffn_line, grad_down_share, grad_gate_share)
    )

    mixer_share = scatter_line(mixer_line.reshape(z_size, -1, span)).astype(low)
    out_grad = scatter_line(out_line)
    grad_normed = halve(grad_normed, lax.axis_index("kh"), 0, lambda v: in_sequence(v, 2))
    ffn = ffn_line[0] + in_ffn_group(ffn_line[1].astype(low), 2).astype(high)
    block_out = (hidden + ffn).astype(low)
    grad_down = swap(grad_down_share).astype(high)
    grad_gate_w = swap(grad_gate_share).astype(high)
    (mixer_share, grad_normed), (grad_up_share,) = stage(
        (mixer_share, grad_normed), (grad_up_share,)
    )

    mixer_parts = lax.all_to_all(
        mixer_share.reshape(parts, -1, span), KV, split_axis=0, concat_axis=0, tiled=True
    ).astype(high)
    slots = [[None] * VALUE_GROUPS, [None] * VALUE_GROUPS]
    for d in range(parts):
        for kind in range(2):
            for j in range(2):
                at = width + kind * pair + j * HEAD_SIZE
                piece = mixer_parts[d, :, at : at + HEAD_SIZE]
                held = slots[kind][d + j]
                slots[kind][d + j] = piece if held is None else held + piece
    qkv_grad = jnp.concatenate(
        [mixer_parts[d, :, :width] for d in range(parts)] + slots[0] + slots[1], axis=1
    )
    moved_inputs = tokens_near.astype(high)
    pushed_one, gain_one_terms = norm_back(
        grad_normed, moved_inputs, rms_scale(moved_inputs), gain_moved
    )
    grad_input = grad_hidden + columns_moved(pushed_one, back=True)
    gain_one_sum = columns_moved(
        jnp.broadcast_to(jnp.sum(gain_one_terms, 0)[None], (8, model)), back=True
    )[0]
    grad_gains = jnp.concatenate(
        [
            gain_one_sum,
            jnp.sum(gain_two_terms, 0),
            gain_q_sum.reshape(-1),
            gain_k_sum.reshape(-1),
        ]
    )
    gains_grad = jnp.sum(
        lax.all_to_all(
            grad_gains.reshape(devices, -1), ALL, split_axis=0, concat_axis=0, tiled=True
        ),
        axis=0,
    )
    grad_up_w = swap(grad_up_share).astype(high)

    steps_done = step_count[0].astype(high)
    new_qkv, moments_qkv = adamw(qkv_weight, qkv_grad, first_qkv, second_qkv, 0.02, 0.1, steps_done)
    new_out, moments_out = adamw(out_weight, out_grad, first_out, second_out, 0.2, 0.1, steps_done)
    new_gains, moments_gains = adamw(
        gains, gains_grad, first_gains, second_gains, 0.6, 0.0, steps_done
    )
    new_gate, moments_gate = adamw(
        gate_weight, grad_gate_w, first_gate, second_gate, 0.02, 0.1, steps_done
    )
    new_up, moments_up = adamw(up_weight, grad_up_w, first_up, second_up, 0.02, 0.1, steps_done)
    new_down, moments_down = adamw(
        down_weight, grad_down, first_down, second_down, 0.013, 0.1, steps_done
    )
    return (
        block_out,
        grad_input,
        new_qkv,
        moments_qkv,
        new_out,
        moments_out,
        new_gains,
        moments_gains,
        new_gate,
        moments_gate,
        new_up,
        moments_up,
        new_down,
        moments_down,
    )


def solution(mesh):
    seqs, parts = mesh.shape["seq"], mesh.shape["kv"]
    sizes = (seqs // 2, 2, parts // 2, 2)
    fine = Mesh(mesh.devices.reshape(sizes), ALL)
    rows = P(ALL, None)
    block = P(SEQ, KV)
    return jax.shard_map(
        functools.partial(local, sizes),
        mesh=fine,
        in_specs=(
            rows, rows, P(SEQ), P(), P(),
            rows, rows, P(ALL), block, block, block,
            rows, rows, P(ALL), block, block, block,
            rows, rows, P(ALL), block, block, block,
        ),
        out_specs=(
            rows, rows,
            rows, P(None, ALL, None),
            rows, P(None, ALL, None),
            P(ALL), P(None, ALL),
            block, P(None, SEQ, KV),
            block, P(None, SEQ, KV),
            block, P(None, SEQ, KV),
        ),
        check_vma=False,
    )
```

```python
import functools

import jax
import jax.numpy as jnp
import numpy as np
from jax import lax
from jax.experimental import pallas as pl
from jax.experimental.pallas import tpu as pltpu
from jax.sharding import Mesh, PartitionSpec as P

QUERY_HEADS = 20
VALUE_GROUPS = 5
HEAD_SIZE = 64

eps_norm = 1e-06
masked_value = -1e30
beta_first = 0.9
beta_second = 0.95
adam_eps = 1e-08

ALL = ("sh", "sl", "kh", "kl")
SEQ = ("sh", "sl")
KV = ("kh", "kl")
OWNERS = ("sh", "kl")
VMEM_LIMIT = 40 * 1024 * 1024
GAIN_ROWS = 8


def rms_scale(value_rows):
    return lax.rsqrt(jnp.mean(value_rows * value_rows, -1, keepdims=True) + eps_norm)


def norm_back(grad_out, value_rows, scale, gain):
    shaped = value_rows * scale
    pushed = grad_out * gain
    grad_in = scale * (pushed - shaped * jnp.mean(pushed * shaped, -1, keepdims=True))
    return (grad_in, grad_out * shaped)


def angle_tables(item_count):
    places = np.arange(item_count).astype(np.float32)
    steps = np.arange(HEAD_SIZE // 2).astype(np.float32) * np.float32(2.0) / np.float32(HEAD_SIZE)
    freqs = np.float32(10000.0) ** (-steps)
    angles = freqs[:, None].astype(np.float32) * places[None, :]
    return (np.cos(angles).astype(np.float32), np.sin(angles).astype(np.float32))


def contract(left, right, left_dim, right_dim):
    return lax.dot_general(
        left,
        right,
        (((left_dim,), (right_dim,)), ((), ())),
        preferred_element_type=jnp.float32,
    )


def head_scale(rows):
    return lax.rsqrt(jnp.mean(rows * rows, 0, keepdims=True) + eps_norm)


def rotated(rows, scale, gain, cosine, sine):
    half = HEAD_SIZE // 2
    shaped = rows * scale * gain
    first, second = shaped[:half], shaped[half:]
    return jnp.concatenate(
        [first * cosine - second * sine, second * cosine + first * sine], axis=0
    )


def unrotated_norm_back(grad, rows, scale, gain, cosine, sine):
    half = HEAD_SIZE // 2
    first, second = grad[:half], grad[half:]
    turned = jnp.concatenate(
        [first * cosine + second * sine, second * cosine - first * sine], axis=0
    )
    shaped = rows * scale
    pushed = turned * gain
    grad_in = scale * (pushed - shaped * jnp.mean(pushed * shaped, 0, keepdims=True))
    return (grad_in, turned * shaped)


def causal(block):
    keys = lax.broadcasted_iota(jnp.int32, (block, block), 0)
    places = lax.broadcasted_iota(jnp.int32, (block, block), 1)
    return keys <= places


def forward_kernel(
    group_ref, qp_ref, kp_ref, vp_ref, cos_ref, sin_ref, gq_ref, gk_ref,
    q_ref, k_ref, v_ref, out_ref, lse_ref, *, block,
):
    cosine, sine = cos_ref[...], sin_ref[...]
    qp, kp = qp_ref[...], kp_ref[...]
    query = (rotated(qp, head_scale(qp), gq_ref[...], cosine, sine) * 0.125).astype(jnp.bfloat16)
    key = rotated(kp, head_scale(kp), gk_ref[...], cosine, sine).astype(jnp.bfloat16)
    value = vp_ref[...].astype(jnp.bfloat16)
    q_ref[0] = query
    k_ref[0] = key
    v_ref[0] = value
    allowed = causal(block)
    for index in range(query.shape[1] // block):
        start, stop = index * block, (index + 1) * block
        part = query[:, start:stop]
        near = contract(key[:, start:stop], part, 0, 0)
        near = jnp.where(allowed, near, masked_value)
        top = jnp.max(near, 0, keepdims=True)
        if index:
            far = contract(key[:, :start], part, 0, 0)
            top = jnp.maximum(top, jnp.max(far, 0, keepdims=True))
        near = jnp.exp(near - top)
        total = jnp.sum(near, 0, keepdims=True)
        if index:
            far = jnp.exp(far - top)
            total = total + jnp.sum(far, 0, keepdims=True)
        share = 1.0 / total
        result = contract(value[:, start:stop], (near * share).astype(jnp.bfloat16), 1, 0)
        if index:
            result = result + contract(value[:, :start], (far * share).astype(jnp.bfloat16), 1, 0)
        out_ref[index] = result.astype(jnp.bfloat16)
        lse_ref[0, :, start:stop] = top + jnp.log(total)


def backward_kernel(
    group_ref, qp_ref, kp_ref, q_ref, k_ref, v_ref, do_ref, lse_ref, cos_ref, sin_ref,
    gq_ref, gk_ref,
    gqp_ref, gkp_ref, gv_ref, gain_q_ref, gain_k_ref,
    dq_ref, dk_ref, dv_ref, sum_q_ref, sum_k_ref, *, block,
):
    head = pl.program_id(0)
    heads = pl.num_programs(0)
    group = group_ref[head]
    opens = jnp.logical_or(head == 0, group_ref[jnp.maximum(head - 1, 0)] != group)
    closes = jnp.logical_or(
        head == heads - 1, group_ref[jnp.minimum(head + 1, heads - 1)] != group
    )

    @pl.when(head == 0)
    def _():
        sum_q_ref[...] = jnp.zeros_like(sum_q_ref)
        sum_k_ref[...] = jnp.zeros_like(sum_k_ref)

    @pl.when(opens)
    def _():
        dk_ref[...] = jnp.zeros_like(dk_ref)
        dv_ref[...] = jnp.zeros_like(dv_ref)

    query, key, value = q_ref[0], k_ref[0], v_ref[0]
    allowed = causal(block)
    for index in range(query.shape[1] // block):
        start, stop = index * block, (index + 1) * block
        part, grad_part = query[:, start:stop], do_ref[index]
        sums_log = lse_ref[0, :, start:stop]
        near = jnp.exp(contract(key[:, start:stop], part, 0, 0) - sums_log)
        near = jnp.where(allowed, near, 0.0)
        grad_near = contract(value[:, start:stop], grad_part, 0, 0)
        inner = jnp.sum(near * grad_near, 0, keepdims=True)
        if index:
            far = jnp.exp(contract(key[:, :start], part, 0, 0) - sums_log)
            grad_far = contract(value[:, :start], grad_part, 0, 0)
            inner = inner + jnp.sum(far * grad_far, 0, keepdims=True)
        step = (near * (grad_near - inner)).astype(jnp.bfloat16)
        total = contract(key[:, start:stop], step, 1, 0)
        dk_ref[:, start:stop] += contract(part, step, 1, 1)
        dv_ref[:, start:stop] += contract(grad_part, near.astype(jnp.bfloat16), 1, 1)
        if index:
            step = (far * (grad_far - inner)).astype(jnp.bfloat16)
            total = total + contract(key[:, :start], step, 1, 0)
            dk_ref[:, :start] += contract(part, step, 1, 1)
            dv_ref[:, :start] += contract(grad_part, far.astype(jnp.bfloat16), 1, 1)
        dq_ref[:, start:stop] = total * 0.125

    cosine, sine = cos_ref[...], sin_ref[...]
    qp = qp_ref[...]
    grad_qp, gain_terms = unrotated_norm_back(
        dq_ref[...].astype(jnp.bfloat16).astype(jnp.float32),
        qp, head_scale(qp), gq_ref[...], cosine, sine,
    )
    gqp_ref[...] = grad_qp.astype(jnp.bfloat16)
    sum_q_ref[...] += gain_terms

    @pl.when(closes)
    def _():
        kp = kp_ref[...]
        grad_kp, terms = unrotated_norm_back(
            dk_ref[...].astype(jnp.bfloat16).astype(jnp.float32),
            kp, head_scale(kp), gk_ref[...], cosine, sine,
        )
        gkp_ref[0] = grad_kp.astype(jnp.bfloat16)
        gv_ref[0] = dv_ref[...].astype(jnp.bfloat16)
        sum_k_ref[...] += terms

    @pl.when(head == heads - 1)
    def _():
        gain_q_ref[...] = jnp.sum(sum_q_ref[...], 1, keepdims=True)
        gain_k_ref[...] = jnp.sum(sum_k_ref[...], 1, keepdims=True)


def attention_specs(length, heads, block):
    half = HEAD_SIZE // 2
    tall = (HEAD_SIZE, length)
    whole = lambda shape: pl.BlockSpec(shape, lambda h, g: (0, 0))
    per_head = pl.BlockSpec((1,) + tall, lambda h, g: (h, 0, 0))
    per_group = pl.BlockSpec((1,) + tall, lambda h, g: (g[h], 0, 0))
    per_row = pl.BlockSpec((1, 1, length), lambda h, g: (h, 0, 0))
    query = pl.BlockSpec(tall, lambda h, g: (h, 0))
    key = pl.BlockSpec(tall, lambda h, g: (heads + g[h], 0))
    value = pl.BlockSpec(tall, lambda h, g: (heads + 2 + g[h], 0))
    table = whole((half, length))
    gain = whole((HEAD_SIZE, 1))
    per_owner = pl.BlockSpec((length // block, HEAD_SIZE, block), lambda h, g: (0, h, 0))
    return (query, key, value, per_head, per_group, per_row, table, gain, per_owner)


def attend(groups, mixed, cosine, sine, gain_q, gain_k, heads, block):
    length = mixed.shape[1]
    query, key, value, per_head, per_group, per_row, table, gain, per_owner = attention_specs(
        length, heads, block
    )
    per = lambda count: jax.ShapeDtypeStruct((count, HEAD_SIZE, length), jnp.bfloat16)
    scores = heads * length * length // 2
    return pl.pallas_call(
        functools.partial(forward_kernel, block=block),
        name="attention_forward",
        out_shape=(
            per(heads), per(2), per(2),
            jax.ShapeDtypeStruct((length // block, heads * HEAD_SIZE, block), jnp.bfloat16),
            jax.ShapeDtypeStruct((heads, 1, length), jnp.float32),
        ),
        grid_spec=pltpu.PrefetchScalarGridSpec(
            num_scalar_prefetch=1,
            grid=(heads,),
            in_specs=[query, key, value, table, table, gain, gain],
            out_specs=[per_head, per_group, per_group, per_owner, per_row],
        ),
        compiler_params=pltpu.CompilerParams(
            dimension_semantics=("arbitrary",), vmem_limit_bytes=VMEM_LIMIT
        ),
        cost_estimate=pl.CostEstimate(
            flops=scores * 4 * HEAD_SIZE, transcendentals=scores, bytes_accessed=8_000_000
        ),
    )(groups, mixed, mixed, mixed, cosine, sine, gain_q, gain_k)


def attend_back(
    groups, mixed, query_rows, key_rows, value_rows, grads, lse, cosine, sine, gain_q, gain_k, heads, block
):
    length = mixed.shape[1]
    query, key, value, per_head, per_group, per_row, table, gain, per_owner = attention_specs(
        length, heads, block
    )
    tall = (HEAD_SIZE, length)
    scores = heads * length * length // 2
    return pl.pallas_call(
        functools.partial(backward_kernel, block=block),
        name="attention_backward",
        out_shape=(
            jax.ShapeDtypeStruct((heads * HEAD_SIZE, length), jnp.bfloat16),
            jax.ShapeDtypeStruct((2,) + tall, jnp.bfloat16),
            jax.ShapeDtypeStruct((2,) + tall, jnp.bfloat16),
            jax.ShapeDtypeStruct((HEAD_SIZE, 1), jnp.float32),
            jax.ShapeDtypeStruct((HEAD_SIZE, 1), jnp.float32),
        ),
        grid_spec=pltpu.PrefetchScalarGridSpec(
            num_scalar_prefetch=1,
            grid=(heads,),
            in_specs=[
                query, key, per_head, per_group, per_group, per_owner, per_row, table, table, gain, gain,
            ],
            out_specs=[query, per_group, per_group, gain, gain],
            scratch_shapes=[pltpu.VMEM(tall, jnp.float32)] * 5,
        ),
        compiler_params=pltpu.CompilerParams(
            dimension_semantics=("arbitrary",), vmem_limit_bytes=VMEM_LIMIT
        ),
        cost_estimate=pl.CostEstimate(
            flops=scores * 10 * HEAD_SIZE, transcendentals=scores, bytes_accessed=10_000_000
        ),
    )(groups, mixed, mixed, query_rows, key_rows, value_rows, grads, lse, cosine, sine, gain_q, gain_k)


def row_order_kernel(mine_ref, in_ref, out_ref, *, offsets, back):
    for index, offset in enumerate(offsets):
        held = mine_ref[0] ^ offset
        if back:
            out_ref[held] = in_ref[index]
        else:
            out_ref[index] = in_ref[held]


def column_order_kernel(mine_ref, in_ref, out_ref, *, lines, parts, back):
    width = in_ref.shape[1] // (2 * lines)
    small = width // parts
    for plane in range(2):
        for line in range(lines):
            held = pl.multiple_of((mine_ref[0] ^ (line * 2 + plane)) * width, width)
            places = [(plane * parts + part) * lines + line for part in range(parts)]
            if back:
                out_ref[:, pl.ds(held, width)] = jnp.concatenate(
                    [in_ref[:, at * small : (at + 1) * small] for at in places], axis=1
                )
            else:
                block = in_ref[:, pl.ds(held, width)]
                for part, at in enumerate(places):
                    out_ref[:, at * small : (at + 1) * small] = block[
                        :, part * small : (part + 1) * small
                    ]


def order_call(kernel, array, mine):
    return pl.pallas_call(
        kernel,
        name="block_order",
        out_shape=jax.ShapeDtypeStruct(array.shape, array.dtype),
        in_specs=[
            pl.BlockSpec(memory_space=pltpu.SMEM),
            pl.BlockSpec(memory_space=pltpu.VMEM),
        ],
        out_specs=pl.BlockSpec(memory_space=pltpu.VMEM),
        compiler_params=pltpu.CompilerParams(vmem_limit_bytes=VMEM_LIMIT),
        cost_estimate=pl.CostEstimate(
            flops=0, transcendentals=0, bytes_accessed=4 * array.size
        ),
    )(mine.reshape(1).astype(jnp.int32), array)


def column_order(array, mine, lines, parts, back=False):
    rows, columns = array.shape
    width = columns // (2 * lines)
    if width % 128 == 0:
        kernel = functools.partial(column_order_kernel, lines=lines, parts=parts, back=back)
        return order_call(kernel, array, mine)
    small = width // parts
    if back:
        array = array.reshape(rows, 2, parts, lines, small).transpose(0, 3, 1, 2, 4)
        return jnp.where(mine == 0, array, array[:, :, ::-1]).reshape(rows, columns)
    array = array.reshape(rows, lines, 2, parts, small)
    array = jnp.where(mine == 0, array, array[:, :, ::-1])
    return array.transpose(0, 2, 3, 1, 4).reshape(rows, columns)


def head_columns(part, width):
    keys_at = QUERY_HEADS * HEAD_SIZE + part * HEAD_SIZE
    values_at = keys_at + VALUE_GROUPS * HEAD_SIZE
    pair = 2 * HEAD_SIZE
    return ((part * width, 0, width), (keys_at, width, pair), (values_at, width + pair, pair))


def split_kernel(in_ref, qkv_ref, out_ref, gain_ref, *, width):
    parts, lines, rows, _ = qkv_ref.shape
    for line in range(lines):
        for part in range(parts):
            for source, target, count in head_columns(part, width):
                qkv_ref[part, line, :, target : target + count] = in_ref[
                    line, :rows, source : source + count
                ]
        out_ref[line] = in_ref[line, rows : rows + out_ref.shape[1], :]
        gain_ref[line] = in_ref[line, rows + out_ref.shape[1] :, : gain_ref.shape[2]]


def split_columns(both, parts, rows, width, gain_width):
    lines, total, model = both.shape
    total = total - GAIN_ROWS
    span = width + 4 * HEAD_SIZE
    return pl.pallas_call(
        functools.partial(split_kernel, width=width),
        name="split_columns",
        out_shape=(
            jax.ShapeDtypeStruct((parts, lines, rows, span), both.dtype),
            jax.ShapeDtypeStruct((lines, total - rows, model), both.dtype),
            jax.ShapeDtypeStruct((lines, GAIN_ROWS, gain_width), both.dtype),
        ),
        compiler_params=pltpu.CompilerParams(vmem_limit_bytes=VMEM_LIMIT),
        cost_estimate=pl.CostEstimate(
            flops=0, transcendentals=0, bytes_accessed=4 * both.size
        ),
    )(both)


def join_kernel(in_ref, qkv_ref, *, width):
    parts, lines, _, _ = in_ref.shape
    for line in range(lines):
        for part in range(parts):
            qkv_ref[line, :, part * width : (part + 1) * width] = in_ref[part, line, :, :width]
        for kind in range(2):
            for group in range(VALUE_GROUPS):
                terms = []
                for part in range(max(group - 1, 0), min(group + 1, parts)):
                    at = width + (2 * kind + group - part) * HEAD_SIZE
                    terms.append(in_ref[part, line, :, at : at + HEAD_SIZE].astype(jnp.float32))
                at = (QUERY_HEADS + kind * VALUE_GROUPS + group) * HEAD_SIZE
                qkv_ref[line, :, at : at + HEAD_SIZE] = sum(terms).astype(qkv_ref.dtype)


def join_columns(qkv_parts, width):
    _, lines, rows, _ = qkv_parts.shape
    shape = (lines, rows, (QUERY_HEADS + 2 * VALUE_GROUPS) * HEAD_SIZE)
    return pl.pallas_call(
        functools.partial(join_kernel, width=width),
        name="join_columns",
        out_shape=jax.ShapeDtypeStruct(shape, jnp.bfloat16),
        compiler_params=pltpu.CompilerParams(vmem_limit_bytes=VMEM_LIMIT),
        cost_estimate=pl.CostEstimate(
            flops=0, transcendentals=0, bytes_accessed=4 * int(np.prod(shape))
        ),
    )(qkv_parts)


def adamw(weight, grad, first, second, rate, shrink, item_count):
    first_new = beta_first * first + (1.0 - beta_first) * grad
    second_new = beta_second * second + (1.0 - beta_second) * grad * grad
    fix_first = 1.0 - jnp.power(beta_first, item_count)
    fix_second = 1.0 - jnp.power(beta_second, item_count)
    stepped = first_new / fix_first / (jnp.sqrt(second_new / fix_second) + adam_eps)
    return (
        weight - rate * (stepped + shrink * weight),
        jnp.stack([first_new, jnp.sqrt(second_new)]),
    )


def local(
    sizes,
    tokens,
    cotangent,
    corpus_id,
    corpus_weight,
    step_count,
    qkv_weight,
    out_weight,
    gains,
    gate_weight,
    up_weight,
    down_weight,
    first_qkv,
    first_out,
    first_gains,
    first_gate,
    first_up,
    first_down,
    second_qkv,
    second_out,
    second_gains,
    second_gate,
    second_up,
    second_down,
):
    low = jnp.bfloat16
    high = jnp.float32
    devices = int(np.prod(sizes))
    seqs = sizes[0] * sizes[1]
    parts = sizes[2] * sizes[3]
    places = np.arange(devices).reshape(sizes)
    where = np.stack(np.unravel_index(np.arange(devices), sizes), -1)

    def permute(array, target):
        pairs = [(int(i), int(places[tuple(target(*where[i]))])) for i in range(devices)]
        return lax.ppermute(array, ALL, [pair for pair in pairs if pair[0] != pair[1]])

    def swap(array):
        moved = permute(array, lambda sh, sl, kh, kl: (sh, kl, kh, sl))
        return jnp.where(lax.axis_index("sl") == lax.axis_index("kl"), array, moved)

    def in_ffn_group(array, r):
        return permute(array, lambda sh, sl, kh, kl: (sh, sl ^ (r & 1), kh ^ (r >> 1), kl))

    def in_sequence(array, r):
        return permute(array, lambda sh, sl, kh, kl: (sh, sl, kh ^ (r >> 1), kl ^ (r & 1)))

    def along_y(array):
        return permute(array, lambda sh, sl, kh, kl: (sh, sl ^ 1, kh, kl))

    z_size = sizes[0]

    def halve(blocks, index, axis, move):
        kept = lax.dynamic_index_in_dim(blocks, index, axis, keepdims=False)
        sent = lax.dynamic_index_in_dim(blocks, index ^ 1, axis, keepdims=False)
        return kept.astype(high) + move(sent.astype(low)).astype(high)

    item_count, model = tokens.shape
    heads = QUERY_HEADS // parts
    width = heads * HEAD_SIZE
    pair = 2 * HEAD_SIZE
    keys_at = QUERY_HEADS * HEAD_SIZE
    values_at = keys_at + VALUE_GROUPS * HEAD_SIZE
    kv = lax.axis_index(KV)
    length = item_count * parts
    cosine, sine = angle_tables(length)
    groups = ((jnp.arange(heads, dtype=jnp.int32) + kv) // 4).astype(jnp.int32)

    def stage(ready, waiting):
        return lax.optimization_barrier((ready, waiting))

    row_offsets = [
        (z * 2 + rs) * parts + r1 * 2 + r0
        for r0 in range(2) for rs in range(2) for r1 in range(2) for z in range(z_size)
    ]

    def columns_moved(array, back=False):
        return column_order(array, lax.axis_index("sl"), z_size, parts, back=back)

    def rows_moved(array, back=False):
        blocks = array.reshape(devices, -1, item_count)
        kernel = functools.partial(row_order_kernel, offsets=tuple(row_offsets), back=back)
        mine = lax.axis_index("sl") * parts + kv
        return order_call(kernel, blocks, mine).reshape(-1, item_count)

    span = width + 2 * pair
    own_rows, total_columns = qkv_weight.shape
    both = jnp.concatenate(
        [
            jnp.pad(qkv_weight.astype(low), ((0, 0), (0, model - total_columns))),
            out_weight.astype(low),
            jnp.pad(gains.astype(low)[None], ((0, GAIN_ROWS - 1), (0, model - gains.shape[0]))),
        ]
    )
    both_line = lax.all_to_all(
        jnp.broadcast_to(both[None], (z_size,) + both.shape), "sh", split_axis=0, concat_axis=0, tiled=True
    )
    tokens_near = columns_moved(tokens)
    tokens_far = in_sequence(tokens_near, 2)
    gate_block = swap(gate_weight.astype(low))
    factor = jnp.sum(
        jnp.where(jnp.arange(corpus_weight.shape[0]) == corpus_id[0], corpus_weight, 0.0)
    )
    weighted = cotangent.astype(high) * factor
    weighted_low = weighted.astype(low)
    weighted_one = in_ffn_group(weighted_low, 1)
    (both_line, tokens_far, gate_block, weighted_one), (up_low, tokens_near, weighted_low) = stage(
        (both_line, tokens_far, gate_block, weighted_one),
        (up_weight.astype(low), tokens_near, weighted_low),
    )
    gate_full = lax.all_gather(gate_block, OWNERS, axis=0, tiled=True)

    gain_width = -(-gains.shape[0] // 128) * 128
    qkv_parts, out_line, gain_line = split_columns(both_line, parts, own_rows, width, gain_width)
    gain_pairs = jnp.stack([gain_line, in_sequence(gain_line, 1)])
    gain_pairs = jnp.stack([gain_pairs, in_sequence(gain_pairs, 2)])
    qkv_rows = lax.all_to_all(
        qkv_parts, KV, split_axis=0, concat_axis=0, tiled=True
    )
    tokens_pair = (in_sequence(tokens_near, 1), in_sequence(tokens_far, 1))
    (qkv_rows, tokens_pair, gain_pairs), (up_low, out_line, down_low, weighted_low) = stage(
        (qkv_rows, tokens_pair, gain_pairs), (up_low, out_line, down_weight.astype(low), weighted_low)
    )

    qkv_far = along_y(qkv_rows)
    up_block = swap(up_low)
    out_far = in_sequence(out_line, 2)
    weighted_far = in_ffn_group(weighted_low, 2)
    held = jnp.arange(2 * parts)
    mine = lax.axis_index("sl") * parts + kv
    selection = held[:, None] == (held[None, :] ^ mine)
    gain_blocks = jnp.stack([gain_pairs, along_y(gain_pairs)])[..., 0, : gains.shape[0]]
    gain_values = contract(selection.astype(low), gain_blocks.reshape(2 * parts, -1), 1, 0)
    gain_values = gain_values.reshape(2, parts, z_size, -1).transpose(2, 0, 1, 3).reshape(-1)
    gain_one = gain_values[:model]
    gain_two = gain_values[model : 2 * model]
    gain_q = gain_values[2 * model : 2 * model + HEAD_SIZE].reshape(HEAD_SIZE, 1)
    gain_k = gain_values[2 * model + HEAD_SIZE :].reshape(HEAD_SIZE, 1)
    gain_moved = columns_moved(jnp.broadcast_to(gain_one[None], (8, model)))[:1]
    all_rows = jnp.zeros((parts, item_count, model), low)
    for r, piece in enumerate((tokens_near, tokens_pair[0], tokens_far, tokens_pair[1])):
        all_rows = lax.dynamic_update_slice_in_dim(all_rows, piece[None], kv ^ r, 0)
    all_rows = all_rows.reshape(length, model).astype(high)
    normed = (all_rows * rms_scale(all_rows) * gain_moved).astype(low)
    (qkv_far, up_block, out_far, normed), (out_line, down_low) = stage(
        (qkv_far, up_block, out_far, normed), (out_line, down_low)
    )
    up_full = lax.all_gather(up_block, OWNERS, axis=0, tiled=True)
    qkv_full = jnp.concatenate([qkv_rows, qkv_far]).reshape(model, span)

    out_near = jnp.stack([out_line, out_far])
    out_other = along_y(out_near)
    mixed = contract(qkv_full, normed, 0, 1)
    query_rows, key_rows, value_rows, outgoing, lse = attend(
        groups, mixed, cosine, sine, gain_q, gain_k, heads, item_count
    )
    (outgoing, weighted_far), (out_near, down_low) = stage((outgoing, weighted_far), (out_near, down_low))
    weighted_rows = jnp.concatenate(
        [weighted_low, weighted_one, weighted_far, in_ffn_group(weighted_far, 1)], axis=0
    )

    down_block = swap(down_low)
    attended = rows_moved(
        lax.all_to_all(outgoing, KV, split_axis=0, concat_axis=0, tiled=True)
    )
    out_full = (out_near, out_other, in_sequence(out_near, 1), in_sequence(out_other, 1))
    out_full = [piece.reshape(-1, model) for piece in out_full]
    (attended, out_full), down_block = stage((attended, out_full), down_block)
    attended = attended.reshape(4, -1, item_count)
    down_full = lax.all_gather(down_block, OWNERS, axis=0, tiled=True)
    inputs = tokens.astype(high)
    hidden = inputs + sum(contract(attended[i], out_full[i], 0, 0) for i in range(4))

    scale_two = rms_scale(hidden)
    normed_two = (hidden * scale_two * gain_two).astype(low)
    ffn_rows = jnp.concatenate(
        [normed_two] + [in_ffn_group(normed_two, r) for r in (1, 2, 3)], axis=0
    )
    gate = contract(ffn_rows, gate_full, 1, 0)
    up_part = contract(ffn_rows, up_full, 1, 0)
    sigma = jax.nn.sigmoid(gate)
    swish = gate * sigma
    acted = (swish * up_part).astype(low)

    def from_group(sent):
        return [
            in_ffn_group(sent[(r - 1) * item_count : r * item_count], r) for r in (1, 2, 3)
        ]

    def share(grad):
        return lax.psum_scatter(grad, OWNERS, scatter_dimension=0, tiled=True)

    grad_down_low = contract(weighted_rows, acted, 0, 0).astype(low)
    down_full, grad_down_low = stage(down_full, grad_down_low)
    grad_down_share = share(grad_down_low)
    grad_acted = contract(weighted_rows, down_full, 1, 0)
    grad_gate = (grad_acted * up_part * sigma * (1.0 + gate * (1.0 - sigma))).astype(low)
    grad_up = (grad_acted * swish).astype(low)
    rows_partial = (
        contract(grad_gate, gate_full, 1, 1) + contract(grad_up, up_full, 1, 1)
    ).astype(low)
    own_partial = rows_partial[:item_count]
    (sent_rows, own_partial), (grad_gate, grad_up) = stage(
        (rows_partial[item_count:], own_partial), (grad_gate, grad_up)
    )
    received = from_group(sent_rows)
    grad_gate_share = share(contract(ffn_rows, grad_gate, 0, 0).astype(low))
    grad_up_low = contract(ffn_rows, grad_up, 0, 0).astype(low)
    ffn_partial = contract(acted, down_full, 1, 1).astype(low)
    (received, grad_down_share), (grad_up_low, ffn_partial) = stage(
        (received, grad_down_share), (grad_up_low, ffn_partial)
    )
    grad_up_share = share(grad_up_low)
    grad_normed_two = own_partial.astype(high) + sum(piece.astype(high) for piece in received)

    pushed_two, gain_two_terms = norm_back(grad_normed_two, hidden, scale_two, gain_two)
    grad_hidden = weighted + pushed_two
    hidden_low = grad_hidden.astype(low)

    attended_gradient = jnp.concatenate(
        [contract(piece, hidden_low, 1, 1).astype(low) for piece in out_full]
    )
    attended_gradient = rows_moved(attended_gradient, back=True)
    incoming = lax.all_to_all(
        attended_gradient.reshape(parts, width, item_count), KV, split_axis=0, concat_axis=0, tiled=True
    )
    ffn_blocks = ffn_partial.reshape(2, 2, item_count, model)
    ffn_moved = [in_ffn_group(ffn_blocks[r, 1], 1) for r in range(2)]
    attended = attended.reshape(2, 2, 2, -1, item_count)
    sent_out = [
        contract(attended[1, :, r].reshape(-1, item_count), hidden_low, 1, 0).astype(low) for r in range(2)
    ]
    kept_out = [
        contract(attended[0, :, r].reshape(-1, item_count), hidden_low, 1, 0) for r in range(2)
    ]
    out_line = [kept_out[r] + in_sequence(sent_out[r], 1).astype(high) for r in range(2)]
    out_far = out_line[1].astype(low)
    incoming, out_far = lax.optimization_barrier((incoming, out_far))

    out_moved = in_sequence(out_far, 2)
    grad_queries, grad_keys, grad_values, gain_q_sum, gain_k_sum = attend_back(
        groups, mixed, query_rows, key_rows, value_rows, incoming, lse,
        cosine, sine, gain_q, gain_k, heads, item_count,
    )
    grad_mixed = jnp.concatenate(
        [grad_queries, grad_keys.reshape(pair, length), grad_values.reshape(pair, length)], axis=0
    )
    half_model = model // 2
    grad_mixed, (ffn_moved, grad_gate_share) = stage(grad_mixed, (ffn_moved, grad_gate_share))
    mixer_sent = contract(normed[:, half_model:], grad_mixed, 0, 1).astype(low)
    (mixer_sent, grad_mixed), (out_line, ffn_blocks) = stage(
        (mixer_sent, grad_mixed), (out_line[0], ffn_blocks)
    )

    mixer_moved = along_y(mixer_sent)
    mixer_line = contract(normed[:, :half_model], grad_mixed, 0, 1)
    grad_normed = contract(grad_mixed, qkv_full, 0, 1).astype(low)
    grad_normed = halve(
        grad_normed.reshape(2, 2, item_count, model), lax.axis_index("kl"), 1, lambda v: in_sequence(v, 1)
    )
    ffn_line = [ffn_blocks[r, 0].astype(high) + ffn_moved[r].astype(high) for r in range(2)]
    ffn_moved = in_ffn_group(ffn_line[1].astype(low), 2)
    mixer_line = lax.optimization_barrier(mixer_line)
    mixer_parts = (mixer_line + mixer_moved.astype(high)).astype(low)
    mixer_parts, out_line = stage(mixer_parts, out_line)

    mixer_parts = lax.all_to_all(
        mixer_parts.reshape(parts, z_size, -1, span), KV, split_axis=0, concat_axis=0, tiled=True
    )
    out_line = (out_line + out_moved.astype(high)).reshape(2, z_size, -1, model)
    out_moved = along_y(out_line[1].astype(low))
    qkv_line = join_columns(mixer_parts, width)
    qkv_line, (grad_normed, ffn_line, out_line, shares) = stage(
        qkv_line, (grad_normed, ffn_line, out_line[0], (grad_down_share, grad_gate_share, grad_up_share))
    )

    qkv_line = lax.all_to_all(qkv_line, "sh", split_axis=0, concat_axis=0, tiled=True)
    grad_normed = halve(grad_normed, lax.axis_index("kh"), 0, lambda v: in_sequence(v, 2))
    out_line = (out_line + out_moved.astype(high)).astype(low)
    qkv_line, out_line = stage(qkv_line, out_line)
    out_line = lax.all_to_all(out_line, "sh", split_axis=0, concat_axis=0, tiled=True)
    block_out = (hidden + (ffn_line[0] + ffn_moved.astype(high))).astype(low)
    qkv_grad = jnp.sum(qkv_line.astype(high), 0)
    out_grad = jnp.sum(out_line.astype(high), 0)
    grad_down, grad_gate_w, grad_up_w = (swap(piece).astype(high) for piece in shares)
    moved_inputs = tokens_near.astype(high)
    pushed_one, gain_one_terms = norm_back(
        grad_normed, moved_inputs, rms_scale(moved_inputs), gain_moved
    )
    grad_input = grad_hidden + columns_moved(pushed_one, back=True)
    gain_one_sum = columns_moved(
        jnp.broadcast_to(jnp.sum(gain_one_terms, 0)[None], (8, model)), back=True
    )[0]
    grad_gains = jnp.concatenate(
        [
            gain_one_sum,
            jnp.sum(gain_two_terms, 0),
            gain_q_sum.reshape(-1),
            gain_k_sum.reshape(-1),
        ]
    )
    grad_gains = grad_gains.reshape(z_size, 2, parts, -1).transpose(1, 2, 0, 3)
    grad_gains = lax.dot_general(
        selection.astype(high), grad_gains.reshape(2 * parts, -1), (((1,), (0,)), ((), ())),
        precision=lax.Precision.HIGHEST, preferred_element_type=high,
    ).reshape(2, 2, 2, -1)
    grad_gains = grad_gains[0] + along_y(grad_gains[1])
    grad_gains = grad_gains[:, 0] + in_sequence(grad_gains[:, 1], 1)
    grad_gains = grad_gains[0] + in_sequence(grad_gains[1], 2)
    grad_gains = grad_gains.reshape(z_size, -1)
    line = lax.axis_index("sh")
    gains_grad = lax.dynamic_index_in_dim(grad_gains, line, 0, keepdims=False)
    for r in range(1, z_size):
        sent = lax.dynamic_index_in_dim(grad_gains, line ^ r, 0, keepdims=False)
        gains_grad = gains_grad + permute(sent, lambda sh, sl, kh, kl: (sh ^ r, sl, kh, kl))

    steps_done = step_count[0].astype(high)
    new_qkv, moments_qkv = adamw(qkv_weight, qkv_grad, first_qkv, second_qkv, 0.02, 0.1, steps_done)
    new_out, moments_out = adamw(out_weight, out_grad, first_out, second_out, 0.2, 0.1, steps_done)
    new_gains, moments_gains = adamw(
        gains, gains_grad, first_gains, second_gains, 0.6, 0.0, steps_done
    )
    new_gate, moments_gate = adamw(
        gate_weight, grad_gate_w, first_gate, second_gate, 0.02, 0.1, steps_done
    )
    new_up, moments_up = adamw(up_weight, grad_up_w, first_up, second_up, 0.02, 0.1, steps_done)
    new_down, moments_down = adamw(
        down_weight, grad_down, first_down, second_down, 0.013, 0.1, steps_done
    )
    return (
        block_out,
        grad_input,
        new_qkv,
        moments_qkv,
        new_out,
        moments_out,
        new_gains,
        moments_gains,
        new_gate,
        moments_gate,
        new_up,
        moments_up,
        new_down,
        moments_down,
    )


def solution(mesh):
    seqs, parts = mesh.shape["seq"], mesh.shape["kv"]
    sizes = (seqs // 2, 2, parts // 2, 2)
    fine = Mesh(mesh.devices.reshape(sizes), ALL)
    rows = P(ALL, None)
    block = P(SEQ, KV)
    return jax.shard_map(
        functools.partial(local, sizes),
        mesh=fine,
        in_specs=(
            rows, rows, P(SEQ), P(), P(),
            rows, rows, P(ALL), block, block, block,
            rows, rows, P(ALL), block, block, block,
            rows, rows, P(ALL), block, block, block,
        ),
        out_specs=(
            rows, rows,
            rows, P(None, ALL, None),
            rows, P(None, ALL, None),
            P(ALL), P(None, ALL),
            block, P(None, SEQ, KV),
            block, P(None, SEQ, KV),
            block, P(None, SEQ, KV),
        ),
        check_vma=False,
    )
```

```python
import functools

import jax
import jax.numpy as jnp
import numpy as np
from jax import lax
from jax.experimental import pallas as pl
from jax.experimental.pallas import tpu as pltpu
from jax.sharding import Mesh, PartitionSpec as P

QUERY_HEADS = 20
VALUE_GROUPS = 5
HEAD_SIZE = 64

eps_norm = 1e-06
masked_value = -1e30
beta_first = 0.9
beta_second = 0.95
adam_eps = 1e-08

ALL = ("sh", "sl", "kh", "kl")
SEQ = ("sh", "sl")
KV = ("kh", "kl")
OWNERS = ("sh", "kl")
VMEM_LIMIT = 40 * 1024 * 1024
GAIN_ROWS = 8


def rms_scale(value_rows):
    return lax.rsqrt(jnp.mean(value_rows * value_rows, -1, keepdims=True) + eps_norm)


def norm_back(grad_out, value_rows, scale, gain):
    shaped = value_rows * scale
    pushed = grad_out * gain
    grad_in = scale * (pushed - shaped * jnp.mean(pushed * shaped, -1, keepdims=True))
    return (grad_in, grad_out * shaped)


def angle_tables(item_count):
    places = np.arange(item_count).astype(np.float32)
    steps = np.arange(HEAD_SIZE // 2).astype(np.float32) * np.float32(2.0) / np.float32(HEAD_SIZE)
    freqs = np.float32(10000.0) ** (-steps)
    angles = freqs[:, None].astype(np.float32) * places[None, :]
    return (np.cos(angles).astype(np.float32), np.sin(angles).astype(np.float32))


def contract(left, right, left_dim, right_dim):
    return lax.dot_general(
        left,
        right,
        (((left_dim,), (right_dim,)), ((), ())),
        preferred_element_type=jnp.float32,
    )


def head_scale(rows):
    return lax.rsqrt(jnp.mean(rows * rows, 0, keepdims=True) + eps_norm)


def rotated(rows, scale, gain, cosine, sine):
    half = HEAD_SIZE // 2
    shaped = rows * scale * gain
    first, second = shaped[:half], shaped[half:]
    return jnp.concatenate(
        [first * cosine - second * sine, second * cosine + first * sine], axis=0
    )


def unrotated_norm_back(grad, rows, scale, gain, cosine, sine):
    half = HEAD_SIZE // 2
    first, second = grad[:half], grad[half:]
    turned = jnp.concatenate(
        [first * cosine + second * sine, second * cosine - first * sine], axis=0
    )
    shaped = rows * scale
    pushed = turned * gain
    grad_in = scale * (pushed - shaped * jnp.mean(pushed * shaped, 0, keepdims=True))
    return (grad_in, turned * shaped)


def causal(block):
    keys = lax.broadcasted_iota(jnp.int32, (block, block), 0)
    places = lax.broadcasted_iota(jnp.int32, (block, block), 1)
    return keys <= places


def forward_kernel(
    group_ref, qp_ref, kp_ref, vp_ref, cos_ref, sin_ref, gq_ref, gk_ref,
    q_ref, k_ref, v_ref, out_ref, lse_ref, *, block,
):
    cosine, sine = cos_ref[...], sin_ref[...]
    qp, kp = qp_ref[...], kp_ref[...]
    query = (rotated(qp, head_scale(qp), gq_ref[...], cosine, sine) * 0.125).astype(jnp.bfloat16)
    key = rotated(kp, head_scale(kp), gk_ref[...], cosine, sine).astype(jnp.bfloat16)
    value = vp_ref[...].astype(jnp.bfloat16)
    q_ref[0] = query
    k_ref[0] = key
    v_ref[0] = value
    allowed = causal(block)
    for index in range(query.shape[1] // block):
        start, stop = index * block, (index + 1) * block
        part = query[:, start:stop]
        near = contract(key[:, start:stop], part, 0, 0)
        near = jnp.where(allowed, near, masked_value)
        top = jnp.max(near, 0, keepdims=True)
        if index:
            far = contract(key[:, :start], part, 0, 0)
            top = jnp.maximum(top, jnp.max(far, 0, keepdims=True))
        near = jnp.exp(near - top)
        total = jnp.sum(near, 0, keepdims=True)
        if index:
            far = jnp.exp(far - top)
            total = total + jnp.sum(far, 0, keepdims=True)
        share = 1.0 / total
        result = contract(value[:, start:stop], (near * share).astype(jnp.bfloat16), 1, 0)
        if index:
            result = result + contract(value[:, :start], (far * share).astype(jnp.bfloat16), 1, 0)
        out_ref[index] = result.astype(jnp.bfloat16)
        lse_ref[0, :, start:stop] = top + jnp.log(total)


def backward_kernel(
    group_ref, qp_ref, kp_ref, q_ref, k_ref, v_ref, do_ref, lse_ref, cos_ref, sin_ref,
    gq_ref, gk_ref,
    gqp_ref, gkp_ref, gv_ref, gain_q_ref, gain_k_ref,
    dq_ref, dk_ref, dv_ref, sum_q_ref, sum_k_ref, *, block,
):
    head = pl.program_id(0)
    heads = pl.num_programs(0)
    group = group_ref[head]
    opens = jnp.logical_or(head == 0, group_ref[jnp.maximum(head - 1, 0)] != group)
    closes = jnp.logical_or(
        head == heads - 1, group_ref[jnp.minimum(head + 1, heads - 1)] != group
    )

    @pl.when(head == 0)
    def _():
        sum_q_ref[...] = jnp.zeros_like(sum_q_ref)
        sum_k_ref[...] = jnp.zeros_like(sum_k_ref)

    @pl.when(opens)
    def _():
        dk_ref[...] = jnp.zeros_like(dk_ref)
        dv_ref[...] = jnp.zeros_like(dv_ref)

    query, key, value = q_ref[0], k_ref[0], v_ref[0]
    allowed = causal(block)
    for index in range(query.shape[1] // block):
        start, stop = index * block, (index + 1) * block
        part, grad_part = query[:, start:stop], do_ref[index]
        sums_log = lse_ref[0, :, start:stop]
        near = jnp.exp(contract(key[:, start:stop], part, 0, 0) - sums_log)
        near = jnp.where(allowed, near, 0.0)
        grad_near = contract(value[:, start:stop], grad_part, 0, 0)
        inner = jnp.sum(near * grad_near, 0, keepdims=True)
        if index:
            far = jnp.exp(contract(key[:, :start], part, 0, 0) - sums_log)
            grad_far = contract(value[:, :start], grad_part, 0, 0)
            inner = inner + jnp.sum(far * grad_far, 0, keepdims=True)
        step = (near * (grad_near - inner)).astype(jnp.bfloat16)
        total = contract(key[:, start:stop], step, 1, 0)
        dk_ref[:, start:stop] += contract(part, step, 1, 1)
        dv_ref[:, start:stop] += contract(grad_part, near.astype(jnp.bfloat16), 1, 1)
        if index:
            step = (far * (grad_far - inner)).astype(jnp.bfloat16)
            total = total + contract(key[:, :start], step, 1, 0)
            dk_ref[:, :start] += contract(part, step, 1, 1)
            dv_ref[:, :start] += contract(grad_part, far.astype(jnp.bfloat16), 1, 1)
        dq_ref[:, start:stop] = total * 0.125

    cosine, sine = cos_ref[...], sin_ref[...]
    qp = qp_ref[...]
    grad_qp, gain_terms = unrotated_norm_back(
        dq_ref[...].astype(jnp.bfloat16).astype(jnp.float32),
        qp, head_scale(qp), gq_ref[...], cosine, sine,
    )
    gqp_ref[...] = grad_qp.astype(jnp.bfloat16)
    sum_q_ref[...] += gain_terms

    @pl.when(closes)
    def _():
        kp = kp_ref[...]
        grad_kp, terms = unrotated_norm_back(
            dk_ref[...].astype(jnp.bfloat16).astype(jnp.float32),
            kp, head_scale(kp), gk_ref[...], cosine, sine,
        )
        gkp_ref[0] = grad_kp.astype(jnp.bfloat16)
        gv_ref[0] = dv_ref[...].astype(jnp.bfloat16)
        sum_k_ref[...] += terms

    @pl.when(head == heads - 1)
    def _():
        gain_q_ref[...] = jnp.sum(sum_q_ref[...], 1, keepdims=True)
        gain_k_ref[...] = jnp.sum(sum_k_ref[...], 1, keepdims=True)


def attention_specs(length, heads, block):
    half = HEAD_SIZE // 2
    tall = (HEAD_SIZE, length)
    whole = lambda shape: pl.BlockSpec(shape, lambda h, g: (0, 0))
    per_head = pl.BlockSpec((1,) + tall, lambda h, g: (h, 0, 0))
    per_group = pl.BlockSpec((1,) + tall, lambda h, g: (g[h], 0, 0))
    per_row = pl.BlockSpec((1, 1, length), lambda h, g: (h, 0, 0))
    query = pl.BlockSpec(tall, lambda h, g: (h, 0))
    key = pl.BlockSpec(tall, lambda h, g: (heads + g[h], 0))
    value = pl.BlockSpec(tall, lambda h, g: (heads + 2 + g[h], 0))
    table = whole((half, length))
    gain = whole((HEAD_SIZE, 1))
    per_owner = pl.BlockSpec((length // block, HEAD_SIZE, block), lambda h, g: (0, h, 0))
    return (query, key, value, per_head, per_group, per_row, table, gain, per_owner)


def attend(groups, mixed, cosine, sine, gain_q, gain_k, heads, block):
    length = mixed.shape[1]
    query, key, value, per_head, per_group, per_row, table, gain, per_owner = attention_specs(
        length, heads, block
    )
    per = lambda count: jax.ShapeDtypeStruct((count, HEAD_SIZE, length), jnp.bfloat16)
    scores = heads * length * length // 2
    return pl.pallas_call(
        functools.partial(forward_kernel, block=block),
        name="attention_forward",
        out_shape=(
            per(heads), per(2), per(2),
            jax.ShapeDtypeStruct((length // block, heads * HEAD_SIZE, block), jnp.bfloat16),
            jax.ShapeDtypeStruct((heads, 1, length), jnp.float32),
        ),
        grid_spec=pltpu.PrefetchScalarGridSpec(
            num_scalar_prefetch=1,
            grid=(heads,),
            in_specs=[query, key, value, table, table, gain, gain],
            out_specs=[per_head, per_group, per_group, per_owner, per_row],
        ),
        compiler_params=pltpu.CompilerParams(
            dimension_semantics=("arbitrary",), vmem_limit_bytes=VMEM_LIMIT
        ),
        cost_estimate=pl.CostEstimate(
            flops=scores * 4 * HEAD_SIZE, transcendentals=scores, bytes_accessed=8_000_000
        ),
    )(groups, mixed, mixed, mixed, cosine, sine, gain_q, gain_k)


def attend_back(
    groups, mixed, query_rows, key_rows, value_rows, grads, lse, cosine, sine, gain_q, gain_k, heads, block
):
    length = mixed.shape[1]
    query, key, value, per_head, per_group, per_row, table, gain, per_owner = attention_specs(
        length, heads, block
    )
    tall = (HEAD_SIZE, length)
    scores = heads * length * length // 2
    return pl.pallas_call(
        functools.partial(backward_kernel, block=block),
        name="attention_backward",
        out_shape=(
            jax.ShapeDtypeStruct((heads * HEAD_SIZE, length), jnp.bfloat16),
            jax.ShapeDtypeStruct((2,) + tall, jnp.bfloat16),
            jax.ShapeDtypeStruct((2,) + tall, jnp.bfloat16),
            jax.ShapeDtypeStruct((HEAD_SIZE, 1), jnp.float32),
            jax.ShapeDtypeStruct((HEAD_SIZE, 1), jnp.float32),
        ),
        grid_spec=pltpu.PrefetchScalarGridSpec(
            num_scalar_prefetch=1,
            grid=(heads,),
            in_specs=[
                query, key, per_head, per_group, per_group, per_owner, per_row, table, table, gain, gain,
            ],
            out_specs=[query, per_group, per_group, gain, gain],
            scratch_shapes=[pltpu.VMEM(tall, jnp.float32)] * 5,
        ),
        compiler_params=pltpu.CompilerParams(
            dimension_semantics=("arbitrary",), vmem_limit_bytes=VMEM_LIMIT
        ),
        cost_estimate=pl.CostEstimate(
            flops=scores * 10 * HEAD_SIZE, transcendentals=scores, bytes_accessed=10_000_000
        ),
    )(groups, mixed, mixed, query_rows, key_rows, value_rows, grads, lse, cosine, sine, gain_q, gain_k)


def row_order_kernel(mine_ref, in_ref, out_ref, *, offsets, back):
    for index, offset in enumerate(offsets):
        held = mine_ref[0] ^ offset
        if back:
            out_ref[held] = in_ref[index]
        else:
            out_ref[index] = in_ref[held]


def column_order_kernel(mine_ref, in_ref, out_ref, *, lines, parts, back):
    width = in_ref.shape[1] // (2 * lines)
    small = width // parts
    for plane in range(2):
        for line in range(lines):
            held = pl.multiple_of((mine_ref[0] ^ (line * 2 + plane)) * width, width)
            places = [(plane * parts + part) * lines + line for part in range(parts)]
            if back:
                out_ref[:, pl.ds(held, width)] = jnp.concatenate(
                    [in_ref[:, at * small : (at + 1) * small] for at in places], axis=1
                )
            else:
                block = in_ref[:, pl.ds(held, width)]
                for part, at in enumerate(places):
                    out_ref[:, at * small : (at + 1) * small] = block[
                        :, part * small : (part + 1) * small
                    ]


def order_call(kernel, array, mine):
    return pl.pallas_call(
        kernel,
        name="block_order",
        out_shape=jax.ShapeDtypeStruct(array.shape, array.dtype),
        in_specs=[
            pl.BlockSpec(memory_space=pltpu.SMEM),
            pl.BlockSpec(memory_space=pltpu.VMEM),
        ],
        out_specs=pl.BlockSpec(memory_space=pltpu.VMEM),
        compiler_params=pltpu.CompilerParams(vmem_limit_bytes=VMEM_LIMIT),
        cost_estimate=pl.CostEstimate(
            flops=0, transcendentals=0, bytes_accessed=4 * array.size
        ),
    )(mine.reshape(1).astype(jnp.int32), array)


def column_order(array, mine, lines, parts, back=False):
    rows, columns = array.shape
    width = columns // (2 * lines)
    if width % 128 == 0:
        kernel = functools.partial(column_order_kernel, lines=lines, parts=parts, back=back)
        return order_call(kernel, array, mine)
    small = width // parts
    if back:
        array = array.reshape(rows, 2, parts, lines, small).transpose(0, 3, 1, 2, 4)
        return jnp.where(mine == 0, array, array[:, :, ::-1]).reshape(rows, columns)
    array = array.reshape(rows, lines, 2, parts, small)
    array = jnp.where(mine == 0, array, array[:, :, ::-1])
    return array.transpose(0, 2, 3, 1, 4).reshape(rows, columns)


def head_columns(part, width):
    keys_at = QUERY_HEADS * HEAD_SIZE + part * HEAD_SIZE
    values_at = keys_at + VALUE_GROUPS * HEAD_SIZE
    pair = 2 * HEAD_SIZE
    return ((part * width, 0, width), (keys_at, width, pair), (values_at, width + pair, pair))


def split_kernel(in_ref, qkv_ref, out_ref, gain_ref, *, width):
    parts, lines, rows, _ = qkv_ref.shape
    for line in range(lines):
        for part in range(parts):
            for source, target, count in head_columns(part, width):
                qkv_ref[part, line, :, target : target + count] = in_ref[
                    line, :rows, source : source + count
                ]
        out_ref[line] = in_ref[line, rows:, :]
        gain_ref[line] = in_ref[line, : gain_ref.shape[1], in_ref.shape[2] - gain_ref.shape[2] :]


def split_columns(both, parts, rows, width, gain_width):
    lines, total, model = both.shape
    span = width + 4 * HEAD_SIZE
    return pl.pallas_call(
        functools.partial(split_kernel, width=width),
        name="split_columns",
        out_shape=(
            jax.ShapeDtypeStruct((parts, lines, rows, span), both.dtype),
            jax.ShapeDtypeStruct((lines, total - rows, model), both.dtype),
            jax.ShapeDtypeStruct((lines, min(GAIN_ROWS, rows), gain_width), both.dtype),
        ),
        compiler_params=pltpu.CompilerParams(vmem_limit_bytes=VMEM_LIMIT),
        cost_estimate=pl.CostEstimate(
            flops=0, transcendentals=0, bytes_accessed=4 * both.size
        ),
    )(both)


def join_kernel(in_ref, qkv_ref, *, width):
    parts, lines, _, _ = in_ref.shape
    for line in range(lines):
        for part in range(parts):
            qkv_ref[line, :, part * width : (part + 1) * width] = in_ref[part, line, :, :width]
        for kind in range(2):
            for group in range(VALUE_GROUPS):
                terms = []
                for part in range(max(group - 1, 0), min(group + 1, parts)):
                    at = width + (2 * kind + group - part) * HEAD_SIZE
                    terms.append(in_ref[part, line, :, at : at + HEAD_SIZE].astype(jnp.float32))
                at = (QUERY_HEADS + kind * VALUE_GROUPS + group) * HEAD_SIZE
                qkv_ref[line, :, at : at + HEAD_SIZE] = sum(terms).astype(qkv_ref.dtype)


def join_columns(qkv_parts, width):
    _, lines, rows, _ = qkv_parts.shape
    shape = (lines, rows, (QUERY_HEADS + 2 * VALUE_GROUPS) * HEAD_SIZE)
    return pl.pallas_call(
        functools.partial(join_kernel, width=width),
        name="join_columns",
        out_shape=jax.ShapeDtypeStruct(shape, jnp.bfloat16),
        compiler_params=pltpu.CompilerParams(vmem_limit_bytes=VMEM_LIMIT),
        cost_estimate=pl.CostEstimate(
            flops=0, transcendentals=0, bytes_accessed=4 * int(np.prod(shape))
        ),
    )(qkv_parts)


def adamw_kernel(
    stays_ref, fixes_ref, weight_ref, own_ref, moved_ref, first_ref, second_ref, new_ref, moments_ref,
    *, rate, shrink,
):
    high = jnp.float32
    grad = jnp.where(stays_ref[0] == 1, own_ref[...].astype(high), moved_ref[...].astype(high))
    first_new = beta_first * first_ref[...] + (1.0 - beta_first) * grad
    second_new = beta_second * second_ref[...] + (1.0 - beta_second) * grad * grad
    stepped = first_new / fixes_ref[0] / (jnp.sqrt(second_new / fixes_ref[1]) + adam_eps)
    weight = weight_ref[...]
    new_ref[...] = weight - rate * (stepped + shrink * weight)
    moments_ref[0] = first_new
    moments_ref[1] = jnp.sqrt(second_new)


def adamw_block(weight, grads, first, second, rate, shrink, stays, fixes):
    rows, columns = weight.shape
    tile = 64 if rows % 64 == 0 else rows
    block = pl.BlockSpec((tile, columns), lambda i: (i, 0))
    scalar = pl.BlockSpec(memory_space=pltpu.SMEM)
    return pl.pallas_call(
        functools.partial(adamw_kernel, rate=rate, shrink=shrink),
        name="adamw",
        out_shape=(
            jax.ShapeDtypeStruct(weight.shape, weight.dtype),
            jax.ShapeDtypeStruct((2,) + weight.shape, weight.dtype),
        ),
        grid=(rows // tile,),
        in_specs=[scalar, scalar] + [block] * 5,
        out_specs=(block, pl.BlockSpec((2, tile, columns), lambda i: (0, i, 0))),
        compiler_params=pltpu.CompilerParams(vmem_limit_bytes=VMEM_LIMIT),
        cost_estimate=pl.CostEstimate(
            flops=20 * weight.size, transcendentals=2 * weight.size, bytes_accessed=28 * weight.size
        ),
    )(stays.reshape(1), fixes, weight, grads[0], grads[1], first, second)


def adamw(weight, grad, first, second, rate, shrink, item_count):
    first_new = beta_first * first + (1.0 - beta_first) * grad
    second_new = beta_second * second + (1.0 - beta_second) * grad * grad
    fix_first = 1.0 - jnp.power(beta_first, item_count)
    fix_second = 1.0 - jnp.power(beta_second, item_count)
    stepped = first_new / fix_first / (jnp.sqrt(second_new / fix_second) + adam_eps)
    return (
        weight - rate * (stepped + shrink * weight),
        jnp.stack([first_new, jnp.sqrt(second_new)]),
    )


def local(
    sizes,
    tokens,
    cotangent,
    corpus_id,
    corpus_weight,
    step_count,
    qkv_weight,
    out_weight,
    gains,
    gate_weight,
    up_weight,
    down_weight,
    first_qkv,
    first_out,
    first_gains,
    first_gate,
    first_up,
    first_down,
    second_qkv,
    second_out,
    second_gains,
    second_gate,
    second_up,
    second_down,
):
    low = jnp.bfloat16
    high = jnp.float32
    devices = int(np.prod(sizes))
    seqs = sizes[0] * sizes[1]
    parts = sizes[2] * sizes[3]
    places = np.arange(devices).reshape(sizes)
    where = np.stack(np.unravel_index(np.arange(devices), sizes), -1)

    def permute(array, target):
        pairs = [(int(i), int(places[tuple(target(*where[i]))])) for i in range(devices)]
        return lax.ppermute(array, ALL, [pair for pair in pairs if pair[0] != pair[1]])

    def swap(array):
        moved = permute(array, lambda sh, sl, kh, kl: (sh, kl, kh, sl))
        return jnp.where(lax.axis_index("sl") == lax.axis_index("kl"), array, moved)

    def in_ffn_group(array, r):
        return permute(array, lambda sh, sl, kh, kl: (sh, sl ^ (r & 1), kh ^ (r >> 1), kl))

    def in_sequence(array, r):
        return permute(array, lambda sh, sl, kh, kl: (sh, sl, kh ^ (r >> 1), kl ^ (r & 1)))

    def along_y(array):
        return permute(array, lambda sh, sl, kh, kl: (sh, sl ^ 1, kh, kl))

    z_size = sizes[0]

    def halve(blocks, index, axis, move):
        kept = lax.dynamic_index_in_dim(blocks, index, axis, keepdims=False)
        sent = lax.dynamic_index_in_dim(blocks, index ^ 1, axis, keepdims=False)
        return (kept.astype(high) + move(sent).astype(high)).astype(low)

    item_count, model = tokens.shape
    heads = QUERY_HEADS // parts
    width = heads * HEAD_SIZE
    pair = 2 * HEAD_SIZE
    keys_at = QUERY_HEADS * HEAD_SIZE
    values_at = keys_at + VALUE_GROUPS * HEAD_SIZE
    kv = lax.axis_index(KV)
    length = item_count * parts
    cosine, sine = angle_tables(length)
    groups = ((jnp.arange(heads, dtype=jnp.int32) + kv) // 4).astype(jnp.int32)

    def stage(ready, waiting):
        return lax.optimization_barrier((ready, waiting))

    row_offsets = [
        (z * 2 + rs) * parts + r1 * 2 + r0
        for r0 in range(2) for rs in range(2) for r1 in range(2) for z in range(z_size)
    ]

    def columns_moved(array, back=False):
        return column_order(array, lax.axis_index("sl"), z_size, parts, back=back)

    def rows_moved(array, back=False):
        blocks = array.reshape(devices, -1, item_count)
        kernel = functools.partial(row_order_kernel, offsets=tuple(row_offsets), back=back)
        mine = lax.axis_index("sl") * parts + kv
        return order_call(kernel, blocks, mine).reshape(-1, item_count)

    span = width + 2 * pair
    own_rows, total_columns = qkv_weight.shape
    spare = model - total_columns
    gain_rows = -(-gains.shape[0] // spare)
    gains_block = jnp.pad(gains.astype(low), (0, own_rows * spare - gains.shape[0]))
    both = jnp.concatenate(
        [
            jnp.concatenate([qkv_weight.astype(low), gains_block.reshape(own_rows, spare)], axis=1),
            out_weight.astype(low),
        ]
    )
    both_line = lax.all_to_all(
        jnp.broadcast_to(both[None], (z_size,) + both.shape), "sh", split_axis=0, concat_axis=0, tiled=True
    )
    tokens_near = columns_moved(tokens)
    tokens_far = in_sequence(tokens_near, 2)
    gate_block = swap(gate_weight.astype(low))
    factor = jnp.sum(
        jnp.where(jnp.arange(corpus_weight.shape[0]) == corpus_id[0], corpus_weight, 0.0)
    )
    weighted = cotangent.astype(high) * factor
    weighted_low = weighted.astype(low)
    weighted_one = in_ffn_group(weighted_low, 1)
    (both_line, tokens_far, gate_block, weighted_one), (up_low, tokens_near, weighted_low) = stage(
        (both_line, tokens_far, gate_block, weighted_one),
        (up_weight.astype(low), tokens_near, weighted_low),
    )
    gate_full = lax.all_gather(gate_block, OWNERS, axis=0, tiled=True)

    qkv_parts, out_line, gain_line = split_columns(both_line, parts, own_rows, width, spare)
    gain_line = gain_line[:, :gain_rows].reshape(z_size, -1)
    gain_pairs = jnp.stack([gain_line, in_sequence(gain_line, 1)])
    gain_pairs = jnp.stack([gain_pairs, in_sequence(gain_pairs, 2)])
    qkv_rows = lax.all_to_all(
        qkv_parts, KV, split_axis=0, concat_axis=0, tiled=True
    )
    tokens_pair = (in_sequence(tokens_near, 1), in_sequence(tokens_far, 1))
    up_block = swap(up_low)
    (qkv_rows, tokens_pair, gain_pairs, up_block), (out_line, down_low, weighted_low) = stage(
        (qkv_rows, tokens_pair, gain_pairs, up_block), (out_line, down_weight.astype(low), weighted_low)
    )
    up_full = lax.all_gather(up_block, OWNERS, axis=0, tiled=True)

    qkv_far = along_y(qkv_rows)
    out_far = in_sequence(out_line, 2)
    weighted_far = in_ffn_group(weighted_low, 2)
    held = jnp.arange(2 * parts)
    mine = lax.axis_index("sl") * parts + kv
    selection = held[:, None] == (held[None, :] ^ mine)
    gain_blocks = jnp.stack([gain_pairs, along_y(gain_pairs)])[..., : gains.shape[0]]
    gain_values = contract(selection.astype(low), gain_blocks.reshape(2 * parts, -1), 1, 0)
    gain_values = gain_values.reshape(2, parts, z_size, -1).transpose(2, 0, 1, 3).reshape(-1)
    gain_one = gain_values[:model]
    gain_two = gain_values[model : 2 * model]
    gain_q = gain_values[2 * model : 2 * model + HEAD_SIZE].reshape(HEAD_SIZE, 1)
    gain_k = gain_values[2 * model + HEAD_SIZE :].reshape(HEAD_SIZE, 1)
    gain_moved = columns_moved(jnp.broadcast_to(gain_one[None], (8, model)))[:1]
    all_rows = jnp.zeros((parts, item_count, model), low)
    for r, piece in enumerate((tokens_near, tokens_pair[0], tokens_far, tokens_pair[1])):
        all_rows = lax.dynamic_update_slice_in_dim(all_rows, piece[None], kv ^ r, 0)
    all_rows = all_rows.reshape(length, model).astype(high)
    normed = (all_rows * rms_scale(all_rows) * gain_moved).astype(low)
    normed, (qkv_rows, out_line) = stage(normed, (qkv_rows, out_line))
    qkv_full = jnp.concatenate([qkv_rows, qkv_far]).reshape(model, span)

    out_near = jnp.stack([out_line, out_far])
    out_other = along_y(out_near)
    mixed = contract(qkv_full, normed, 0, 1)
    query_rows, key_rows, value_rows, outgoing, lse = attend(
        groups, mixed, cosine, sine, gain_q, gain_k, heads, item_count
    )
    (outgoing, weighted_far), (out_near, down_low) = stage((outgoing, weighted_far), (out_near, down_low))
    weighted_rows = (
        jnp.concatenate([weighted_low, weighted_one, weighted_far]), in_ffn_group(weighted_far, 1)
    )

    down_block = swap(down_low)
    attended = rows_moved(
        lax.all_to_all(outgoing, KV, split_axis=0, concat_axis=0, tiled=True)
    )
    out_full = (out_near, out_other, in_sequence(out_near, 1), in_sequence(out_other, 1))
    out_full = [piece.reshape(-1, model) for piece in out_full]
    (attended, out_full), down_block = stage((attended, out_full), down_block)
    attended = attended.reshape(4, -1, item_count)
    down_full = lax.all_gather(down_block, OWNERS, axis=0, tiled=True)
    inputs = tokens.astype(high)
    hidden = inputs + sum(contract(attended[i], out_full[i], 0, 0) for i in range(4))

    scale_two = rms_scale(hidden)
    normed_two = (hidden * scale_two * gain_two).astype(low)
    ffn_moved = [in_ffn_group(normed_two, r) for r in (3, 1, 2)]
    ffn_rows = (jnp.concatenate([normed_two, ffn_moved[1], ffn_moved[2]]), ffn_moved[0])

    def activation(rows, gate_full, up_full):
        gate = contract(rows, gate_full, 1, 0)
        up_part = contract(rows, up_full, 1, 0)
        sigma = jax.nn.sigmoid(gate)
        return (gate, up_part, sigma, (gate * sigma * up_part).astype(low))

    def activation_back(rows, down_full, gate, up_part, sigma):
        grad_acted = contract(rows, down_full, 1, 0)
        grad_gate = (grad_acted * up_part * sigma * (1.0 + gate * (1.0 - sigma))).astype(low)
        return (grad_gate, (grad_acted * (gate * sigma)).astype(low))

    def weight_gradient(left, right):
        return sum(contract(left[i], right[i], 0, 0) for i in range(2)).astype(low)

    def share(grad):
        return lax.psum_scatter(grad, OWNERS, scatter_dimension=0, tiled=True)

    near = activation(ffn_rows[0], gate_full, up_full)
    near, (gate_full, up_full) = stage(near, (gate_full, up_full))
    far = activation(ffn_rows[1], gate_full, up_full)
    acted = (near[3], far[3])
    grad_down_low = weight_gradient(weighted_rows, acted)
    down_full, grad_down_low = stage(down_full, grad_down_low)
    grad_down_share = share(grad_down_low)
    far_gate, far_up = activation_back(weighted_rows[1], down_full, *far[:3])
    sent_far = (contract(far_gate, gate_full, 1, 1) + contract(far_up, up_full, 1, 1)).astype(low)
    sent_far, weighted_near = stage(sent_far, weighted_rows[0])
    received = [in_ffn_group(sent_far, 3)]
    near_gate, near_up = activation_back(weighted_near, down_full, *near[:3])
    rows_partial = (contract(near_gate, gate_full, 1, 1) + contract(near_up, up_full, 1, 1)).astype(low)
    grad_gate, grad_up = (near_gate, far_gate), (near_up, far_up)
    rows_partial, (grad_gate, grad_up) = stage(rows_partial, (grad_gate, grad_up))
    received += [
        in_ffn_group(rows_partial[r * item_count : (r + 1) * item_count], r) for r in (1, 2)
    ]
    grad_gate_share = share(weight_gradient(ffn_rows, grad_gate))
    grad_up_low = weight_gradient(ffn_rows, grad_up)
    ffn_partial = [contract(part, down_full, 1, 1).astype(low) for part in acted]
    (received, grad_down_share), (grad_up_low, ffn_partial) = stage(
        (received, grad_down_share), (grad_up_low, ffn_partial)
    )
    grad_up_share = share(grad_up_low)
    grad_normed_two = rows_partial[:item_count].astype(high) + sum(
        piece.astype(high) for piece in received
    )

    pushed_two, gain_two_terms = norm_back(grad_normed_two, hidden, scale_two, gain_two)
    grad_hidden = weighted + pushed_two
    hidden_low = grad_hidden.astype(low)

    attended_gradient = jnp.concatenate(
        [contract(piece, hidden_low, 1, 1).astype(low) for piece in out_full]
    )
    attended_gradient = rows_moved(attended_gradient, back=True)
    incoming = lax.all_to_all(
        attended_gradient.reshape(parts, width, item_count), KV, split_axis=0, concat_axis=0, tiled=True
    )
    ffn_blocks = ffn_partial[0].reshape(3, item_count, model)
    ffn_moved = [in_ffn_group(ffn_blocks[1], 1), in_ffn_group(ffn_partial[1], 1)]
    attended = attended.reshape(2, 2, 2, -1, item_count)
    sent_out = [
        contract(attended[1, :, r].reshape(-1, item_count), hidden_low, 1, 0).astype(low) for r in range(2)
    ]
    kept_out = [
        contract(attended[0, :, r].reshape(-1, item_count), hidden_low, 1, 0) for r in range(2)
    ]
    out_line = [
        (kept_out[r] + in_sequence(sent_out[r], 1).astype(high)).astype(low) for r in range(2)
    ]
    incoming, out_line = lax.optimization_barrier((incoming, out_line))

    out_moved = in_sequence(out_line[1], 2)
    grad_queries, grad_keys, grad_values, gain_q_sum, gain_k_sum = attend_back(
        groups, mixed, query_rows, key_rows, value_rows, incoming, lse,
        cosine, sine, gain_q, gain_k, heads, item_count,
    )
    grad_mixed = jnp.concatenate(
        [grad_queries, grad_keys.reshape(pair, length), grad_values.reshape(pair, length)], axis=0
    )
    half_model = model // 2
    grad_mixed, (ffn_moved, grad_gate_share) = stage(grad_mixed, (ffn_moved, grad_gate_share))
    mixer_sent = contract(normed[:, half_model:], grad_mixed, 0, 1).astype(low)
    (mixer_sent, grad_mixed), (out_line, ffn_blocks) = stage(
        (mixer_sent, grad_mixed), (out_line[0], ffn_blocks)
    )

    mixer_moved = along_y(mixer_sent)
    mixer_line = contract(normed[:, :half_model], grad_mixed, 0, 1)
    grad_normed = contract(grad_mixed, qkv_full, 0, 1).astype(low)
    grad_normed = halve(
        grad_normed.reshape(2, 2, item_count, model), lax.axis_index("kl"), 1, lambda v: in_sequence(v, 1)
    )
    ffn_line = [
        ffn_blocks[2 * r].astype(high) + ffn_moved[r].astype(high) for r in range(2)
    ]
    mixer_line = lax.optimization_barrier(mixer_line)
    mixer_parts = (mixer_line + mixer_moved.astype(high)).astype(low)
    mixer_parts, out_line = stage(mixer_parts, out_line)

    mixer_parts = lax.all_to_all(
        mixer_parts.reshape(parts, z_size, -1, span), KV, split_axis=0, concat_axis=0, tiled=True
    )
    out_line = (out_line.astype(high) + out_moved.astype(high)).astype(low).reshape(2, z_size, -1, model)
    out_moved = along_y(out_line[1])
    qkv_line = join_columns(mixer_parts, width)
    qkv_line, (grad_normed, ffn_line, out_line, shares) = stage(
        qkv_line, (grad_normed, ffn_line, out_line[0], (grad_down_share, grad_gate_share, grad_up_share))
    )

    qkv_line = lax.all_to_all(qkv_line, "sh", split_axis=0, concat_axis=0, tiled=True)
    grad_normed = halve(grad_normed, lax.axis_index("kh"), 0, lambda v: in_sequence(v, 2)).astype(high)
    grad_normed, ffn_line = stage(grad_normed, ffn_line)
    ffn_moved = in_ffn_group(ffn_line[1].astype(low), 2)
    line = lax.axis_index("sh")

    def sum_line(blocks):
        total = lax.dynamic_index_in_dim(blocks, line, 0, keepdims=False).astype(high)
        for r in range(1, z_size):
            sent = lax.dynamic_index_in_dim(blocks, line ^ r, 0, keepdims=False)
            total = total + permute(sent, lambda sh, sl, kh, kl: (sh ^ r, sl, kh, kl)).astype(high)
        return total

    out_grad = sum_line((out_line.astype(high) + out_moved.astype(high)).astype(low))
    block_out = (hidden + (ffn_line[0] + ffn_moved.astype(high))).astype(low)
    qkv_grad = jnp.sum(qkv_line.astype(high), 0)
    grad_down, grad_gate_w, grad_up_w = (
        (piece, permute(piece, lambda sh, sl, kh, kl: (sh, kl, kh, sl))) for piece in shares
    )
    moved_inputs = tokens_near.astype(high)
    pushed_one, gain_one_terms = norm_back(
        grad_normed, moved_inputs, rms_scale(moved_inputs), gain_moved
    )
    grad_input = grad_hidden + columns_moved(pushed_one, back=True)
    gain_one_sum = columns_moved(
        jnp.broadcast_to(jnp.sum(gain_one_terms, 0)[None], (8, model)), back=True
    )[0]
    grad_gains = jnp.concatenate(
        [
            gain_one_sum,
            jnp.sum(gain_two_terms, 0),
            gain_q_sum.reshape(-1),
            gain_k_sum.reshape(-1),
        ]
    )
    grad_gains = grad_gains.reshape(z_size, 2, parts, -1).transpose(1, 2, 0, 3)
    grad_gains = lax.dot_general(
        selection.astype(high), grad_gains.reshape(2 * parts, -1), (((1,), (0,)), ((), ())),
        precision=lax.Precision.HIGHEST, preferred_element_type=high,
    ).reshape(2, 2, 2, -1)
    grad_gains = grad_gains[0] + along_y(grad_gains[1])
    grad_gains = grad_gains[:, 0] + in_sequence(grad_gains[:, 1], 1)
    grad_gains = grad_gains[0] + in_sequence(grad_gains[1], 2)
    gains_grad = sum_line(grad_gains.reshape(z_size, -1))

    steps_done = step_count[0].astype(high)
    new_qkv, moments_qkv = adamw(qkv_weight, qkv_grad, first_qkv, second_qkv, 0.02, 0.1, steps_done)
    new_out, moments_out = adamw(out_weight, out_grad, first_out, second_out, 0.2, 0.1, steps_done)
    new_gains, moments_gains = adamw(
        gains, gains_grad, first_gains, second_gains, 0.6, 0.0, steps_done
    )
    stays = (lax.axis_index("sl") == lax.axis_index("kl")).astype(jnp.int32)
    fixes = jnp.stack(
        [1.0 - jnp.power(beta_first, steps_done), 1.0 - jnp.power(beta_second, steps_done)]
    )
    new_gate, moments_gate = adamw_block(
        gate_weight, grad_gate_w, first_gate, second_gate, 0.02, 0.1, stays, fixes
    )
    new_up, moments_up = adamw_block(
        up_weight, grad_up_w, first_up, second_up, 0.02, 0.1, stays, fixes
    )
    new_down, moments_down = adamw_block(
        down_weight, grad_down, first_down, second_down, 0.013, 0.1, stays, fixes
    )
    return (
        block_out,
        grad_input,
        new_qkv,
        moments_qkv,
        new_out,
        moments_out,
        new_gains,
        moments_gains,
        new_gate,
        moments_gate,
        new_up,
        moments_up,
        new_down,
        moments_down,
    )


def solution(mesh):
    seqs, parts = mesh.shape["seq"], mesh.shape["kv"]
    sizes = (seqs // 2, 2, parts // 2, 2)
    fine = Mesh(mesh.devices.reshape(sizes), ALL)
    rows = P(ALL, None)
    block = P(SEQ, KV)
    return jax.shard_map(
        functools.partial(local, sizes),
        mesh=fine,
        in_specs=(
            rows, rows, P(SEQ), P(), P(),
            rows, rows, P(ALL), block, block, block,
            rows, rows, P(ALL), block, block, block,
            rows, rows, P(ALL), block, block, block,
        ),
        out_specs=(
            rows, rows,
            rows, P(None, ALL, None),
            rows, P(None, ALL, None),
            P(ALL), P(None, ALL),
            block, P(None, SEQ, KV),
            block, P(None, SEQ, KV),
            block, P(None, SEQ, KV),
        ),
        check_vma=False,
    )
```

```python
import functools

import jax
import jax.numpy as jnp
import numpy as np
from jax import lax
from jax.experimental import pallas as pl
from jax.experimental.pallas import tpu as pltpu
from jax.sharding import Mesh, PartitionSpec as P

QUERY_HEADS = 20
VALUE_GROUPS = 5
HEAD_SIZE = 64

eps_norm = 1e-06
masked_value = -1e30
beta_first = 0.9
beta_second = 0.95
adam_eps = 1e-08

ALL = ("sh", "sl", "kh", "kl")
SEQ = ("sh", "sl")
KV = ("kh", "kl")
OWNERS = ("sh", "kl")
VMEM_LIMIT = 40 * 1024 * 1024
GAIN_ROWS = 8


def rms_scale(value_rows):
    return lax.rsqrt(jnp.mean(value_rows * value_rows, -1, keepdims=True) + eps_norm)


def norm_back(grad_out, value_rows, scale, gain):
    shaped = value_rows * scale
    pushed = grad_out * gain
    grad_in = scale * (pushed - shaped * jnp.mean(pushed * shaped, -1, keepdims=True))
    return (grad_in, grad_out * shaped)


def angle_tables(item_count):
    places = np.arange(item_count).astype(np.float32)
    steps = np.arange(HEAD_SIZE // 2).astype(np.float32) * np.float32(2.0) / np.float32(HEAD_SIZE)
    freqs = np.float32(10000.0) ** (-steps)
    angles = freqs[:, None].astype(np.float32) * places[None, :]
    return (np.cos(angles).astype(np.float32), np.sin(angles).astype(np.float32))


def contract(left, right, left_dim, right_dim):
    return lax.dot_general(
        left,
        right,
        (((left_dim,), (right_dim,)), ((), ())),
        preferred_element_type=jnp.float32,
    )


def head_scale(rows):
    return lax.rsqrt(jnp.mean(rows * rows, 0, keepdims=True) + eps_norm)


def rotated(rows, scale, gain, cosine, sine):
    half = HEAD_SIZE // 2
    shaped = rows * scale * gain
    first, second = shaped[:half], shaped[half:]
    return jnp.concatenate(
        [first * cosine - second * sine, second * cosine + first * sine], axis=0
    )


def unrotated_norm_back(grad, rows, scale, gain, cosine, sine):
    half = HEAD_SIZE // 2
    first, second = grad[:half], grad[half:]
    turned = jnp.concatenate(
        [first * cosine + second * sine, second * cosine - first * sine], axis=0
    )
    shaped = rows * scale
    pushed = turned * gain
    grad_in = scale * (pushed - shaped * jnp.mean(pushed * shaped, 0, keepdims=True))
    return (grad_in, turned * shaped)


def causal(block):
    keys = lax.broadcasted_iota(jnp.int32, (block, block), 0)
    places = lax.broadcasted_iota(jnp.int32, (block, block), 1)
    return keys <= places


def forward_kernel(
    group_ref, qp_ref, kp_ref, vp_ref, cos_ref, sin_ref, gq_ref, gk_ref,
    q_ref, k_ref, v_ref, out_ref, lse_ref, *, block,
):
    cosine, sine = cos_ref[...], sin_ref[...]
    qp, kp = qp_ref[...], kp_ref[...]
    query = (rotated(qp, head_scale(qp), gq_ref[...], cosine, sine) * 0.125).astype(jnp.bfloat16)
    key = rotated(kp, head_scale(kp), gk_ref[...], cosine, sine).astype(jnp.bfloat16)
    value = vp_ref[...].astype(jnp.bfloat16)
    q_ref[0] = query
    k_ref[0] = key
    v_ref[0] = value
    allowed = causal(block)
    for index in range(query.shape[1] // block):
        start, stop = index * block, (index + 1) * block
        part = query[:, start:stop]
        near = contract(key[:, start:stop], part, 0, 0)
        near = jnp.where(allowed, near, masked_value)
        top = jnp.max(near, 0, keepdims=True)
        if index:
            far = contract(key[:, :start], part, 0, 0)
            top = jnp.maximum(top, jnp.max(far, 0, keepdims=True))
        near = jnp.exp(near - top)
        total = jnp.sum(near, 0, keepdims=True)
        if index:
            far = jnp.exp(far - top)
            total = total + jnp.sum(far, 0, keepdims=True)
        share = 1.0 / total
        result = contract(value[:, start:stop], (near * share).astype(jnp.bfloat16), 1, 0)
        if index:
            result = result + contract(value[:, :start], (far * share).astype(jnp.bfloat16), 1, 0)
        out_ref[index] = result.astype(jnp.bfloat16)
        lse_ref[0, :, start:stop] = top + jnp.log(total)


def backward_kernel(
    group_ref, qp_ref, kp_ref, q_ref, k_ref, v_ref, do_ref, lse_ref, cos_ref, sin_ref,
    gq_ref, gk_ref,
    gqp_ref, gkp_ref, gv_ref, gain_q_ref, gain_k_ref,
    dq_ref, dk_ref, dv_ref, sum_q_ref, sum_k_ref, *, block,
):
    head = pl.program_id(0)
    heads = pl.num_programs(0)
    group = group_ref[head]
    opens = jnp.logical_or(head == 0, group_ref[jnp.maximum(head - 1, 0)] != group)
    closes = jnp.logical_or(
        head == heads - 1, group_ref[jnp.minimum(head + 1, heads - 1)] != group
    )

    @pl.when(head == 0)
    def _():
        sum_q_ref[...] = jnp.zeros_like(sum_q_ref)
        sum_k_ref[...] = jnp.zeros_like(sum_k_ref)

    @pl.when(opens)
    def _():
        dk_ref[...] = jnp.zeros_like(dk_ref)
        dv_ref[...] = jnp.zeros_like(dv_ref)

    query, key, value = q_ref[0], k_ref[0], v_ref[0]
    allowed = causal(block)
    for index in range(query.shape[1] // block):
        start, stop = index * block, (index + 1) * block
        part, grad_part = query[:, start:stop], do_ref[index]
        sums_log = lse_ref[0, :, start:stop]
        near = jnp.exp(contract(key[:, start:stop], part, 0, 0) - sums_log)
        near = jnp.where(allowed, near, 0.0)
        grad_near = contract(value[:, start:stop], grad_part, 0, 0)
        inner = jnp.sum(near * grad_near, 0, keepdims=True)
        if index:
            far = jnp.exp(contract(key[:, :start], part, 0, 0) - sums_log)
            grad_far = contract(value[:, :start], grad_part, 0, 0)
            inner = inner + jnp.sum(far * grad_far, 0, keepdims=True)
        step = (near * (grad_near - inner)).astype(jnp.bfloat16)
        total = contract(key[:, start:stop], step, 1, 0)
        dk_ref[:, start:stop] += contract(part, step, 1, 1)
        dv_ref[:, start:stop] += contract(grad_part, near.astype(jnp.bfloat16), 1, 1)
        if index:
            step = (far * (grad_far - inner)).astype(jnp.bfloat16)
            total = total + contract(key[:, :start], step, 1, 0)
            dk_ref[:, :start] += contract(part, step, 1, 1)
            dv_ref[:, :start] += contract(grad_part, far.astype(jnp.bfloat16), 1, 1)
        dq_ref[:, start:stop] = total * 0.125

    cosine, sine = cos_ref[...], sin_ref[...]
    qp = qp_ref[...]
    grad_qp, gain_terms = unrotated_norm_back(
        dq_ref[...].astype(jnp.bfloat16).astype(jnp.float32),
        qp, head_scale(qp), gq_ref[...], cosine, sine,
    )
    gqp_ref[...] = grad_qp.astype(jnp.bfloat16)
    sum_q_ref[...] += gain_terms

    @pl.when(closes)
    def _():
        kp = kp_ref[...]
        grad_kp, terms = unrotated_norm_back(
            dk_ref[...].astype(jnp.bfloat16).astype(jnp.float32),
            kp, head_scale(kp), gk_ref[...], cosine, sine,
        )
        gkp_ref[0] = grad_kp.astype(jnp.bfloat16)
        gv_ref[0] = dv_ref[...].astype(jnp.bfloat16)
        sum_k_ref[...] += terms

    @pl.when(head == heads - 1)
    def _():
        gain_q_ref[...] = jnp.sum(sum_q_ref[...], 1, keepdims=True)
        gain_k_ref[...] = jnp.sum(sum_k_ref[...], 1, keepdims=True)


def attention_specs(length, heads, block):
    half = HEAD_SIZE // 2
    tall = (HEAD_SIZE, length)
    whole = lambda shape: pl.BlockSpec(shape, lambda h, g: (0, 0))
    per_head = pl.BlockSpec((1,) + tall, lambda h, g: (h, 0, 0))
    per_group = pl.BlockSpec((1,) + tall, lambda h, g: (g[h], 0, 0))
    per_row = pl.BlockSpec((1, 1, length), lambda h, g: (h, 0, 0))
    query = pl.BlockSpec(tall, lambda h, g: (h, 0))
    key = pl.BlockSpec(tall, lambda h, g: (heads + g[h], 0))
    value = pl.BlockSpec(tall, lambda h, g: (heads + 2 + g[h], 0))
    table = whole((half, length))
    gain = whole((HEAD_SIZE, 1))
    per_owner = pl.BlockSpec((length // block, HEAD_SIZE, block), lambda h, g: (0, h, 0))
    return (query, key, value, per_head, per_group, per_row, table, gain, per_owner)


def attend(groups, mixed, cosine, sine, gain_q, gain_k, heads, block):
    length = mixed.shape[1]
    query, key, value, per_head, per_group, per_row, table, gain, per_owner = attention_specs(
        length, heads, block
    )
    per = lambda count: jax.ShapeDtypeStruct((count, HEAD_SIZE, length), jnp.bfloat16)
    scores = heads * length * length // 2
    return pl.pallas_call(
        functools.partial(forward_kernel, block=block),
        name="attention_forward",
        out_shape=(
            per(heads), per(2), per(2),
            jax.ShapeDtypeStruct((length // block, heads * HEAD_SIZE, block), jnp.bfloat16),
            jax.ShapeDtypeStruct((heads, 1, length), jnp.float32),
        ),
        grid_spec=pltpu.PrefetchScalarGridSpec(
            num_scalar_prefetch=1,
            grid=(heads,),
            in_specs=[query, key, value, table, table, gain, gain],
            out_specs=[per_head, per_group, per_group, per_owner, per_row],
        ),
        compiler_params=pltpu.CompilerParams(
            dimension_semantics=("arbitrary",), vmem_limit_bytes=VMEM_LIMIT
        ),
        cost_estimate=pl.CostEstimate(
            flops=scores * 4 * HEAD_SIZE, transcendentals=scores, bytes_accessed=8_000_000
        ),
    )(groups, mixed, mixed, mixed, cosine, sine, gain_q, gain_k)


def attend_back(
    groups, mixed, query_rows, key_rows, value_rows, grads, lse, cosine, sine, gain_q, gain_k, heads, block
):
    length = mixed.shape[1]
    query, key, value, per_head, per_group, per_row, table, gain, per_owner = attention_specs(
        length, heads, block
    )
    tall = (HEAD_SIZE, length)
    scores = heads * length * length // 2
    return pl.pallas_call(
        functools.partial(backward_kernel, block=block),
        name="attention_backward",
        out_shape=(
            jax.ShapeDtypeStruct((heads * HEAD_SIZE, length), jnp.bfloat16),
            jax.ShapeDtypeStruct((2,) + tall, jnp.bfloat16),
            jax.ShapeDtypeStruct((2,) + tall, jnp.bfloat16),
            jax.ShapeDtypeStruct((HEAD_SIZE, 1), jnp.float32),
            jax.ShapeDtypeStruct((HEAD_SIZE, 1), jnp.float32),
        ),
        grid_spec=pltpu.PrefetchScalarGridSpec(
            num_scalar_prefetch=1,
            grid=(heads,),
            in_specs=[
                query, key, per_head, per_group, per_group, per_owner, per_row, table, table, gain, gain,
            ],
            out_specs=[query, per_group, per_group, gain, gain],
            scratch_shapes=[pltpu.VMEM(tall, jnp.float32)] * 5,
        ),
        compiler_params=pltpu.CompilerParams(
            dimension_semantics=("arbitrary",), vmem_limit_bytes=VMEM_LIMIT
        ),
        cost_estimate=pl.CostEstimate(
            flops=scores * 10 * HEAD_SIZE, transcendentals=scores, bytes_accessed=10_000_000
        ),
    )(groups, mixed, mixed, query_rows, key_rows, value_rows, grads, lse, cosine, sine, gain_q, gain_k)


def row_order_kernel(mine_ref, in_ref, out_ref, *, offsets, back):
    for index, offset in enumerate(offsets):
        held = mine_ref[0] ^ offset
        if back:
            out_ref[held] = in_ref[index]
        else:
            out_ref[index] = in_ref[held]


def column_order_kernel(mine_ref, in_ref, out_ref, *, lines, parts, back):
    width = in_ref.shape[1] // (2 * lines)
    small = width // parts
    for plane in range(2):
        for line in range(lines):
            held = pl.multiple_of((mine_ref[0] ^ (line * 2 + plane)) * width, width)
            places = [(plane * parts + part) * lines + line for part in range(parts)]
            if back:
                out_ref[:, pl.ds(held, width)] = jnp.concatenate(
                    [in_ref[:, at * small : (at + 1) * small] for at in places], axis=1
                )
            else:
                block = in_ref[:, pl.ds(held, width)]
                for part, at in enumerate(places):
                    out_ref[:, at * small : (at + 1) * small] = block[
                        :, part * small : (part + 1) * small
                    ]


def order_call(kernel, array, mine):
    return pl.pallas_call(
        kernel,
        name="block_order",
        out_shape=jax.ShapeDtypeStruct(array.shape, array.dtype),
        in_specs=[
            pl.BlockSpec(memory_space=pltpu.SMEM),
            pl.BlockSpec(memory_space=pltpu.VMEM),
        ],
        out_specs=pl.BlockSpec(memory_space=pltpu.VMEM),
        compiler_params=pltpu.CompilerParams(vmem_limit_bytes=VMEM_LIMIT),
        cost_estimate=pl.CostEstimate(
            flops=0, transcendentals=0, bytes_accessed=4 * array.size
        ),
    )(mine.reshape(1).astype(jnp.int32), array)


def column_order(array, mine, lines, parts, back=False):
    rows, columns = array.shape
    width = columns // (2 * lines)
    if width % 128 == 0:
        kernel = functools.partial(column_order_kernel, lines=lines, parts=parts, back=back)
        return order_call(kernel, array, mine)
    small = width // parts
    if back:
        array = array.reshape(rows, 2, parts, lines, small).transpose(0, 3, 1, 2, 4)
        return jnp.where(mine == 0, array, array[:, :, ::-1]).reshape(rows, columns)
    array = array.reshape(rows, lines, 2, parts, small)
    array = jnp.where(mine == 0, array, array[:, :, ::-1])
    return array.transpose(0, 2, 3, 1, 4).reshape(rows, columns)


def head_columns(part, width):
    keys_at = QUERY_HEADS * HEAD_SIZE + part * HEAD_SIZE
    values_at = keys_at + VALUE_GROUPS * HEAD_SIZE
    pair = 2 * HEAD_SIZE
    return ((part * width, 0, width), (keys_at, width, pair), (values_at, width + pair, pair))


def split_kernel(in_ref, qkv_ref, out_ref, gain_ref, *, width):
    parts, lines, rows, _ = qkv_ref.shape
    for line in range(lines):
        for part in range(parts):
            for source, target, count in head_columns(part, width):
                qkv_ref[part, line, :, target : target + count] = in_ref[
                    line, :rows, source : source + count
                ]
        out_ref[line] = in_ref[line, rows:, :]
        gain_ref[line] = in_ref[line, : gain_ref.shape[1], in_ref.shape[2] - gain_ref.shape[2] :]


def split_columns(both, parts, rows, width, gain_width):
    lines, total, model = both.shape
    span = width + 4 * HEAD_SIZE
    return pl.pallas_call(
        functools.partial(split_kernel, width=width),
        name="split_columns",
        out_shape=(
            jax.ShapeDtypeStruct((parts, lines, rows, span), both.dtype),
            jax.ShapeDtypeStruct((lines, total - rows, model), both.dtype),
            jax.ShapeDtypeStruct((lines, min(GAIN_ROWS, rows), gain_width), both.dtype),
        ),
        compiler_params=pltpu.CompilerParams(vmem_limit_bytes=VMEM_LIMIT),
        cost_estimate=pl.CostEstimate(
            flops=0, transcendentals=0, bytes_accessed=4 * both.size
        ),
    )(both)


def join_kernel(in_ref, qkv_ref, *, width):
    parts, lines, _, _ = in_ref.shape
    for line in range(lines):
        for part in range(parts):
            qkv_ref[line, :, part * width : (part + 1) * width] = in_ref[part, line, :, :width]
        for kind in range(2):
            for group in range(VALUE_GROUPS):
                terms = []
                for part in range(max(group - 1, 0), min(group + 1, parts)):
                    at = width + (2 * kind + group - part) * HEAD_SIZE
                    terms.append(in_ref[part, line, :, at : at + HEAD_SIZE].astype(jnp.float32))
                at = (QUERY_HEADS + kind * VALUE_GROUPS + group) * HEAD_SIZE
                qkv_ref[line, :, at : at + HEAD_SIZE] = sum(terms).astype(qkv_ref.dtype)


def join_columns(qkv_parts, width):
    _, lines, rows, _ = qkv_parts.shape
    shape = (lines, rows, (QUERY_HEADS + 2 * VALUE_GROUPS) * HEAD_SIZE)
    return pl.pallas_call(
        functools.partial(join_kernel, width=width),
        name="join_columns",
        out_shape=jax.ShapeDtypeStruct(shape, jnp.bfloat16),
        compiler_params=pltpu.CompilerParams(vmem_limit_bytes=VMEM_LIMIT),
        cost_estimate=pl.CostEstimate(
            flops=0, transcendentals=0, bytes_accessed=4 * int(np.prod(shape))
        ),
    )(qkv_parts)


def adamw_kernel(
    stays_ref, fixes_ref, weight_ref, own_ref, moved_ref, first_ref, second_ref, new_ref, moments_ref,
    *, rate, shrink,
):
    high = jnp.float32
    grad = jnp.where(stays_ref[0] == 1, own_ref[...].astype(high), moved_ref[...].astype(high))
    first_new = beta_first * first_ref[...] + (1.0 - beta_first) * grad
    second_new = beta_second * second_ref[...] + (1.0 - beta_second) * grad * grad
    stepped = first_new / fixes_ref[0] / (jnp.sqrt(second_new / fixes_ref[1]) + adam_eps)
    weight = weight_ref[...]
    new_ref[...] = weight - rate * (stepped + shrink * weight)
    moments_ref[0] = first_new
    moments_ref[1] = jnp.sqrt(second_new)


def adamw_block(weight, grads, first, second, rate, shrink, stays, fixes):
    rows, columns = weight.shape
    tile = 64 if rows % 64 == 0 else rows
    block = pl.BlockSpec((tile, columns), lambda i: (i, 0))
    scalar = pl.BlockSpec(memory_space=pltpu.SMEM)
    return pl.pallas_call(
        functools.partial(adamw_kernel, rate=rate, shrink=shrink),
        name="adamw",
        out_shape=(
            jax.ShapeDtypeStruct(weight.shape, weight.dtype),
            jax.ShapeDtypeStruct((2,) + weight.shape, weight.dtype),
        ),
        grid=(rows // tile,),
        in_specs=[scalar, scalar] + [block] * 5,
        out_specs=(block, pl.BlockSpec((2, tile, columns), lambda i: (0, i, 0))),
        compiler_params=pltpu.CompilerParams(vmem_limit_bytes=VMEM_LIMIT),
        cost_estimate=pl.CostEstimate(
            flops=20 * weight.size, transcendentals=2 * weight.size, bytes_accessed=28 * weight.size
        ),
    )(stays.reshape(1), fixes, weight, grads[0], grads[1], first, second)


def adamw(weight, grad, first, second, rate, shrink, item_count):
    first_new = beta_first * first + (1.0 - beta_first) * grad
    second_new = beta_second * second + (1.0 - beta_second) * grad * grad
    fix_first = 1.0 - jnp.power(beta_first, item_count)
    fix_second = 1.0 - jnp.power(beta_second, item_count)
    stepped = first_new / fix_first / (jnp.sqrt(second_new / fix_second) + adam_eps)
    return (
        weight - rate * (stepped + shrink * weight),
        jnp.stack([first_new, jnp.sqrt(second_new)]),
    )


def local(
    sizes,
    tokens,
    cotangent,
    corpus_id,
    corpus_weight,
    step_count,
    qkv_weight,
    out_weight,
    gains,
    gate_weight,
    up_weight,
    down_weight,
    first_qkv,
    first_out,
    first_gains,
    first_gate,
    first_up,
    first_down,
    second_qkv,
    second_out,
    second_gains,
    second_gate,
    second_up,
    second_down,
):
    low = jnp.bfloat16
    high = jnp.float32
    devices = int(np.prod(sizes))
    seqs = sizes[0] * sizes[1]
    parts = sizes[2] * sizes[3]
    places = np.arange(devices).reshape(sizes)
    where = np.stack(np.unravel_index(np.arange(devices), sizes), -1)

    def permute(array, target):
        pairs = [(int(i), int(places[tuple(target(*where[i]))])) for i in range(devices)]
        return lax.ppermute(array, ALL, [pair for pair in pairs if pair[0] != pair[1]])

    def swap(array):
        moved = permute(array, lambda sh, sl, kh, kl: (sh, kl, kh, sl))
        return jnp.where(lax.axis_index("sl") == lax.axis_index("kl"), array, moved)

    def in_ffn_group(array, r):
        return permute(array, lambda sh, sl, kh, kl: (sh, sl ^ (r & 1), kh ^ (r >> 1), kl))

    def in_sequence(array, r):
        return permute(array, lambda sh, sl, kh, kl: (sh, sl, kh ^ (r >> 1), kl ^ (r & 1)))

    def along_y(array):
        return permute(array, lambda sh, sl, kh, kl: (sh, sl ^ 1, kh, kl))

    z_size = sizes[0]

    def halve(blocks, index, axis, move):
        kept = lax.dynamic_index_in_dim(blocks, index, axis, keepdims=False)
        sent = lax.dynamic_index_in_dim(blocks, index ^ 1, axis, keepdims=False)
        return (kept.astype(high) + move(sent).astype(high)).astype(low)

    item_count, model = tokens.shape
    heads = QUERY_HEADS // parts
    width = heads * HEAD_SIZE
    pair = 2 * HEAD_SIZE
    keys_at = QUERY_HEADS * HEAD_SIZE
    values_at = keys_at + VALUE_GROUPS * HEAD_SIZE
    kv = lax.axis_index(KV)
    length = item_count * parts
    cosine, sine = angle_tables(length)
    groups = ((jnp.arange(heads, dtype=jnp.int32) + kv) // 4).astype(jnp.int32)

    def stage(ready, waiting):
        return lax.optimization_barrier((ready, waiting))

    row_offsets = [
        (z * 2 + rs) * parts + r1 * 2 + r0
        for r0 in range(2) for r1 in range(2) for rs in range(2) for z in range(z_size)
    ]

    def columns_moved(array, back=False):
        return column_order(array, lax.axis_index("sl"), z_size, parts, back=back)

    def rows_moved(array, back=False):
        blocks = array.reshape(devices, -1, item_count)
        kernel = functools.partial(row_order_kernel, offsets=tuple(row_offsets), back=back)
        mine = lax.axis_index("sl") * parts + kv
        return order_call(kernel, blocks, mine).reshape(-1, item_count)

    span = width + 2 * pair
    own_rows, total_columns = qkv_weight.shape
    spare = model - total_columns
    gain_rows = -(-gains.shape[0] // spare)
    gains_block = jnp.pad(gains.astype(low), (0, own_rows * spare - gains.shape[0]))
    both = jnp.concatenate(
        [
            jnp.concatenate([qkv_weight.astype(low), gains_block.reshape(own_rows, spare)], axis=1),
            out_weight.astype(low),
        ]
    )
    both_line = lax.all_to_all(
        jnp.broadcast_to(both[None], (z_size,) + both.shape), "sh", split_axis=0, concat_axis=0, tiled=True
    )
    tokens_near = columns_moved(tokens)
    tokens_far = in_sequence(tokens_near, 2)
    gate_block = swap(gate_weight.astype(low))
    factor = jnp.sum(
        jnp.where(jnp.arange(corpus_weight.shape[0]) == corpus_id[0], corpus_weight, 0.0)
    )
    weighted = cotangent.astype(high) * factor
    weighted_low = weighted.astype(low)
    weighted_one = in_ffn_group(weighted_low, 1)
    (both_line, tokens_far, gate_block, weighted_one), (up_low, tokens_near, weighted_low) = stage(
        (both_line, tokens_far, gate_block, weighted_one),
        (up_weight.astype(low), tokens_near, weighted_low),
    )
    gate_full = lax.all_gather(gate_block, OWNERS, axis=0, tiled=True)

    qkv_parts, out_line, gain_line = split_columns(both_line, parts, own_rows, width, spare)
    gain_line = gain_line[:, :gain_rows].reshape(z_size, -1)
    gain_pairs = jnp.stack([gain_line, in_sequence(gain_line, 1)])
    gain_pairs = jnp.stack([gain_pairs, in_sequence(gain_pairs, 2)])
    qkv_rows = lax.all_to_all(
        qkv_parts, KV, split_axis=0, concat_axis=0, tiled=True
    )
    tokens_pair = (in_sequence(tokens_near, 1), in_sequence(tokens_far, 1))
    up_block = swap(up_low)
    out_near = jnp.stack([out_line, along_y(out_line)])
    (qkv_rows, tokens_pair, gain_pairs, up_block, out_near), (down_low, weighted_low) = stage(
        (qkv_rows, tokens_pair, gain_pairs, up_block, out_near), (down_weight.astype(low), weighted_low)
    )
    up_full = lax.all_gather(up_block, OWNERS, axis=0, tiled=True)

    qkv_far = along_y(qkv_rows)
    out_far = in_sequence(out_near, 2)
    held = jnp.arange(2 * parts)
    mine = lax.axis_index("sl") * parts + kv
    selection = held[:, None] == (held[None, :] ^ mine)
    gain_blocks = jnp.stack([gain_pairs, along_y(gain_pairs)])[..., : gains.shape[0]]
    gain_values = contract(selection.astype(low), gain_blocks.reshape(2 * parts, -1), 1, 0)
    gain_values = gain_values.reshape(2, parts, z_size, -1).transpose(2, 0, 1, 3).reshape(-1)
    gain_one = gain_values[:model]
    gain_two = gain_values[model : 2 * model]
    gain_q = gain_values[2 * model : 2 * model + HEAD_SIZE].reshape(HEAD_SIZE, 1)
    gain_k = gain_values[2 * model + HEAD_SIZE :].reshape(HEAD_SIZE, 1)
    gain_moved = columns_moved(jnp.broadcast_to(gain_one[None], (8, model)))[:1]
    all_rows = jnp.zeros((parts, item_count, model), low)
    for r, piece in enumerate((tokens_near, tokens_pair[0], tokens_far, tokens_pair[1])):
        all_rows = lax.dynamic_update_slice_in_dim(all_rows, piece[None], kv ^ r, 0)
    all_rows = all_rows.reshape(length, model).astype(high)
    normed = (all_rows * rms_scale(all_rows) * gain_moved).astype(low)
    normed, qkv_rows = stage(normed, qkv_rows)
    qkv_full = jnp.concatenate([qkv_rows, qkv_far]).reshape(model, span)

    mixed = contract(qkv_full, normed, 0, 1)
    mixed, weighted_low = stage(mixed, weighted_low)
    weighted_far = in_ffn_group(weighted_low, 2)
    query_rows, key_rows, value_rows, outgoing, lse = attend(
        groups, mixed, cosine, sine, gain_q, gain_k, heads, item_count
    )
    outgoing, (out_near, down_low) = stage(outgoing, (out_near, down_low))
    weighted_rows = (
        jnp.concatenate([weighted_low, weighted_one, weighted_far]), in_ffn_group(weighted_far, 1)
    )

    down_block = swap(down_low)
    attended = rows_moved(
        lax.all_to_all(outgoing, KV, split_axis=0, concat_axis=0, tiled=True)
    )
    out_full = (out_near, out_far, in_sequence(out_near, 1), in_sequence(out_far, 1))
    out_full = [piece.reshape(-1, model) for piece in out_full]
    (attended, out_full), down_block = stage((attended, out_full), down_block)
    attended = attended.reshape(4, -1, item_count)
    down_full = lax.all_gather(down_block, OWNERS, axis=0, tiled=True)
    inputs = tokens.astype(high)
    hidden = inputs + sum(contract(attended[i], out_full[i], 0, 0) for i in range(4))

    scale_two = rms_scale(hidden)
    normed_two = (hidden * scale_two * gain_two).astype(low)
    ffn_moved = [in_ffn_group(normed_two, r) for r in (3, 1, 2)]
    ffn_rows = (jnp.concatenate([normed_two, ffn_moved[1], ffn_moved[2]]), ffn_moved[0])

    def activation(rows, gate_full, up_full):
        gate = contract(rows, gate_full, 1, 0)
        up_part = contract(rows, up_full, 1, 0)
        sigma = jax.nn.sigmoid(gate)
        return (gate, up_part, sigma, (gate * sigma * up_part).astype(low))

    def activation_back(rows, down_full, gate, up_part, sigma):
        grad_acted = contract(rows, down_full, 1, 0)
        grad_gate = (grad_acted * up_part * sigma * (1.0 + gate * (1.0 - sigma))).astype(low)
        return (grad_gate, (grad_acted * (gate * sigma)).astype(low))

    def weight_gradient(left, right):
        return sum(contract(left[i], right[i], 0, 0) for i in range(2)).astype(low)

    def share(grad):
        return lax.psum_scatter(grad, OWNERS, scatter_dimension=0, tiled=True)

    near = activation(ffn_rows[0], gate_full, up_full)
    near, (gate_full, up_full) = stage(near, (gate_full, up_full))
    far = activation(ffn_rows[1], gate_full, up_full)
    acted = (near[3], far[3])
    grad_down_low = weight_gradient(weighted_rows, acted)
    down_full, grad_down_low = stage(down_full, grad_down_low)
    grad_down_share = share(grad_down_low)
    far_gate, far_up = activation_back(weighted_rows[1], down_full, *far[:3])
    sent_far = (contract(far_gate, gate_full, 1, 1) + contract(far_up, up_full, 1, 1)).astype(low)
    sent_far, weighted_near = stage(sent_far, weighted_rows[0])
    received_far = in_ffn_group(sent_far, 3)
    near_gate, near_up = activation_back(weighted_near, down_full, *near[:3])
    rows_partial = (contract(near_gate, gate_full, 1, 1) + contract(near_up, up_full, 1, 1)).astype(low)
    received = [
        in_ffn_group(rows_partial[r * item_count : (r + 1) * item_count], r) for r in (1, 2)
    ]
    grad_gate, grad_up = (near_gate, far_gate), (near_up, far_up)
    (received_far, rows_partial), (grad_gate, grad_up) = stage(
        (received_far, rows_partial), (grad_gate, grad_up)
    )
    grad_gate_share = share(weight_gradient(ffn_rows, grad_gate))
    grad_up_low = weight_gradient(ffn_rows, grad_up)
    ffn_partial = [contract(part, down_full, 1, 1).astype(low) for part in acted]
    (received, grad_down_share), (grad_up_low, ffn_partial) = stage(
        (received, grad_down_share), (grad_up_low, ffn_partial)
    )
    received = received + [received_far]
    grad_up_share = share(grad_up_low)
    grad_normed_two = rows_partial[:item_count].astype(high) + sum(
        piece.astype(high) for piece in received
    )

    pushed_two, gain_two_terms = norm_back(grad_normed_two, hidden, scale_two, gain_two)
    grad_hidden = weighted + pushed_two
    hidden_low = grad_hidden.astype(low)

    attended_gradient = jnp.concatenate(
        [contract(piece, hidden_low, 1, 1).astype(low) for piece in out_full]
    )
    attended_gradient = rows_moved(attended_gradient, back=True)
    incoming = lax.all_to_all(
        attended_gradient.reshape(parts, width, item_count), KV, split_axis=0, concat_axis=0, tiled=True
    )
    ffn_blocks = ffn_partial[0].reshape(3, item_count, model)
    ffn_moved = [in_ffn_group(ffn_blocks[1], 1), in_ffn_group(ffn_partial[1], 1)]
    sent_out = [
        contract(attended[2 + r], hidden_low, 1, 0).astype(low) for r in range(2)
    ]
    kept_out = [
        contract(attended[r], hidden_low, 1, 0) for r in range(2)
    ]
    out_line = [
        (kept_out[r] + in_sequence(sent_out[r], 1).astype(high)).astype(low) for r in range(2)
    ]
    incoming, out_line = lax.optimization_barrier((incoming, out_line))

    out_moved = in_sequence(out_line[1], 2)
    grad_queries, grad_keys, grad_values, gain_q_sum, gain_k_sum = attend_back(
        groups, mixed, query_rows, key_rows, value_rows, incoming, lse,
        cosine, sine, gain_q, gain_k, heads, item_count,
    )
    grad_mixed = jnp.concatenate(
        [grad_queries, grad_keys.reshape(pair, length), grad_values.reshape(pair, length)], axis=0
    )
    half_model = model // 2
    grad_mixed, (ffn_moved, grad_gate_share) = stage(grad_mixed, (ffn_moved, grad_gate_share))
    mixer_sent = contract(normed[:, half_model:], grad_mixed, 0, 1).astype(low)
    (mixer_sent, grad_mixed), (out_line, ffn_blocks) = stage(
        (mixer_sent, grad_mixed), (out_line[0], ffn_blocks)
    )

    mixer_moved = along_y(mixer_sent)
    mixer_line = contract(normed[:, :half_model], grad_mixed, 0, 1)
    grad_normed = contract(grad_mixed, qkv_full, 0, 1).astype(low)
    grad_normed = grad_normed.reshape(2, 2, item_count, model)
    core = lax.axis_index("kl")
    normed_moved = in_sequence(lax.dynamic_index_in_dim(grad_normed, core ^ 1, 1, keepdims=False), 1)
    ffn_line = [
        ffn_blocks[2 * r].astype(high) + ffn_moved[r].astype(high) for r in range(2)
    ]
    mixer_line = lax.optimization_barrier(mixer_line)
    mixer_parts = (mixer_line + mixer_moved.astype(high)).astype(low)
    mixer_parts, (out_line, shares, ffn_line) = stage(
        mixer_parts, (out_line, (grad_down_share, grad_gate_share), ffn_line)
    )
    swapped = [permute(piece, lambda sh, sl, kh, kl: (sh, kl, kh, sl)) for piece in shares]
    ffn_moved = in_ffn_group(ffn_line[1].astype(low), 2)
    swapped, ffn_moved = stage(swapped, ffn_moved)

    mixer_parts = lax.all_to_all(
        mixer_parts.reshape(parts, z_size, -1, span), KV, split_axis=0, concat_axis=0, tiled=True
    )
    out_line = (out_line.astype(high) + out_moved.astype(high)).astype(low).reshape(2, z_size, -1, model)
    out_moved = along_y(out_line[1])
    qkv_line = join_columns(mixer_parts, width)
    qkv_line, (grad_normed, normed_moved, out_line, grad_up_share) = stage(
        qkv_line, (grad_normed, normed_moved, out_line[0], grad_up_share)
    )

    qkv_line = lax.all_to_all(qkv_line, "sh", split_axis=0, concat_axis=0, tiled=True)
    grad_normed = lax.dynamic_index_in_dim(grad_normed, core, 1, keepdims=False).astype(high)
    grad_normed = (grad_normed + normed_moved.astype(high)).astype(low)
    grad_normed = halve(grad_normed, lax.axis_index("kh"), 0, lambda v: in_sequence(v, 2)).astype(high)
    line = lax.axis_index("sh")

    def sum_line(blocks):
        total = lax.dynamic_index_in_dim(blocks, line, 0, keepdims=False).astype(high)
        for r in range(1, z_size):
            sent = lax.dynamic_index_in_dim(blocks, line ^ r, 0, keepdims=False)
            total = total + permute(sent, lambda sh, sl, kh, kl: (sh ^ r, sl, kh, kl)).astype(high)
        return total

    out_grad = sum_line((out_line.astype(high) + out_moved.astype(high)).astype(low))
    block_out = (hidden + (ffn_line[0] + ffn_moved.astype(high))).astype(low)
    qkv_grad = jnp.sum(qkv_line.astype(high), 0)
    grad_down, grad_gate_w = zip(shares, swapped)
    grad_up_w = (grad_up_share, permute(grad_up_share, lambda sh, sl, kh, kl: (sh, kl, kh, sl)))
    moved_inputs = tokens_near.astype(high)
    pushed_one, gain_one_terms = norm_back(
        grad_normed, moved_inputs, rms_scale(moved_inputs), gain_moved
    )
    grad_input = grad_hidden + columns_moved(pushed_one, back=True)
    gain_one_sum = columns_moved(
        jnp.broadcast_to(jnp.sum(gain_one_terms, 0)[None], (8, model)), back=True
    )[0]
    grad_gains = jnp.concatenate(
        [
            gain_one_sum,
            jnp.sum(gain_two_terms, 0),
            gain_q_sum.reshape(-1),
            gain_k_sum.reshape(-1),
        ]
    )
    grad_gains = grad_gains.reshape(z_size, 2, parts, -1).transpose(1, 2, 0, 3)
    grad_gains = lax.dot_general(
        selection.astype(high), grad_gains.reshape(2 * parts, -1), (((1,), (0,)), ((), ())),
        precision=lax.Precision.HIGHEST, preferred_element_type=high,
    ).reshape(2, 2, 2, -1)
    grad_gains = grad_gains[0] + along_y(grad_gains[1])
    grad_gains = grad_gains[:, 0] + in_sequence(grad_gains[:, 1], 1)
    grad_gains = grad_gains[0] + in_sequence(grad_gains[1], 2)
    gains_grad = sum_line(grad_gains.reshape(z_size, -1))

    steps_done = step_count[0].astype(high)
    new_qkv, moments_qkv = adamw(qkv_weight, qkv_grad, first_qkv, second_qkv, 0.02, 0.1, steps_done)
    new_out, moments_out = adamw(out_weight, out_grad, first_out, second_out, 0.2, 0.1, steps_done)
    new_gains, moments_gains = adamw(
        gains, gains_grad, first_gains, second_gains, 0.6, 0.0, steps_done
    )
    stays = (lax.axis_index("sl") == lax.axis_index("kl")).astype(jnp.int32)
    fixes = jnp.stack(
        [1.0 - jnp.power(beta_first, steps_done), 1.0 - jnp.power(beta_second, steps_done)]
    )
    new_gate, moments_gate = adamw_block(
        gate_weight, grad_gate_w, first_gate, second_gate, 0.02, 0.1, stays, fixes
    )
    new_up, moments_up = adamw_block(
        up_weight, grad_up_w, first_up, second_up, 0.02, 0.1, stays, fixes
    )
    new_down, moments_down = adamw_block(
        down_weight, grad_down, first_down, second_down, 0.013, 0.1, stays, fixes
    )
    return (
        block_out,
        grad_input,
        new_qkv,
        moments_qkv,
        new_out,
        moments_out,
        new_gains,
        moments_gains,
        new_gate,
        moments_gate,
        new_up,
        moments_up,
        new_down,
        moments_down,
    )


def solution(mesh):
    seqs, parts = mesh.shape["seq"], mesh.shape["kv"]
    sizes = (seqs // 2, 2, parts // 2, 2)
    fine = Mesh(mesh.devices.reshape(sizes), ALL)
    rows = P(ALL, None)
    block = P(SEQ, KV)
    return jax.shard_map(
        functools.partial(local, sizes),
        mesh=fine,
        in_specs=(
            rows, rows, P(SEQ), P(), P(),
            rows, rows, P(ALL), block, block, block,
            rows, rows, P(ALL), block, block, block,
            rows, rows, P(ALL), block, block, block,
        ),
        out_specs=(
            rows, rows,
            rows, P(None, ALL, None),
            rows, P(None, ALL, None),
            P(ALL), P(None, ALL),
            block, P(None, SEQ, KV),
            block, P(None, SEQ, KV),
            block, P(None, SEQ, KV),
        ),
        check_vma=False,
    )
```

```python
import functools

import jax
import jax.numpy as jnp
import numpy as np
from jax import lax
from jax.experimental import pallas as pl
from jax.experimental.pallas import tpu as pltpu
from jax.sharding import Mesh, PartitionSpec as P

QUERY_HEADS = 20
VALUE_GROUPS = 5
HEAD_SIZE = 64

eps_norm = 1e-06
masked_value = -1e30
beta_first = 0.9
beta_second = 0.95
adam_eps = 1e-08

ALL = ("sh", "sl", "kh", "kl")
SEQ = ("sh", "sl")
KV = ("kh", "kl")
OWNERS = ("sh", "kl")
VMEM_LIMIT = 40 * 1024 * 1024
GAIN_ROWS = 8


def rms_scale(value_rows):
    return lax.rsqrt(jnp.mean(value_rows * value_rows, -1, keepdims=True) + eps_norm)


def norm_back(grad_out, value_rows, scale, gain):
    shaped = value_rows * scale
    pushed = grad_out * gain
    grad_in = scale * (pushed - shaped * jnp.mean(pushed * shaped, -1, keepdims=True))
    return (grad_in, grad_out * shaped)


def angle_tables(item_count):
    places = np.arange(item_count).astype(np.float32)
    steps = np.arange(HEAD_SIZE // 2).astype(np.float32) * np.float32(2.0) / np.float32(HEAD_SIZE)
    freqs = np.float32(10000.0) ** (-steps)
    angles = freqs[:, None].astype(np.float32) * places[None, :]
    return (np.cos(angles).astype(np.float32), np.sin(angles).astype(np.float32))


def contract(left, right, left_dim, right_dim):
    return lax.dot_general(
        left,
        right,
        (((left_dim,), (right_dim,)), ((), ())),
        preferred_element_type=jnp.float32,
    )


def head_scale(rows):
    return lax.rsqrt(jnp.mean(rows * rows, 0, keepdims=True) + eps_norm)


def rotated(rows, scale, gain, cosine, sine):
    half = HEAD_SIZE // 2
    shaped = rows * scale * gain
    first, second = shaped[:half], shaped[half:]
    return jnp.concatenate(
        [first * cosine - second * sine, second * cosine + first * sine], axis=0
    )


def unrotated_norm_back(grad, rows, scale, gain, cosine, sine):
    half = HEAD_SIZE // 2
    first, second = grad[:half], grad[half:]
    turned = jnp.concatenate(
        [first * cosine + second * sine, second * cosine - first * sine], axis=0
    )
    shaped = rows * scale
    pushed = turned * gain
    grad_in = scale * (pushed - shaped * jnp.mean(pushed * shaped, 0, keepdims=True))
    return (grad_in, turned * shaped)


def causal(block):
    keys = lax.broadcasted_iota(jnp.int32, (block, block), 0)
    places = lax.broadcasted_iota(jnp.int32, (block, block), 1)
    return keys <= places


def forward_kernel(
    group_ref, qp_ref, kp_ref, vp_ref, cos_ref, sin_ref, gq_ref, gk_ref,
    q_ref, k_ref, v_ref, out_ref, lse_ref, *, block,
):
    cosine, sine = cos_ref[...], sin_ref[...]
    qp, kp = qp_ref[...], kp_ref[...]
    query = (rotated(qp, head_scale(qp), gq_ref[...], cosine, sine) * 0.125).astype(jnp.bfloat16)
    key = rotated(kp, head_scale(kp), gk_ref[...], cosine, sine).astype(jnp.bfloat16)
    value = vp_ref[...].astype(jnp.bfloat16)
    q_ref[0] = query
    k_ref[0] = key
    v_ref[0] = value
    allowed = causal(block)
    for index in range(query.shape[1] // block):
        start, stop = index * block, (index + 1) * block
        part = query[:, start:stop]
        near = contract(key[:, start:stop], part, 0, 0)
        near = jnp.where(allowed, near, masked_value)
        top = jnp.max(near, 0, keepdims=True)
        if index:
            far = contract(key[:, :start], part, 0, 0)
            top = jnp.maximum(top, jnp.max(far, 0, keepdims=True))
        near = jnp.exp(near - top)
        total = jnp.sum(near, 0, keepdims=True)
        if index:
            far = jnp.exp(far - top)
            total = total + jnp.sum(far, 0, keepdims=True)
        share = 1.0 / total
        result = contract(value[:, start:stop], (near * share).astype(jnp.bfloat16), 1, 0)
        if index:
            result = result + contract(value[:, :start], (far * share).astype(jnp.bfloat16), 1, 0)
        out_ref[index] = result.astype(jnp.bfloat16)
        lse_ref[0, :, start:stop] = top + jnp.log(total)


def backward_kernel(
    group_ref, qp_ref, kp_ref, q_ref, k_ref, v_ref, do_ref, lse_ref, cos_ref, sin_ref,
    gq_ref, gk_ref,
    gqp_ref, gkp_ref, gv_ref, gain_q_ref, gain_k_ref,
    dq_ref, dk_ref, dv_ref, sum_q_ref, sum_k_ref, *, block,
):
    head = pl.program_id(0)
    heads = pl.num_programs(0)
    group = group_ref[head]
    opens = jnp.logical_or(head == 0, group_ref[jnp.maximum(head - 1, 0)] != group)
    closes = jnp.logical_or(
        head == heads - 1, group_ref[jnp.minimum(head + 1, heads - 1)] != group
    )

    @pl.when(head == 0)
    def _():
        sum_q_ref[...] = jnp.zeros_like(sum_q_ref)
        sum_k_ref[...] = jnp.zeros_like(sum_k_ref)

    @pl.when(opens)
    def _():
        dk_ref[...] = jnp.zeros_like(dk_ref)
        dv_ref[...] = jnp.zeros_like(dv_ref)

    query, key, value = q_ref[0], k_ref[0], v_ref[0]
    allowed = causal(block)
    for index in range(query.shape[1] // block):
        start, stop = index * block, (index + 1) * block
        part, grad_part = query[:, start:stop], do_ref[index]
        sums_log = lse_ref[0, :, start:stop]
        near = jnp.exp(contract(key[:, start:stop], part, 0, 0) - sums_log)
        near = jnp.where(allowed, near, 0.0)
        grad_near = contract(value[:, start:stop], grad_part, 0, 0)
        inner = jnp.sum(near * grad_near, 0, keepdims=True)
        if index:
            far = jnp.exp(contract(key[:, :start], part, 0, 0) - sums_log)
            grad_far = contract(value[:, :start], grad_part, 0, 0)
            inner = inner + jnp.sum(far * grad_far, 0, keepdims=True)
        step = (near * (grad_near - inner)).astype(jnp.bfloat16)
        total = contract(key[:, start:stop], step, 1, 0)
        dk_ref[:, start:stop] += contract(part, step, 1, 1)
        dv_ref[:, start:stop] += contract(grad_part, near.astype(jnp.bfloat16), 1, 1)
        if index:
            step = (far * (grad_far - inner)).astype(jnp.bfloat16)
            total = total + contract(key[:, :start], step, 1, 0)
            dk_ref[:, :start] += contract(part, step, 1, 1)
            dv_ref[:, :start] += contract(grad_part, far.astype(jnp.bfloat16), 1, 1)
        dq_ref[:, start:stop] = total * 0.125

    cosine, sine = cos_ref[...], sin_ref[...]
    qp = qp_ref[...]
    grad_qp, gain_terms = unrotated_norm_back(
        dq_ref[...].astype(jnp.bfloat16).astype(jnp.float32),
        qp, head_scale(qp), gq_ref[...], cosine, sine,
    )
    gqp_ref[...] = grad_qp.astype(jnp.bfloat16)
    sum_q_ref[...] += gain_terms

    @pl.when(closes)
    def _():
        kp = kp_ref[...]
        grad_kp, terms = unrotated_norm_back(
            dk_ref[...].astype(jnp.bfloat16).astype(jnp.float32),
            kp, head_scale(kp), gk_ref[...], cosine, sine,
        )
        gkp_ref[0] = grad_kp.astype(jnp.bfloat16)
        gv_ref[0] = dv_ref[...].astype(jnp.bfloat16)
        sum_k_ref[...] += terms

    @pl.when(head == heads - 1)
    def _():
        gain_q_ref[...] = jnp.sum(sum_q_ref[...], 1, keepdims=True)
        gain_k_ref[...] = jnp.sum(sum_k_ref[...], 1, keepdims=True)


def attention_specs(length, heads, block):
    half = HEAD_SIZE // 2
    tall = (HEAD_SIZE, length)
    whole = lambda shape: pl.BlockSpec(shape, lambda h, g: (0, 0))
    per_head = pl.BlockSpec((1,) + tall, lambda h, g: (h, 0, 0))
    per_group = pl.BlockSpec((1,) + tall, lambda h, g: (g[h], 0, 0))
    per_row = pl.BlockSpec((1, 1, length), lambda h, g: (h, 0, 0))
    query = pl.BlockSpec(tall, lambda h, g: (h, 0))
    key = pl.BlockSpec(tall, lambda h, g: (heads + g[h], 0))
    value = pl.BlockSpec(tall, lambda h, g: (heads + 2 + g[h], 0))
    table = whole((half, length))
    gain = whole((HEAD_SIZE, 1))
    per_owner = pl.BlockSpec((length // block, HEAD_SIZE, block), lambda h, g: (0, h, 0))
    return (query, key, value, per_head, per_group, per_row, table, gain, per_owner)


def attend(groups, mixed, cosine, sine, gain_q, gain_k, heads, block):
    length = mixed.shape[1]
    query, key, value, per_head, per_group, per_row, table, gain, per_owner = attention_specs(
        length, heads, block
    )
    per = lambda count: jax.ShapeDtypeStruct((count, HEAD_SIZE, length), jnp.bfloat16)
    scores = heads * length * length // 2
    return pl.pallas_call(
        functools.partial(forward_kernel, block=block),
        name="attention_forward",
        out_shape=(
            per(heads), per(2), per(2),
            jax.ShapeDtypeStruct((length // block, heads * HEAD_SIZE, block), jnp.bfloat16),
            jax.ShapeDtypeStruct((heads, 1, length), jnp.float32),
        ),
        grid_spec=pltpu.PrefetchScalarGridSpec(
            num_scalar_prefetch=1,
            grid=(heads,),
            in_specs=[query, key, value, table, table, gain, gain],
            out_specs=[per_head, per_group, per_group, per_owner, per_row],
        ),
        compiler_params=pltpu.CompilerParams(
            dimension_semantics=("arbitrary",), vmem_limit_bytes=VMEM_LIMIT
        ),
        cost_estimate=pl.CostEstimate(
            flops=scores * 4 * HEAD_SIZE, transcendentals=scores, bytes_accessed=8_000_000
        ),
    )(groups, mixed, mixed, mixed, cosine, sine, gain_q, gain_k)


def attend_back(
    groups, mixed, query_rows, key_rows, value_rows, grads, lse, cosine, sine, gain_q, gain_k, heads, block
):
    length = mixed.shape[1]
    query, key, value, per_head, per_group, per_row, table, gain, per_owner = attention_specs(
        length, heads, block
    )
    tall = (HEAD_SIZE, length)
    scores = heads * length * length // 2
    return pl.pallas_call(
        functools.partial(backward_kernel, block=block),
        name="attention_backward",
        out_shape=(
            jax.ShapeDtypeStruct((heads * HEAD_SIZE, length), jnp.bfloat16),
            jax.ShapeDtypeStruct((2,) + tall, jnp.bfloat16),
            jax.ShapeDtypeStruct((2,) + tall, jnp.bfloat16),
            jax.ShapeDtypeStruct((HEAD_SIZE, 1), jnp.float32),
            jax.ShapeDtypeStruct((HEAD_SIZE, 1), jnp.float32),
        ),
        grid_spec=pltpu.PrefetchScalarGridSpec(
            num_scalar_prefetch=1,
            grid=(heads,),
            in_specs=[
                query, key, per_head, per_group, per_group, per_owner, per_row, table, table, gain, gain,
            ],
            out_specs=[query, per_group, per_group, gain, gain],
            scratch_shapes=[pltpu.VMEM(tall, jnp.float32)] * 5,
        ),
        compiler_params=pltpu.CompilerParams(
            dimension_semantics=("arbitrary",), vmem_limit_bytes=VMEM_LIMIT
        ),
        cost_estimate=pl.CostEstimate(
            flops=scores * 10 * HEAD_SIZE, transcendentals=scores, bytes_accessed=10_000_000
        ),
    )(groups, mixed, mixed, query_rows, key_rows, value_rows, grads, lse, cosine, sine, gain_q, gain_k)


def row_order_kernel(mine_ref, in_ref, out_ref, *, offsets, back):
    for index, offset in enumerate(offsets):
        held = mine_ref[0] ^ offset
        if back:
            out_ref[held] = in_ref[index]
        else:
            out_ref[index] = in_ref[held]


def column_order_kernel(mine_ref, in_ref, out_ref, *, lines, parts, back):
    width = in_ref.shape[1] // (2 * lines)
    small = width // parts
    for plane in range(2):
        for line in range(lines):
            held = pl.multiple_of((mine_ref[0] ^ (line * 2 + plane)) * width, width)
            places = [(plane * parts + part) * lines + line for part in range(parts)]
            if back:
                out_ref[:, pl.ds(held, width)] = jnp.concatenate(
                    [in_ref[:, at * small : (at + 1) * small] for at in places], axis=1
                )
            else:
                block = in_ref[:, pl.ds(held, width)]
                for part, at in enumerate(places):
                    out_ref[:, at * small : (at + 1) * small] = block[
                        :, part * small : (part + 1) * small
                    ]


def order_call(kernel, array, mine):
    return pl.pallas_call(
        kernel,
        name="block_order",
        out_shape=jax.ShapeDtypeStruct(array.shape, array.dtype),
        in_specs=[
            pl.BlockSpec(memory_space=pltpu.SMEM),
            pl.BlockSpec(memory_space=pltpu.VMEM),
        ],
        out_specs=pl.BlockSpec(memory_space=pltpu.VMEM),
        compiler_params=pltpu.CompilerParams(vmem_limit_bytes=VMEM_LIMIT),
        cost_estimate=pl.CostEstimate(
            flops=0, transcendentals=0, bytes_accessed=4 * array.size
        ),
    )(mine.reshape(1).astype(jnp.int32), array)


def column_order(array, mine, lines, parts, back=False):
    rows, columns = array.shape
    width = columns // (2 * lines)
    if width % 128 == 0:
        kernel = functools.partial(column_order_kernel, lines=lines, parts=parts, back=back)
        return order_call(kernel, array, mine)
    small = width // parts
    if back:
        array = array.reshape(rows, 2, parts, lines, small).transpose(0, 3, 1, 2, 4)
        return jnp.where(mine == 0, array, array[:, :, ::-1]).reshape(rows, columns)
    array = array.reshape(rows, lines, 2, parts, small)
    array = jnp.where(mine == 0, array, array[:, :, ::-1])
    return array.transpose(0, 2, 3, 1, 4).reshape(rows, columns)


def head_columns(part, width):
    keys_at = QUERY_HEADS * HEAD_SIZE + part * HEAD_SIZE
    values_at = keys_at + VALUE_GROUPS * HEAD_SIZE
    pair = 2 * HEAD_SIZE
    return ((part * width, 0, width), (keys_at, width, pair), (values_at, width + pair, pair))


def split_kernel(in_ref, qkv_ref, out_ref, gain_ref, *, width):
    parts, lines, rows, _ = qkv_ref.shape
    for line in range(lines):
        for part in range(parts):
            for source, target, count in head_columns(part, width):
                qkv_ref[part, line, :, target : target + count] = in_ref[
                    line, :rows, source : source + count
                ]
        out_ref[line] = in_ref[line, rows:, :]
        gain_ref[line] = in_ref[line, : gain_ref.shape[1], in_ref.shape[2] - gain_ref.shape[2] :]


def split_columns(both, parts, rows, width, gain_width):
    lines, total, model = both.shape
    span = width + 4 * HEAD_SIZE
    return pl.pallas_call(
        functools.partial(split_kernel, width=width),
        name="split_columns",
        out_shape=(
            jax.ShapeDtypeStruct((parts, lines, rows, span), both.dtype),
            jax.ShapeDtypeStruct((lines, total - rows, model), both.dtype),
            jax.ShapeDtypeStruct((lines, min(GAIN_ROWS, rows), gain_width), both.dtype),
        ),
        compiler_params=pltpu.CompilerParams(vmem_limit_bytes=VMEM_LIMIT),
        cost_estimate=pl.CostEstimate(
            flops=0, transcendentals=0, bytes_accessed=4 * both.size
        ),
    )(both)


def join_kernel(in_ref, qkv_ref, *, width):
    parts, lines, _, _ = in_ref.shape
    for line in range(lines):
        for part in range(parts):
            qkv_ref[line, :, part * width : (part + 1) * width] = in_ref[part, line, :, :width]
        for kind in range(2):
            for group in range(VALUE_GROUPS):
                terms = []
                for part in range(max(group - 1, 0), min(group + 1, parts)):
                    at = width + (2 * kind + group - part) * HEAD_SIZE
                    terms.append(in_ref[part, line, :, at : at + HEAD_SIZE].astype(jnp.float32))
                at = (QUERY_HEADS + kind * VALUE_GROUPS + group) * HEAD_SIZE
                qkv_ref[line, :, at : at + HEAD_SIZE] = sum(terms).astype(qkv_ref.dtype)


def join_columns(qkv_parts, width):
    _, lines, rows, _ = qkv_parts.shape
    shape = (lines, rows, (QUERY_HEADS + 2 * VALUE_GROUPS) * HEAD_SIZE)
    return pl.pallas_call(
        functools.partial(join_kernel, width=width),
        name="join_columns",
        out_shape=jax.ShapeDtypeStruct(shape, jnp.bfloat16),
        compiler_params=pltpu.CompilerParams(vmem_limit_bytes=VMEM_LIMIT),
        cost_estimate=pl.CostEstimate(
            flops=0, transcendentals=0, bytes_accessed=4 * int(np.prod(shape))
        ),
    )(qkv_parts)


def adamw_kernel(
    stays_ref, fixes_ref, weight_ref, own_ref, moved_ref, first_ref, second_ref, new_ref, moments_ref,
    *, rate, shrink,
):
    high = jnp.float32
    grad = jnp.where(stays_ref[0] == 1, own_ref[...].astype(high), moved_ref[...].astype(high))
    first_new = beta_first * first_ref[...] + (1.0 - beta_first) * grad
    second_new = beta_second * second_ref[...] + (1.0 - beta_second) * grad * grad
    stepped = first_new / fixes_ref[0] / (jnp.sqrt(second_new / fixes_ref[1]) + adam_eps)
    weight = weight_ref[...]
    new_ref[...] = weight - rate * (stepped + shrink * weight)
    moments_ref[0] = first_new
    moments_ref[1] = jnp.sqrt(second_new)


def adamw_block(weight, grads, first, second, rate, shrink, stays, fixes):
    rows, columns = weight.shape
    tile = 64 if rows % 64 == 0 else rows
    block = pl.BlockSpec((tile, columns), lambda i: (i, 0))
    scalar = pl.BlockSpec(memory_space=pltpu.SMEM)
    return pl.pallas_call(
        functools.partial(adamw_kernel, rate=rate, shrink=shrink),
        name="adamw",
        out_shape=(
            jax.ShapeDtypeStruct(weight.shape, weight.dtype),
            jax.ShapeDtypeStruct((2,) + weight.shape, weight.dtype),
        ),
        grid=(rows // tile,),
        in_specs=[scalar, scalar] + [block] * 5,
        out_specs=(block, pl.BlockSpec((2, tile, columns), lambda i: (0, i, 0))),
        compiler_params=pltpu.CompilerParams(vmem_limit_bytes=VMEM_LIMIT),
        cost_estimate=pl.CostEstimate(
            flops=20 * weight.size, transcendentals=2 * weight.size, bytes_accessed=28 * weight.size
        ),
    )(stays.reshape(1), fixes, weight, grads[0], grads[1], first, second)


def adamw(weight, grad, first, second, rate, shrink, item_count):
    first_new = beta_first * first + (1.0 - beta_first) * grad
    second_new = beta_second * second + (1.0 - beta_second) * grad * grad
    fix_first = 1.0 - jnp.power(beta_first, item_count)
    fix_second = 1.0 - jnp.power(beta_second, item_count)
    stepped = first_new / fix_first / (jnp.sqrt(second_new / fix_second) + adam_eps)
    return (
        weight - rate * (stepped + shrink * weight),
        jnp.stack([first_new, jnp.sqrt(second_new)]),
    )


def local(
    sizes,
    tokens,
    cotangent,
    corpus_id,
    corpus_weight,
    step_count,
    qkv_weight,
    out_weight,
    gains,
    gate_weight,
    up_weight,
    down_weight,
    first_qkv,
    first_out,
    first_gains,
    first_gate,
    first_up,
    first_down,
    second_qkv,
    second_out,
    second_gains,
    second_gate,
    second_up,
    second_down,
):
    low = jnp.bfloat16
    high = jnp.float32
    devices = int(np.prod(sizes))
    seqs = sizes[0] * sizes[1]
    parts = sizes[2] * sizes[3]
    places = np.arange(devices).reshape(sizes)
    where = np.stack(np.unravel_index(np.arange(devices), sizes), -1)

    def permute(array, target):
        pairs = [(int(i), int(places[tuple(target(*where[i]))])) for i in range(devices)]
        return lax.ppermute(array, ALL, [pair for pair in pairs if pair[0] != pair[1]])

    def swap(array):
        moved = permute(array, lambda sh, sl, kh, kl: (sh, kl, kh, sl))
        return jnp.where(lax.axis_index("sl") == lax.axis_index("kl"), array, moved)

    def in_ffn_group(array, r):
        return permute(array, lambda sh, sl, kh, kl: (sh, sl ^ (r & 1), kh ^ (r >> 1), kl))

    def in_sequence(array, r):
        return permute(array, lambda sh, sl, kh, kl: (sh, sl, kh ^ (r >> 1), kl ^ (r & 1)))

    def along_y(array):
        return permute(array, lambda sh, sl, kh, kl: (sh, sl ^ 1, kh, kl))

    z_size = sizes[0]

    def halve(blocks, index, axis, move):
        kept = lax.dynamic_index_in_dim(blocks, index, axis, keepdims=False)
        sent = lax.dynamic_index_in_dim(blocks, index ^ 1, axis, keepdims=False)
        return (kept.astype(high) + move(sent).astype(high)).astype(low)

    item_count, model = tokens.shape
    heads = QUERY_HEADS // parts
    width = heads * HEAD_SIZE
    pair = 2 * HEAD_SIZE
    keys_at = QUERY_HEADS * HEAD_SIZE
    values_at = keys_at + VALUE_GROUPS * HEAD_SIZE
    kv = lax.axis_index(KV)
    length = item_count * parts
    cosine, sine = angle_tables(length)
    groups = ((jnp.arange(heads, dtype=jnp.int32) + kv) // 4).astype(jnp.int32)

    def stage(ready, waiting):
        return lax.optimization_barrier((ready, waiting))

    row_offsets = [
        (z * 2 + rs) * parts + r1 * 2 + r0
        for r0 in range(2) for r1 in range(2) for rs in range(2) for z in range(z_size)
    ]

    def columns_moved(array, back=False):
        return column_order(array, lax.axis_index("sl"), z_size, parts, back=back)

    def rows_moved(array, back=False):
        blocks = array.reshape(devices, -1, item_count)
        kernel = functools.partial(row_order_kernel, offsets=tuple(row_offsets), back=back)
        mine = lax.axis_index("sl") * parts + kv
        return order_call(kernel, blocks, mine).reshape(-1, item_count)

    span = width + 2 * pair
    own_rows, total_columns = qkv_weight.shape
    spare = model - total_columns
    gain_rows = -(-gains.shape[0] // spare)
    gains_block = jnp.pad(gains.astype(low), (0, own_rows * spare - gains.shape[0]))
    both = jnp.concatenate(
        [
            jnp.concatenate([qkv_weight.astype(low), gains_block.reshape(own_rows, spare)], axis=1),
            out_weight.astype(low),
        ]
    )
    both_line = lax.all_to_all(
        jnp.broadcast_to(both[None], (z_size,) + both.shape), "sh", split_axis=0, concat_axis=0, tiled=True
    )
    tokens_near = columns_moved(tokens)
    tokens_far = in_sequence(tokens_near, 2)
    gate_block = swap(gate_weight.astype(low))
    factor = jnp.sum(
        jnp.where(jnp.arange(corpus_weight.shape[0]) == corpus_id[0], corpus_weight, 0.0)
    )
    weighted = cotangent.astype(high) * factor
    weighted_low = weighted.astype(low)
    weighted_one = in_ffn_group(weighted_low, 1)
    (both_line, tokens_far, gate_block, weighted_one), (up_low, tokens_near, weighted_low) = stage(
        (both_line, tokens_far, gate_block, weighted_one),
        (up_weight.astype(low), tokens_near, weighted_low),
    )
    gate_full = lax.all_gather(gate_block, OWNERS, axis=0, tiled=True)

    qkv_parts, out_line, gain_line = split_columns(both_line, parts, own_rows, width, spare)
    gain_line = gain_line[:, :gain_rows].reshape(z_size, -1)
    gain_pairs = jnp.stack([gain_line, in_sequence(gain_line, 1)])
    gain_pairs = jnp.stack([gain_pairs, in_sequence(gain_pairs, 2)])
    qkv_rows = lax.all_to_all(
        qkv_parts, KV, split_axis=0, concat_axis=0, tiled=True
    )
    tokens_pair = (in_sequence(tokens_near, 1), in_sequence(tokens_far, 1))
    up_block = swap(up_low)
    out_near = jnp.stack([out_line, along_y(out_line)])
    (qkv_rows, tokens_pair, gain_pairs, up_block, out_near), (down_low, own_cotangent) = stage(
        (qkv_rows, tokens_pair, gain_pairs, up_block, out_near), (down_weight.astype(low), cotangent)
    )
    up_full = lax.all_gather(up_block, OWNERS, axis=0, tiled=True)

    qkv_far = along_y(qkv_rows)
    cotangent_far, out_near = stage(in_ffn_group(own_cotangent, 2), out_near)
    weighted_far = (cotangent_far.astype(high) * factor).astype(low)
    out_far = in_sequence(out_near, 2)
    held = jnp.arange(2 * parts)
    mine = lax.axis_index("sl") * parts + kv
    selection = held[:, None] == (held[None, :] ^ mine)
    gain_blocks = jnp.stack([gain_pairs, along_y(gain_pairs)])[..., : gains.shape[0]]
    gain_values = contract(selection.astype(low), gain_blocks.reshape(2 * parts, -1), 1, 0)
    gain_values = gain_values.reshape(2, parts, z_size, -1).transpose(2, 0, 1, 3).reshape(-1)
    gain_one = gain_values[:model]
    gain_two = gain_values[model : 2 * model]
    gain_q = gain_values[2 * model : 2 * model + HEAD_SIZE].reshape(HEAD_SIZE, 1)
    gain_k = gain_values[2 * model + HEAD_SIZE :].reshape(HEAD_SIZE, 1)
    gain_moved = columns_moved(jnp.broadcast_to(gain_one[None], (8, model)))[:1]
    all_rows = jnp.zeros((parts, item_count, model), low)
    for r, piece in enumerate((tokens_near, tokens_pair[0], tokens_far, tokens_pair[1])):
        all_rows = lax.dynamic_update_slice_in_dim(all_rows, piece[None], kv ^ r, 0)
    all_rows = all_rows.reshape(length, model).astype(high)
    normed = (all_rows * rms_scale(all_rows) * gain_moved).astype(low)
    normed, qkv_rows = stage(normed, qkv_rows)
    qkv_full = jnp.concatenate([qkv_rows, qkv_far]).reshape(model, span)

    mixed = contract(qkv_full, normed, 0, 1)
    query_rows, key_rows, value_rows, outgoing, lse = attend(
        groups, mixed, cosine, sine, gain_q, gain_k, heads, item_count
    )
    weighted_two = in_ffn_group(weighted_far, 1)
    (outgoing, weighted_two), (out_near, down_low) = stage((outgoing, weighted_two), (out_near, down_low))
    weighted_rows = (jnp.concatenate([weighted_low, weighted_one, weighted_far]), weighted_two)

    down_block = swap(down_low)
    attended = rows_moved(
        lax.all_to_all(outgoing, KV, split_axis=0, concat_axis=0, tiled=True)
    )
    out_full = (out_near, out_far, in_sequence(out_near, 1), in_sequence(out_far, 1))
    out_full = [piece.reshape(-1, model) for piece in out_full]
    (attended, out_full), down_block = stage((attended, out_full), down_block)
    attended = attended.reshape(4, -1, item_count)
    down_full = lax.all_gather(down_block, OWNERS, axis=0, tiled=True)
    inputs = tokens.astype(high)
    hidden = inputs + sum(contract(attended[i], out_full[i], 0, 0) for i in range(4))

    scale_two = rms_scale(hidden)
    normed_two = (hidden * scale_two * gain_two).astype(low)
    ffn_moved = [in_ffn_group(normed_two, r) for r in (3, 1, 2)]
    ffn_rows = (jnp.concatenate([normed_two, ffn_moved[1], ffn_moved[2]]), ffn_moved[0])

    def activation(rows, gate_full, up_full):
        gate = contract(rows, gate_full, 1, 0)
        up_part = contract(rows, up_full, 1, 0)
        sigma = jax.nn.sigmoid(gate)
        return (gate, up_part, sigma, (gate * sigma * up_part).astype(low))

    def activation_back(rows, down_full, gate, up_part, sigma):
        grad_acted = contract(rows, down_full, 1, 0)
        grad_gate = (grad_acted * up_part * sigma * (1.0 + gate * (1.0 - sigma))).astype(low)
        return (grad_gate, (grad_acted * (gate * sigma)).astype(low))

    def weight_gradient(left, right):
        return sum(contract(left[i], right[i], 0, 0) for i in range(2)).astype(low)

    def share(grad):
        return lax.psum_scatter(grad, OWNERS, scatter_dimension=0, tiled=True)

    near = activation(ffn_rows[0], gate_full, up_full)
    near, (gate_full, up_full) = stage(near, (gate_full, up_full))
    far = activation(ffn_rows[1], gate_full, up_full)
    acted = (near[3], far[3])
    grad_down_low = weight_gradient(weighted_rows, acted)
    down_full, grad_down_low = stage(down_full, grad_down_low)
    grad_down_share = share(grad_down_low)
    far_gate, far_up = activation_back(weighted_rows[1], down_full, *far[:3])
    sent_far = (contract(far_gate, gate_full, 1, 1) + contract(far_up, up_full, 1, 1)).astype(low)
    sent_far, weighted_near = stage(sent_far, weighted_rows[0])
    received_far = in_ffn_group(sent_far, 3)
    near_gate, near_up = activation_back(weighted_near, down_full, *near[:3])
    rows_partial = (contract(near_gate, gate_full, 1, 1) + contract(near_up, up_full, 1, 1)).astype(low)
    received = [
        in_ffn_group(rows_partial[r * item_count : (r + 1) * item_count], r) for r in (1, 2)
    ]
    grad_gate, grad_up = (near_gate, far_gate), (near_up, far_up)
    (received_far, rows_partial), (grad_gate, grad_up) = stage(
        (received_far, rows_partial), (grad_gate, grad_up)
    )
    grad_gate_share = share(weight_gradient(ffn_rows, grad_gate))
    grad_up_low = weight_gradient(ffn_rows, grad_up)
    ffn_partial = [contract(part, down_full, 1, 1).astype(low) for part in acted]
    (received, grad_down_share), (grad_up_low, ffn_partial) = stage(
        (received, grad_down_share), (grad_up_low, ffn_partial)
    )
    received = received + [received_far]
    grad_up_share = share(grad_up_low)
    grad_normed_two = rows_partial[:item_count].astype(high) + sum(
        piece.astype(high) for piece in received
    )

    pushed_two, gain_two_terms = norm_back(grad_normed_two, hidden, scale_two, gain_two)
    grad_hidden = weighted + pushed_two
    hidden_low = grad_hidden.astype(low)

    attended_gradient = jnp.concatenate(
        [contract(piece, hidden_low, 1, 1).astype(low) for piece in out_full]
    )
    attended_gradient = rows_moved(attended_gradient, back=True)
    incoming = lax.all_to_all(
        attended_gradient.reshape(parts, width, item_count), KV, split_axis=0, concat_axis=0, tiled=True
    )
    ffn_blocks = ffn_partial[0].reshape(3, item_count, model)
    ffn_moved = [in_ffn_group(ffn_blocks[1], 1), in_ffn_group(ffn_partial[1], 1)]
    sent_out = [
        contract(attended[2 + r], hidden_low, 1, 0).astype(low) for r in range(2)
    ]
    kept_out = [
        contract(attended[r], hidden_low, 1, 0) for r in range(2)
    ]
    out_line = [
        (kept_out[r] + in_sequence(sent_out[r], 1).astype(high)).astype(low) for r in range(2)
    ]
    incoming, out_line = lax.optimization_barrier((incoming, out_line))

    out_moved = in_sequence(out_line[1], 2)
    grad_queries, grad_keys, grad_values, gain_q_sum, gain_k_sum = attend_back(
        groups, mixed, query_rows, key_rows, value_rows, incoming, lse,
        cosine, sine, gain_q, gain_k, heads, item_count,
    )
    grad_mixed = jnp.concatenate(
        [grad_queries, grad_keys.reshape(pair, length), grad_values.reshape(pair, length)], axis=0
    )
    half_model = model // 2
    grad_mixed, (ffn_moved, grad_gate_share) = stage(grad_mixed, (ffn_moved, grad_gate_share))
    mixer_sent = contract(normed[:, half_model:], grad_mixed, 0, 1).astype(low)
    (mixer_sent, grad_mixed), (out_line, ffn_blocks) = stage(
        (mixer_sent, grad_mixed), (out_line[0], ffn_blocks)
    )

    mixer_moved = along_y(mixer_sent)
    mixer_line = contract(normed[:, :half_model], grad_mixed, 0, 1)
    grad_normed = contract(grad_mixed, qkv_full, 0, 1).astype(low)
    grad_normed = grad_normed.reshape(2, 2, item_count, model)
    core = lax.axis_index("kl")
    normed_moved = in_sequence(lax.dynamic_index_in_dim(grad_normed, core ^ 1, 1, keepdims=False), 1)
    ffn_line = [
        ffn_blocks[2 * r].astype(high) + ffn_moved[r].astype(high) for r in range(2)
    ]
    mixer_line = lax.optimization_barrier(mixer_line)
    mixer_parts = (mixer_line + mixer_moved.astype(high)).astype(low)
    mixer_parts, (out_line, shares) = stage(
        mixer_parts, (out_line, (grad_down_share, grad_gate_share))
    )
    swapped = [permute(piece, lambda sh, sl, kh, kl: (sh, kl, kh, sl)) for piece in shares]
    ffn_moved = in_ffn_group(ffn_line[1].astype(low), 2)
    swapped, ffn_moved = stage(swapped, ffn_moved)

    mixer_parts = lax.all_to_all(
        mixer_parts.reshape(parts, z_size, -1, span), KV, split_axis=0, concat_axis=0, tiled=True
    )
    out_line = (out_line.astype(high) + out_moved.astype(high)).astype(low).reshape(2, z_size, -1, model)
    out_moved = along_y(out_line[1])
    qkv_line = join_columns(mixer_parts, width)
    qkv_line, (grad_normed, normed_moved, out_line, grad_up_share) = stage(
        qkv_line, (grad_normed, normed_moved, out_line[0], grad_up_share)
    )

    qkv_line = lax.all_to_all(qkv_line, "sh", split_axis=0, concat_axis=0, tiled=True)
    grad_normed = lax.dynamic_index_in_dim(grad_normed, core, 1, keepdims=False).astype(high)
    grad_normed = (grad_normed + normed_moved.astype(high)).astype(low)
    grad_normed = halve(grad_normed, lax.axis_index("kh"), 0, lambda v: in_sequence(v, 2)).astype(high)
    steps_done = step_count[0].astype(high)
    fixes = jnp.stack(
        [1.0 - jnp.power(beta_first, steps_done), 1.0 - jnp.power(beta_second, steps_done)]
    )
    grad_normed, fixes = stage(grad_normed, fixes)
    line = lax.axis_index("sh")

    def sum_line(blocks):
        total = lax.dynamic_index_in_dim(blocks, line, 0, keepdims=False).astype(high)
        for r in range(1, z_size):
            sent = lax.dynamic_index_in_dim(blocks, line ^ r, 0, keepdims=False)
            total = total + permute(sent, lambda sh, sl, kh, kl: (sh ^ r, sl, kh, kl)).astype(high)
        return total

    out_grad = sum_line((out_line.astype(high) + out_moved.astype(high)).astype(low))
    block_out = (hidden + (ffn_line[0] + ffn_moved.astype(high))).astype(low)
    qkv_grad = jnp.sum(qkv_line.astype(high), 0)
    grad_down, grad_gate_w = zip(shares, swapped)
    grad_up_w = (grad_up_share, permute(grad_up_share, lambda sh, sl, kh, kl: (sh, kl, kh, sl)))
    moved_inputs = tokens_near.astype(high)
    pushed_one, gain_one_terms = norm_back(
        grad_normed, moved_inputs, rms_scale(moved_inputs), gain_moved
    )
    grad_input = grad_hidden + columns_moved(pushed_one, back=True)
    gain_one_sum = columns_moved(
        jnp.broadcast_to(jnp.sum(gain_one_terms, 0)[None], (8, model)), back=True
    )[0]
    grad_gains = jnp.concatenate(
        [
            gain_one_sum,
            jnp.sum(gain_two_terms, 0),
            gain_q_sum.reshape(-1),
            gain_k_sum.reshape(-1),
        ]
    )
    grad_gains = grad_gains.reshape(z_size, 2, parts, -1).transpose(1, 2, 0, 3)
    grad_gains = lax.dot_general(
        selection.astype(high), grad_gains.reshape(2 * parts, -1), (((1,), (0,)), ((), ())),
        precision=lax.Precision.HIGHEST, preferred_element_type=high,
    ).reshape(2, 2, 2, -1)
    grad_gains = grad_gains[0] + along_y(grad_gains[1])
    grad_gains = grad_gains[:, 0] + in_sequence(grad_gains[:, 1], 1)
    grad_gains = grad_gains[0] + in_sequence(grad_gains[1], 2)
    gains_grad = sum_line(grad_gains.reshape(z_size, -1))

    new_qkv, moments_qkv = adamw(qkv_weight, qkv_grad, first_qkv, second_qkv, 0.02, 0.1, steps_done)
    new_out, moments_out = adamw(out_weight, out_grad, first_out, second_out, 0.2, 0.1, steps_done)
    new_gains, moments_gains = adamw(
        gains, gains_grad, first_gains, second_gains, 0.6, 0.0, steps_done
    )
    stays = (lax.axis_index("sl") == lax.axis_index("kl")).astype(jnp.int32)
    new_gate, moments_gate = adamw_block(
        gate_weight, grad_gate_w, first_gate, second_gate, 0.02, 0.1, stays, fixes
    )
    new_up, moments_up = adamw_block(
        up_weight, grad_up_w, first_up, second_up, 0.02, 0.1, stays, fixes
    )
    new_down, moments_down = adamw_block(
        down_weight, grad_down, first_down, second_down, 0.013, 0.1, stays, fixes
    )
    return (
        block_out,
        grad_input,
        new_qkv,
        moments_qkv,
        new_out,
        moments_out,
        new_gains,
        moments_gains,
        new_gate,
        moments_gate,
        new_up,
        moments_up,
        new_down,
        moments_down,
    )


def solution(mesh):
    seqs, parts = mesh.shape["seq"], mesh.shape["kv"]
    sizes = (seqs // 2, 2, parts // 2, 2)
    fine = Mesh(mesh.devices.reshape(sizes), ALL)
    rows = P(ALL, None)
    block = P(SEQ, KV)
    return jax.shard_map(
        functools.partial(local, sizes),
        mesh=fine,
        in_specs=(
            rows, rows, P(SEQ), P(), P(),
            rows, rows, P(ALL), block, block, block,
            rows, rows, P(ALL), block, block, block,
            rows, rows, P(ALL), block, block, block,
        ),
        out_specs=(
            rows, rows,
            rows, P(None, ALL, None),
            rows, P(None, ALL, None),
            P(ALL), P(None, ALL),
            block, P(None, SEQ, KV),
            block, P(None, SEQ, KV),
            block, P(None, SEQ, KV),
        ),
        check_vma=False,
    )
```

```python
import functools

import jax
import jax.numpy as jnp
import numpy as np
from jax import lax
from jax.experimental import pallas as pl
from jax.experimental.pallas import tpu as pltpu
from jax.sharding import Mesh, PartitionSpec as P

QUERY_HEADS = 20
VALUE_GROUPS = 5
HEAD_SIZE = 64

eps_norm = 1e-06
masked_value = -1e30
beta_first = 0.9
beta_second = 0.95
adam_eps = 1e-08

ALL = ("sh", "sl", "kh", "kl")
SEQ = ("sh", "sl")
KV = ("kh", "kl")
OWNERS = ("sh", "kl")
VMEM_LIMIT = 40 * 1024 * 1024
GAIN_ROWS = 8


def rms_scale(value_rows):
    return lax.rsqrt(jnp.mean(value_rows * value_rows, -1, keepdims=True) + eps_norm)


def norm_back(grad_out, value_rows, scale, gain):
    shaped = value_rows * scale
    pushed = grad_out * gain
    grad_in = scale * (pushed - shaped * jnp.mean(pushed * shaped, -1, keepdims=True))
    return (grad_in, grad_out * shaped)


def angle_tables(item_count):
    places = np.arange(item_count).astype(np.float32)
    steps = np.arange(HEAD_SIZE // 2).astype(np.float32) * np.float32(2.0) / np.float32(HEAD_SIZE)
    freqs = np.float32(10000.0) ** (-steps)
    angles = freqs[:, None].astype(np.float32) * places[None, :]
    return (np.cos(angles).astype(np.float32), np.sin(angles).astype(np.float32))


def contract(left, right, left_dim, right_dim):
    return lax.dot_general(
        left,
        right,
        (((left_dim,), (right_dim,)), ((), ())),
        preferred_element_type=jnp.float32,
    )


def head_scale(rows):
    return lax.rsqrt(jnp.mean(rows * rows, 0, keepdims=True) + eps_norm)


def rotated(rows, scale, gain, cosine, sine):
    half = HEAD_SIZE // 2
    shaped = rows * scale * gain
    first, second = shaped[:half], shaped[half:]
    return jnp.concatenate(
        [first * cosine - second * sine, second * cosine + first * sine], axis=0
    )


def unrotated_norm_back(grad, rows, scale, gain, cosine, sine):
    half = HEAD_SIZE // 2
    first, second = grad[:half], grad[half:]
    turned = jnp.concatenate(
        [first * cosine + second * sine, second * cosine - first * sine], axis=0
    )
    shaped = rows * scale
    pushed = turned * gain
    grad_in = scale * (pushed - shaped * jnp.mean(pushed * shaped, 0, keepdims=True))
    return (grad_in, turned * shaped)


def causal(block):
    keys = lax.broadcasted_iota(jnp.int32, (block, block), 0)
    places = lax.broadcasted_iota(jnp.int32, (block, block), 1)
    return keys <= places


def forward_kernel(
    group_ref, qp_ref, kp_ref, vp_ref, cos_ref, sin_ref, gq_ref, gk_ref,
    q_ref, k_ref, v_ref, out_ref, lse_ref, *, block,
):
    cosine, sine = cos_ref[...], sin_ref[...]
    qp, kp = qp_ref[...], kp_ref[...]
    query = (rotated(qp, head_scale(qp), gq_ref[...], cosine, sine) * 0.125).astype(jnp.bfloat16)
    key = rotated(kp, head_scale(kp), gk_ref[...], cosine, sine).astype(jnp.bfloat16)
    value = vp_ref[...].astype(jnp.bfloat16)
    q_ref[0] = query
    k_ref[0] = key
    v_ref[0] = value
    allowed = causal(block)
    for index in range(query.shape[1] // block):
        start, stop = index * block, (index + 1) * block
        part = query[:, start:stop]
        near = contract(key[:, start:stop], part, 0, 0)
        near = jnp.where(allowed, near, masked_value)
        top = jnp.max(near, 0, keepdims=True)
        if index:
            far = contract(key[:, :start], part, 0, 0)
            top = jnp.maximum(top, jnp.max(far, 0, keepdims=True))
        near = jnp.exp(near - top)
        total = jnp.sum(near, 0, keepdims=True)
        if index:
            far = jnp.exp(far - top)
            total = total + jnp.sum(far, 0, keepdims=True)
        share = 1.0 / total
        result = contract(value[:, start:stop], (near * share).astype(jnp.bfloat16), 1, 0)
        if index:
            result = result + contract(value[:, :start], (far * share).astype(jnp.bfloat16), 1, 0)
        out_ref[index] = result.astype(jnp.bfloat16)
        lse_ref[0, :, start:stop] = top + jnp.log(total)


def backward_kernel(
    group_ref, qp_ref, kp_ref, q_ref, k_ref, v_ref, do_ref, lse_ref, cos_ref, sin_ref,
    gq_ref, gk_ref,
    gqp_ref, gkp_ref, gv_ref, gain_q_ref, gain_k_ref,
    dq_ref, dk_ref, dv_ref, sum_q_ref, sum_k_ref, *, block,
):
    head = pl.program_id(0)
    heads = pl.num_programs(0)
    group = group_ref[head]
    opens = jnp.logical_or(head == 0, group_ref[jnp.maximum(head - 1, 0)] != group)
    closes = jnp.logical_or(
        head == heads - 1, group_ref[jnp.minimum(head + 1, heads - 1)] != group
    )

    @pl.when(head == 0)
    def _():
        sum_q_ref[...] = jnp.zeros_like(sum_q_ref)
        sum_k_ref[...] = jnp.zeros_like(sum_k_ref)

    @pl.when(opens)
    def _():
        dk_ref[...] = jnp.zeros_like(dk_ref)
        dv_ref[...] = jnp.zeros_like(dv_ref)

    query, key, value = q_ref[0], k_ref[0], v_ref[0]
    allowed = causal(block)
    for index in range(query.shape[1] // block):
        start, stop = index * block, (index + 1) * block
        part, grad_part = query[:, start:stop], do_ref[index]
        sums_log = lse_ref[0, :, start:stop]
        near = jnp.exp(contract(key[:, start:stop], part, 0, 0) - sums_log)
        near = jnp.where(allowed, near, 0.0)
        grad_near = contract(value[:, start:stop], grad_part, 0, 0)
        inner = jnp.sum(near * grad_near, 0, keepdims=True)
        if index:
            far = jnp.exp(contract(key[:, :start], part, 0, 0) - sums_log)
            grad_far = contract(value[:, :start], grad_part, 0, 0)
            inner = inner + jnp.sum(far * grad_far, 0, keepdims=True)
        step = (near * (grad_near - inner)).astype(jnp.bfloat16)
        total = contract(key[:, start:stop], step, 1, 0)
        dk_ref[:, start:stop] += contract(part, step, 1, 1)
        dv_ref[:, start:stop] += contract(grad_part, near.astype(jnp.bfloat16), 1, 1)
        if index:
            step = (far * (grad_far - inner)).astype(jnp.bfloat16)
            total = total + contract(key[:, :start], step, 1, 0)
            dk_ref[:, :start] += contract(part, step, 1, 1)
            dv_ref[:, :start] += contract(grad_part, far.astype(jnp.bfloat16), 1, 1)
        dq_ref[:, start:stop] = total * 0.125

    cosine, sine = cos_ref[...], sin_ref[...]
    qp = qp_ref[...]
    grad_qp, gain_terms = unrotated_norm_back(
        dq_ref[...].astype(jnp.bfloat16).astype(jnp.float32),
        qp, head_scale(qp), gq_ref[...], cosine, sine,
    )
    gqp_ref[...] = grad_qp.astype(jnp.bfloat16)
    sum_q_ref[...] += gain_terms

    @pl.when(closes)
    def _():
        kp = kp_ref[...]
        grad_kp, terms = unrotated_norm_back(
            dk_ref[...].astype(jnp.bfloat16).astype(jnp.float32),
            kp, head_scale(kp), gk_ref[...], cosine, sine,
        )
        gkp_ref[0] = grad_kp.astype(jnp.bfloat16)
        gv_ref[0] = dv_ref[...].astype(jnp.bfloat16)
        sum_k_ref[...] += terms

    @pl.when(head == heads - 1)
    def _():
        gain_q_ref[...] = jnp.sum(sum_q_ref[...], 1, keepdims=True)
        gain_k_ref[...] = jnp.sum(sum_k_ref[...], 1, keepdims=True)


def attention_specs(length, heads, block):
    half = HEAD_SIZE // 2
    tall = (HEAD_SIZE, length)
    whole = lambda shape: pl.BlockSpec(shape, lambda h, g: (0, 0))
    per_head = pl.BlockSpec((1,) + tall, lambda h, g: (h, 0, 0))
    per_group = pl.BlockSpec((1,) + tall, lambda h, g: (g[h], 0, 0))
    per_row = pl.BlockSpec((1, 1, length), lambda h, g: (h, 0, 0))
    query = pl.BlockSpec(tall, lambda h, g: (h, 0))
    key = pl.BlockSpec(tall, lambda h, g: (heads + g[h], 0))
    value = pl.BlockSpec(tall, lambda h, g: (heads + 2 + g[h], 0))
    table = whole((half, length))
    gain = whole((HEAD_SIZE, 1))
    per_owner = pl.BlockSpec((length // block, HEAD_SIZE, block), lambda h, g: (0, h, 0))
    return (query, key, value, per_head, per_group, per_row, table, gain, per_owner)


def attend(groups, mixed, cosine, sine, gain_q, gain_k, heads, block):
    length = mixed.shape[1]
    query, key, value, per_head, per_group, per_row, table, gain, per_owner = attention_specs(
        length, heads, block
    )
    per = lambda count: jax.ShapeDtypeStruct((count, HEAD_SIZE, length), jnp.bfloat16)
    scores = heads * length * length // 2
    return pl.pallas_call(
        functools.partial(forward_kernel, block=block),
        name="attention_forward",
        out_shape=(
            per(heads), per(2), per(2),
            jax.ShapeDtypeStruct((length // block, heads * HEAD_SIZE, block), jnp.bfloat16),
            jax.ShapeDtypeStruct((heads, 1, length), jnp.float32),
        ),
        grid_spec=pltpu.PrefetchScalarGridSpec(
            num_scalar_prefetch=1,
            grid=(heads,),
            in_specs=[query, key, value, table, table, gain, gain],
            out_specs=[per_head, per_group, per_group, per_owner, per_row],
        ),
        compiler_params=pltpu.CompilerParams(
            dimension_semantics=("arbitrary",), vmem_limit_bytes=VMEM_LIMIT
        ),
        cost_estimate=pl.CostEstimate(
            flops=scores * 4 * HEAD_SIZE, transcendentals=scores, bytes_accessed=8_000_000
        ),
    )(groups, mixed, mixed, mixed, cosine, sine, gain_q, gain_k)


def attend_back(
    groups, mixed, query_rows, key_rows, value_rows, grads, lse, cosine, sine, gain_q, gain_k, heads, block
):
    length = mixed.shape[1]
    query, key, value, per_head, per_group, per_row, table, gain, per_owner = attention_specs(
        length, heads, block
    )
    tall = (HEAD_SIZE, length)
    scores = heads * length * length // 2
    return pl.pallas_call(
        functools.partial(backward_kernel, block=block),
        name="attention_backward",
        out_shape=(
            jax.ShapeDtypeStruct((heads * HEAD_SIZE, length), jnp.bfloat16),
            jax.ShapeDtypeStruct((2,) + tall, jnp.bfloat16),
            jax.ShapeDtypeStruct((2,) + tall, jnp.bfloat16),
            jax.ShapeDtypeStruct((HEAD_SIZE, 1), jnp.float32),
            jax.ShapeDtypeStruct((HEAD_SIZE, 1), jnp.float32),
        ),
        grid_spec=pltpu.PrefetchScalarGridSpec(
            num_scalar_prefetch=1,
            grid=(heads,),
            in_specs=[
                query, key, per_head, per_group, per_group, per_owner, per_row, table, table, gain, gain,
            ],
            out_specs=[query, per_group, per_group, gain, gain],
            scratch_shapes=[pltpu.VMEM(tall, jnp.float32)] * 5,
        ),
        compiler_params=pltpu.CompilerParams(
            dimension_semantics=("arbitrary",), vmem_limit_bytes=VMEM_LIMIT
        ),
        cost_estimate=pl.CostEstimate(
            flops=scores * 10 * HEAD_SIZE, transcendentals=scores, bytes_accessed=10_000_000
        ),
    )(groups, mixed, mixed, query_rows, key_rows, value_rows, grads, lse, cosine, sine, gain_q, gain_k)


def row_order_kernel(mine_ref, in_ref, out_ref, *, offsets, back):
    for index, offset in enumerate(offsets):
        held = mine_ref[0] ^ offset
        if back:
            out_ref[held] = in_ref[index]
        else:
            out_ref[index] = in_ref[held]


def column_order_kernel(mine_ref, in_ref, out_ref, *, lines, parts, back):
    width = in_ref.shape[1] // (2 * lines)
    small = width // parts
    for plane in range(2):
        for line in range(lines):
            held = pl.multiple_of((mine_ref[0] ^ (line * 2 + plane)) * width, width)
            places = [(plane * parts + part) * lines + line for part in range(parts)]
            if back:
                out_ref[:, pl.ds(held, width)] = jnp.concatenate(
                    [in_ref[:, at * small : (at + 1) * small] for at in places], axis=1
                )
            else:
                block = in_ref[:, pl.ds(held, width)]
                for part, at in enumerate(places):
                    out_ref[:, at * small : (at + 1) * small] = block[
                        :, part * small : (part + 1) * small
                    ]


def order_call(kernel, array, mine):
    return pl.pallas_call(
        kernel,
        name="block_order",
        out_shape=jax.ShapeDtypeStruct(array.shape, array.dtype),
        in_specs=[
            pl.BlockSpec(memory_space=pltpu.SMEM),
            pl.BlockSpec(memory_space=pltpu.VMEM),
        ],
        out_specs=pl.BlockSpec(memory_space=pltpu.VMEM),
        compiler_params=pltpu.CompilerParams(vmem_limit_bytes=VMEM_LIMIT),
        cost_estimate=pl.CostEstimate(
            flops=0, transcendentals=0, bytes_accessed=4 * array.size
        ),
    )(mine.reshape(1).astype(jnp.int32), array)


def column_order(array, mine, lines, parts, back=False):
    rows, columns = array.shape
    width = columns // (2 * lines)
    if width % 128 == 0:
        kernel = functools.partial(column_order_kernel, lines=lines, parts=parts, back=back)
        return order_call(kernel, array, mine)
    small = width // parts
    if back:
        array = array.reshape(rows, 2, parts, lines, small).transpose(0, 3, 1, 2, 4)
        return jnp.where(mine == 0, array, array[:, :, ::-1]).reshape(rows, columns)
    array = array.reshape(rows, lines, 2, parts, small)
    array = jnp.where(mine == 0, array, array[:, :, ::-1])
    return array.transpose(0, 2, 3, 1, 4).reshape(rows, columns)


def head_columns(part, width):
    keys_at = QUERY_HEADS * HEAD_SIZE + part * HEAD_SIZE
    values_at = keys_at + VALUE_GROUPS * HEAD_SIZE
    pair = 2 * HEAD_SIZE
    return ((part * width, 0, width), (keys_at, width, pair), (values_at, width + pair, pair))


def split_kernel(in_ref, qkv_ref, out_ref, gain_ref, *, width):
    parts, lines, rows, _ = qkv_ref.shape
    for line in range(lines):
        for part in range(parts):
            for source, target, count in head_columns(part, width):
                qkv_ref[part, line, :, target : target + count] = in_ref[
                    line, :rows, source : source + count
                ]
        out_ref[line] = in_ref[line, rows:, :]
        gain_ref[line] = in_ref[line, : gain_ref.shape[1], in_ref.shape[2] - gain_ref.shape[2] :]


def split_columns(both, parts, rows, width, gain_width):
    lines, total, model = both.shape
    span = width + 4 * HEAD_SIZE
    return pl.pallas_call(
        functools.partial(split_kernel, width=width),
        name="split_columns",
        out_shape=(
            jax.ShapeDtypeStruct((parts, lines, rows, span), both.dtype),
            jax.ShapeDtypeStruct((lines, total - rows, model), both.dtype),
            jax.ShapeDtypeStruct((lines, min(GAIN_ROWS, rows), gain_width), both.dtype),
        ),
        compiler_params=pltpu.CompilerParams(vmem_limit_bytes=VMEM_LIMIT),
        cost_estimate=pl.CostEstimate(
            flops=0, transcendentals=0, bytes_accessed=4 * both.size
        ),
    )(both)


def join_kernel(in_ref, qkv_ref, *, width):
    parts, lines, _, _ = in_ref.shape
    for line in range(lines):
        for part in range(parts):
            qkv_ref[line, :, part * width : (part + 1) * width] = in_ref[part, line, :, :width]
        for kind in range(2):
            for group in range(VALUE_GROUPS):
                terms = []
                for part in range(max(group - 1, 0), min(group + 1, parts)):
                    at = width + (2 * kind + group - part) * HEAD_SIZE
                    terms.append(in_ref[part, line, :, at : at + HEAD_SIZE].astype(jnp.float32))
                at = (QUERY_HEADS + kind * VALUE_GROUPS + group) * HEAD_SIZE
                qkv_ref[line, :, at : at + HEAD_SIZE] = sum(terms).astype(qkv_ref.dtype)


def join_columns(qkv_parts, width):
    _, lines, rows, _ = qkv_parts.shape
    shape = (lines, rows, (QUERY_HEADS + 2 * VALUE_GROUPS) * HEAD_SIZE)
    return pl.pallas_call(
        functools.partial(join_kernel, width=width),
        name="join_columns",
        out_shape=jax.ShapeDtypeStruct(shape, jnp.bfloat16),
        compiler_params=pltpu.CompilerParams(vmem_limit_bytes=VMEM_LIMIT),
        cost_estimate=pl.CostEstimate(
            flops=0, transcendentals=0, bytes_accessed=4 * int(np.prod(shape))
        ),
    )(qkv_parts)


def adamw_kernel(
    stays_ref, fixes_ref, weight_ref, own_ref, moved_ref, first_ref, second_ref, new_ref, moments_ref,
    *, rate, shrink,
):
    high = jnp.float32
    grad = jnp.where(stays_ref[0] == 1, own_ref[...].astype(high), moved_ref[...].astype(high))
    first_new = beta_first * first_ref[...] + (1.0 - beta_first) * grad
    second_new = beta_second * second_ref[...] + (1.0 - beta_second) * grad * grad
    stepped = first_new / fixes_ref[0] / (jnp.sqrt(second_new / fixes_ref[1]) + adam_eps)
    weight = weight_ref[...]
    new_ref[...] = weight - rate * (stepped + shrink * weight)
    moments_ref[0] = first_new
    moments_ref[1] = jnp.sqrt(second_new)


def adamw_block(weight, grads, first, second, rate, shrink, stays, fixes):
    rows, columns = weight.shape
    tile = 64 if rows % 64 == 0 else rows
    block = pl.BlockSpec((tile, columns), lambda i: (i, 0))
    scalar = pl.BlockSpec(memory_space=pltpu.SMEM)
    return pl.pallas_call(
        functools.partial(adamw_kernel, rate=rate, shrink=shrink),
        name="adamw",
        out_shape=(
            jax.ShapeDtypeStruct(weight.shape, weight.dtype),
            jax.ShapeDtypeStruct((2,) + weight.shape, weight.dtype),
        ),
        grid=(rows // tile,),
        in_specs=[scalar, scalar] + [block] * 5,
        out_specs=(block, pl.BlockSpec((2, tile, columns), lambda i: (0, i, 0))),
        compiler_params=pltpu.CompilerParams(vmem_limit_bytes=VMEM_LIMIT),
        cost_estimate=pl.CostEstimate(
            flops=20 * weight.size, transcendentals=2 * weight.size, bytes_accessed=28 * weight.size
        ),
    )(stays.reshape(1), fixes, weight, grads[0], grads[1], first, second)


def adamw(weight, grad, first, second, rate, shrink, item_count):
    first_new = beta_first * first + (1.0 - beta_first) * grad
    second_new = beta_second * second + (1.0 - beta_second) * grad * grad
    fix_first = 1.0 - jnp.power(beta_first, item_count)
    fix_second = 1.0 - jnp.power(beta_second, item_count)
    stepped = first_new / fix_first / (jnp.sqrt(second_new / fix_second) + adam_eps)
    return (
        weight - rate * (stepped + shrink * weight),
        jnp.stack([first_new, jnp.sqrt(second_new)]),
    )


def local(
    sizes,
    tokens,
    cotangent,
    corpus_id,
    corpus_weight,
    step_count,
    qkv_weight,
    out_weight,
    gains,
    gate_weight,
    up_weight,
    down_weight,
    first_qkv,
    first_out,
    first_gains,
    first_gate,
    first_up,
    first_down,
    second_qkv,
    second_out,
    second_gains,
    second_gate,
    second_up,
    second_down,
):
    low = jnp.bfloat16
    high = jnp.float32
    devices = int(np.prod(sizes))
    seqs = sizes[0] * sizes[1]
    parts = sizes[2] * sizes[3]
    places = np.arange(devices).reshape(sizes)
    where = np.stack(np.unravel_index(np.arange(devices), sizes), -1)

    def permute(array, target):
        pairs = [(int(i), int(places[tuple(target(*where[i]))])) for i in range(devices)]
        return lax.ppermute(array, ALL, [pair for pair in pairs if pair[0] != pair[1]])

    def swap(array):
        moved = permute(array, lambda sh, sl, kh, kl: (sh, kl, kh, sl))
        return jnp.where(lax.axis_index("sl") == lax.axis_index("kl"), array, moved)

    def in_ffn_group(array, r):
        return permute(array, lambda sh, sl, kh, kl: (sh, sl ^ (r & 1), kh ^ (r >> 1), kl))

    def in_sequence(array, r):
        return permute(array, lambda sh, sl, kh, kl: (sh, sl, kh ^ (r >> 1), kl ^ (r & 1)))

    def along_y(array):
        return permute(array, lambda sh, sl, kh, kl: (sh, sl ^ 1, kh, kl))

    z_size = sizes[0]

    def halve(blocks, index, axis, move):
        kept = lax.dynamic_index_in_dim(blocks, index, axis, keepdims=False)
        sent = lax.dynamic_index_in_dim(blocks, index ^ 1, axis, keepdims=False)
        return (kept.astype(high) + move(sent).astype(high)).astype(low)

    item_count, model = tokens.shape
    heads = QUERY_HEADS // parts
    width = heads * HEAD_SIZE
    pair = 2 * HEAD_SIZE
    keys_at = QUERY_HEADS * HEAD_SIZE
    values_at = keys_at + VALUE_GROUPS * HEAD_SIZE
    kv = lax.axis_index(KV)
    length = item_count * parts
    cosine, sine = angle_tables(length)
    groups = ((jnp.arange(heads, dtype=jnp.int32) + kv) // 4).astype(jnp.int32)

    def stage(ready, waiting):
        return lax.optimization_barrier((ready, waiting))

    row_offsets = [
        (z * 2 + rs) * parts + r1 * 2 + r0
        for r0 in range(2) for r1 in range(2) for rs in range(2) for z in range(z_size)
    ]

    def columns_moved(array, back=False):
        return column_order(array, lax.axis_index("sl"), z_size, parts, back=back)

    def rows_moved(array, back=False):
        blocks = array.reshape(devices, -1, item_count)
        kernel = functools.partial(row_order_kernel, offsets=tuple(row_offsets), back=back)
        mine = lax.axis_index("sl") * parts + kv
        return order_call(kernel, blocks, mine).reshape(-1, item_count)

    span = width + 2 * pair
    own_rows, total_columns = qkv_weight.shape
    spare = model - total_columns
    gain_rows = -(-gains.shape[0] // spare)
    gains_block = jnp.pad(gains.astype(low), (0, own_rows * spare - gains.shape[0]))
    both = jnp.concatenate(
        [
            jnp.concatenate([qkv_weight.astype(low), gains_block.reshape(own_rows, spare)], axis=1),
            out_weight.astype(low),
        ]
    )
    both_line = lax.all_to_all(
        jnp.broadcast_to(both[None], (z_size,) + both.shape), "sh", split_axis=0, concat_axis=0, tiled=True
    )
    tokens_near = columns_moved(tokens)
    tokens_far = in_sequence(tokens_near, 2)
    gate_block = swap(gate_weight.astype(low))
    factor = jnp.sum(
        jnp.where(jnp.arange(corpus_weight.shape[0]) == corpus_id[0], corpus_weight, 0.0)
    )
    weighted = cotangent.astype(high) * factor
    weighted_low = weighted.astype(low)
    weighted_one = in_ffn_group(weighted_low, 1)
    (both_line, tokens_far, gate_block, weighted_one), (up_low, tokens_near, weighted_low) = stage(
        (both_line, tokens_far, gate_block, weighted_one),
        (up_weight.astype(low), tokens_near, weighted_low),
    )
    gate_full = lax.all_gather(gate_block, OWNERS, axis=0, tiled=True)

    qkv_parts, out_line, gain_line = split_columns(both_line, parts, own_rows, width, spare)
    gain_line = gain_line[:, :gain_rows].reshape(z_size, -1)
    gain_pairs = jnp.stack([gain_line, in_sequence(gain_line, 1)])
    gain_pairs = jnp.stack([gain_pairs, in_sequence(gain_pairs, 2)])
    qkv_rows = lax.all_to_all(
        qkv_parts, KV, split_axis=0, concat_axis=0, tiled=True
    )
    tokens_pair = (in_sequence(tokens_near, 1), in_sequence(tokens_far, 1))
    up_block = swap(up_low)
    out_near = jnp.stack([out_line, along_y(out_line)])
    (qkv_rows, tokens_pair, gain_pairs, up_block, out_near), (down_low, own_cotangent) = stage(
        (qkv_rows, tokens_pair, gain_pairs, up_block, out_near), (down_weight.astype(low), cotangent)
    )
    up_full = lax.all_gather(up_block, OWNERS, axis=0, tiled=True)

    qkv_far = along_y(qkv_rows)
    cotangent_far, out_near = stage(in_ffn_group(own_cotangent, 2), out_near)
    weighted_far = (cotangent_far.astype(high) * factor).astype(low)
    out_far = in_sequence(out_near, 2)
    held = jnp.arange(2 * parts)
    mine = lax.axis_index("sl") * parts + kv
    selection = held[:, None] == (held[None, :] ^ mine)
    gain_blocks = jnp.stack([gain_pairs, along_y(gain_pairs)])[..., : gains.shape[0]]
    gain_values = contract(selection.astype(low), gain_blocks.reshape(2 * parts, -1), 1, 0)
    gain_values = gain_values.reshape(2, parts, z_size, -1).transpose(2, 0, 1, 3).reshape(-1)
    gain_one = gain_values[:model]
    gain_two = gain_values[model : 2 * model]
    gain_q = gain_values[2 * model : 2 * model + HEAD_SIZE].reshape(HEAD_SIZE, 1)
    gain_k = gain_values[2 * model + HEAD_SIZE :].reshape(HEAD_SIZE, 1)
    gain_moved = columns_moved(jnp.broadcast_to(gain_one[None], (8, model)))[:1]
    all_rows = jnp.zeros((parts, item_count, model), low)
    for r, piece in enumerate((tokens_near, tokens_pair[0], tokens_far, tokens_pair[1])):
        all_rows = lax.dynamic_update_slice_in_dim(all_rows, piece[None], kv ^ r, 0)
    all_rows = all_rows.reshape(length, model).astype(high)
    normed = (all_rows * rms_scale(all_rows) * gain_moved).astype(low)
    normed, qkv_rows = stage(normed, qkv_rows)
    qkv_full = jnp.concatenate([qkv_rows, qkv_far]).reshape(model, span)

    mixed = contract(qkv_rows.reshape(-1, span), normed[:, : model // 2], 0, 1)
    mixed = lax.optimization_barrier(mixed)
    mixed = mixed + contract(qkv_far.reshape(-1, span), normed[:, model // 2 :], 0, 1)
    query_rows, key_rows, value_rows, outgoing, lse = attend(
        groups, mixed, cosine, sine, gain_q, gain_k, heads, item_count
    )
    weighted_two = in_ffn_group(weighted_far, 1)
    (outgoing, weighted_two), (out_near, down_low) = stage((outgoing, weighted_two), (out_near, down_low))
    weighted_rows = (jnp.concatenate([weighted_low, weighted_one, weighted_far]), weighted_two)

    down_block = swap(down_low)
    attended = rows_moved(
        lax.all_to_all(outgoing, KV, split_axis=0, concat_axis=0, tiled=True)
    )
    out_full = (out_near, out_far, in_sequence(out_near, 1), in_sequence(out_far, 1))
    out_full = [piece.reshape(-1, model) for piece in out_full]
    (attended, out_full), down_block = stage((attended, out_full), down_block)
    attended = attended.reshape(4, -1, item_count)
    down_full = lax.all_gather(down_block, OWNERS, axis=0, tiled=True)
    inputs = tokens.astype(high)
    hidden = inputs + sum(contract(attended[i], out_full[i], 0, 0) for i in range(4))

    scale_two = rms_scale(hidden)
    normed_two = (hidden * scale_two * gain_two).astype(low)
    ffn_moved = [in_ffn_group(normed_two, r) for r in (3, 1, 2)]
    ffn_rows = (jnp.concatenate([normed_two, ffn_moved[1], ffn_moved[2]]), ffn_moved[0])

    def activation(rows, gate_full, up_full):
        gate = contract(rows, gate_full, 1, 0)
        up_part = contract(rows, up_full, 1, 0)
        sigma = jax.nn.sigmoid(gate)
        return (gate, up_part, sigma, (gate * sigma * up_part).astype(low))

    def activation_back(rows, down_full, gate, up_part, sigma):
        grad_acted = contract(rows, down_full, 1, 0)
        grad_gate = (grad_acted * up_part * sigma * (1.0 + gate * (1.0 - sigma))).astype(low)
        return (grad_gate, (grad_acted * (gate * sigma)).astype(low))

    def weight_gradient(left, right):
        return sum(contract(left[i], right[i], 0, 0) for i in range(2)).astype(low)

    def share(grad):
        return lax.psum_scatter(grad, OWNERS, scatter_dimension=0, tiled=True)

    near = activation(ffn_rows[0], gate_full, up_full)
    near, (gate_full, up_full) = stage(near, (gate_full, up_full))
    far = activation(ffn_rows[1], gate_full, up_full)
    acted = (near[3], far[3])
    grad_down_low = weight_gradient(weighted_rows, acted)
    down_full, grad_down_low = stage(down_full, grad_down_low)
    grad_down_share = share(grad_down_low)
    far_gate, far_up = activation_back(weighted_rows[1], down_full, *far[:3])
    sent_far = (contract(far_gate, gate_full, 1, 1) + contract(far_up, up_full, 1, 1)).astype(low)
    sent_far, weighted_near = stage(sent_far, weighted_rows[0])
    received_far = in_ffn_group(sent_far, 3)
    near_gate, near_up = activation_back(weighted_near, down_full, *near[:3])
    rows_partial = (contract(near_gate, gate_full, 1, 1) + contract(near_up, up_full, 1, 1)).astype(low)
    received = [
        in_ffn_group(rows_partial[r * item_count : (r + 1) * item_count], r) for r in (1, 2)
    ]
    grad_gate, grad_up = (near_gate, far_gate), (near_up, far_up)
    (received_far, rows_partial), (grad_gate, grad_up) = stage(
        (received_far, rows_partial), (grad_gate, grad_up)
    )
    grad_gate_share = share(weight_gradient(ffn_rows, grad_gate))
    grad_up_low = weight_gradient(ffn_rows, grad_up)
    ffn_partial = [contract(part, down_full, 1, 1).astype(low) for part in acted]
    (received, grad_down_share), (grad_up_low, ffn_partial) = stage(
        (received, grad_down_share), (grad_up_low, ffn_partial)
    )
    received = received + [received_far]
    grad_up_share = share(grad_up_low)
    grad_normed_two = rows_partial[:item_count].astype(high) + sum(
        piece.astype(high) for piece in received
    )

    pushed_two, gain_two_terms = norm_back(grad_normed_two, hidden, scale_two, gain_two)
    grad_hidden = weighted + pushed_two
    hidden_low = grad_hidden.astype(low)

    attended_gradient = jnp.concatenate(
        [contract(piece, hidden_low, 1, 1).astype(low) for piece in out_full]
    )
    attended_gradient = rows_moved(attended_gradient, back=True)
    incoming = lax.all_to_all(
        attended_gradient.reshape(parts, width, item_count), KV, split_axis=0, concat_axis=0, tiled=True
    )
    ffn_blocks = ffn_partial[0].reshape(3, item_count, model)
    ffn_moved = [in_ffn_group(ffn_blocks[1], 1), in_ffn_group(ffn_partial[1], 1)]
    sent_out = [
        contract(attended[2 + r], hidden_low, 1, 0).astype(low) for r in range(2)
    ]
    kept_out = [
        contract(attended[r], hidden_low, 1, 0) for r in range(2)
    ]
    out_line = [
        (kept_out[r] + in_sequence(sent_out[r], 1).astype(high)).astype(low) for r in range(2)
    ]
    incoming, out_line = lax.optimization_barrier((incoming, out_line))

    out_moved = in_sequence(out_line[1], 2)
    grad_queries, grad_keys, grad_values, gain_q_sum, gain_k_sum = attend_back(
        groups, mixed, query_rows, key_rows, value_rows, incoming, lse,
        cosine, sine, gain_q, gain_k, heads, item_count,
    )
    grad_mixed = jnp.concatenate(
        [grad_queries, grad_keys.reshape(pair, length), grad_values.reshape(pair, length)], axis=0
    )
    half_model = model // 2
    grad_mixed, (ffn_moved, grad_gate_share) = stage(grad_mixed, (ffn_moved, grad_gate_share))
    mixer_sent = contract(normed[:, half_model:], grad_mixed, 0, 1).astype(low)
    (mixer_sent, grad_mixed), (out_line, ffn_blocks) = stage(
        (mixer_sent, grad_mixed), (out_line[0], ffn_blocks)
    )

    mixer_moved = along_y(mixer_sent)
    mixer_line = contract(normed[:, :half_model], grad_mixed, 0, 1)
    grad_normed = contract(grad_mixed, qkv_full, 0, 1).astype(low)
    grad_normed = grad_normed.reshape(2, 2, item_count, model)
    core = lax.axis_index("kl")
    normed_moved = in_sequence(lax.dynamic_index_in_dim(grad_normed, core ^ 1, 1, keepdims=False), 1)
    ffn_line = [
        ffn_blocks[2 * r].astype(high) + ffn_moved[r].astype(high) for r in range(2)
    ]
    mixer_line = lax.optimization_barrier(mixer_line)
    mixer_parts = (mixer_line + mixer_moved.astype(high)).astype(low)
    mixer_parts, (out_line, shares) = stage(
        mixer_parts, (out_line, (grad_down_share, grad_gate_share))
    )
    swapped = [permute(piece, lambda sh, sl, kh, kl: (sh, kl, kh, sl)) for piece in shares]
    ffn_moved = in_ffn_group(ffn_line[1].astype(low), 2)
    swapped, ffn_moved = stage(swapped, ffn_moved)

    mixer_parts = lax.all_to_all(
        mixer_parts.reshape(parts, z_size, -1, span), KV, split_axis=0, concat_axis=0, tiled=True
    )
    out_line = (out_line.astype(high) + out_moved.astype(high)).astype(low).reshape(2, z_size, -1, model)
    out_moved = along_y(out_line[1])
    qkv_line = join_columns(mixer_parts, width)
    qkv_line, (grad_normed, normed_moved, out_line, grad_up_share) = stage(
        qkv_line, (grad_normed, normed_moved, out_line[0], grad_up_share)
    )

    qkv_line = lax.all_to_all(qkv_line, "sh", split_axis=0, concat_axis=0, tiled=True)
    grad_normed = lax.dynamic_index_in_dim(grad_normed, core, 1, keepdims=False).astype(high)
    grad_normed = (grad_normed + normed_moved.astype(high)).astype(low)
    grad_normed = halve(grad_normed, lax.axis_index("kh"), 0, lambda v: in_sequence(v, 2)).astype(high)
    line = lax.axis_index("sh")

    def sum_line(blocks):
        total = lax.dynamic_index_in_dim(blocks, line, 0, keepdims=False).astype(high)
        for r in range(1, z_size):
            sent = lax.dynamic_index_in_dim(blocks, line ^ r, 0, keepdims=False)
            total = total + permute(sent, lambda sh, sl, kh, kl: (sh ^ r, sl, kh, kl)).astype(high)
        return total

    out_grad = sum_line((out_line.astype(high) + out_moved.astype(high)).astype(low))
    block_out = (hidden + (ffn_line[0] + ffn_moved.astype(high))).astype(low)
    qkv_grad = jnp.sum(qkv_line.astype(high), 0)
    grad_down, grad_gate_w = zip(shares, swapped)
    grad_up_w = (grad_up_share, permute(grad_up_share, lambda sh, sl, kh, kl: (sh, kl, kh, sl)))
    moved_inputs = tokens_near.astype(high)
    pushed_one, gain_one_terms = norm_back(
        grad_normed, moved_inputs, rms_scale(moved_inputs), gain_moved
    )
    grad_input = grad_hidden + columns_moved(pushed_one, back=True)
    gain_one_sum = columns_moved(
        jnp.broadcast_to(jnp.sum(gain_one_terms, 0)[None], (8, model)), back=True
    )[0]
    grad_gains = jnp.concatenate(
        [
            gain_one_sum,
            jnp.sum(gain_two_terms, 0),
            gain_q_sum.reshape(-1),
            gain_k_sum.reshape(-1),
        ]
    )
    grad_gains = grad_gains.reshape(z_size, 2, parts, -1).transpose(1, 2, 0, 3)
    grad_gains = lax.dot_general(
        selection.astype(high), grad_gains.reshape(2 * parts, -1), (((1,), (0,)), ((), ())),
        precision=lax.Precision.HIGHEST, preferred_element_type=high,
    ).reshape(2, 2, 2, -1)
    grad_gains = grad_gains[0] + along_y(grad_gains[1])
    grad_gains = grad_gains[:, 0] + in_sequence(grad_gains[:, 1], 1)
    grad_gains = grad_gains[0] + in_sequence(grad_gains[1], 2)
    gains_grad = sum_line(grad_gains.reshape(z_size, -1))

    steps_done = step_count[0].astype(high)
    new_qkv, moments_qkv = adamw(qkv_weight, qkv_grad, first_qkv, second_qkv, 0.02, 0.1, steps_done)
    new_out, moments_out = adamw(out_weight, out_grad, first_out, second_out, 0.2, 0.1, steps_done)
    new_gains, moments_gains = adamw(
        gains, gains_grad, first_gains, second_gains, 0.6, 0.0, steps_done
    )
    stays = (lax.axis_index("sl") == lax.axis_index("kl")).astype(jnp.int32)
    fixes = jnp.stack(
        [1.0 - jnp.power(beta_first, steps_done), 1.0 - jnp.power(beta_second, steps_done)]
    )
    new_gate, moments_gate = adamw_block(
        gate_weight, grad_gate_w, first_gate, second_gate, 0.02, 0.1, stays, fixes
    )
    new_up, moments_up = adamw_block(
        up_weight, grad_up_w, first_up, second_up, 0.02, 0.1, stays, fixes
    )
    new_down, moments_down = adamw_block(
        down_weight, grad_down, first_down, second_down, 0.013, 0.1, stays, fixes
    )
    return (
        block_out,
        grad_input,
        new_qkv,
        moments_qkv,
        new_out,
        moments_out,
        new_gains,
        moments_gains,
        new_gate,
        moments_gate,
        new_up,
        moments_up,
        new_down,
        moments_down,
    )


def solution(mesh):
    seqs, parts = mesh.shape["seq"], mesh.shape["kv"]
    sizes = (seqs // 2, 2, parts // 2, 2)
    fine = Mesh(mesh.devices.reshape(sizes), ALL)
    rows = P(ALL, None)
    block = P(SEQ, KV)
    return jax.shard_map(
        functools.partial(local, sizes),
        mesh=fine,
        in_specs=(
            rows, rows, P(SEQ), P(), P(),
            rows, rows, P(ALL), block, block, block,
            rows, rows, P(ALL), block, block, block,
            rows, rows, P(ALL), block, block, block,
        ),
        out_specs=(
            rows, rows,
            rows, P(None, ALL, None),
            rows, P(None, ALL, None),
            P(ALL), P(None, ALL),
            block, P(None, SEQ, KV),
            block, P(None, SEQ, KV),
            block, P(None, SEQ, KV),
        ),
        check_vma=False,
    )
```
